32 devices in a mesh: wide: 16 (over z, y, core), narrow: 2 (over x).
Axes of the slice: x: 2, y: 2, z: 4, core: 2. Of those that a mesh axis runs over, the one named last changes fastest.
Arguments:
- spin: float32 [3, 32, 32, 256], P(None, None, 'wide', 'narrow'), may hold values from -1 to 1, as said below
- region: int32 [32, 32, 256], P(None, 'wide', 'narrow'), may hold values 0 or 1
- material: int32 [32, 32, 256], P(None, 'wide', 'narrow'), may hold values from 0 to 3
- saturation: float32 [4], replicated, may hold values from 0.5 to 2
- anisotropy: float32 [4], replicated, may hold values from 0.2 to 1
- damping: float32 [4], replicated, may hold values from 0.05 to 0.5
- applied: float32 [3], replicated, may hold values from -3 to 3
- demag_spectrum: bfloat16 [6, 64, 64, 512], P(None, 'wide', 'narrow'), may hold values from -2.5 to 2.5, as said below
Outputs:
- rate: float32 [3, 32, 32, 256], P(None, None, 'wide', 'narrow')
- demag_field: float32 [3, 32, 32, 256], P(None, None, 'wide', 'narrow')
The draws below stay inside these ranges and needn't reach their ends.
Inputs may be any that keep to these rules, and one draw needn't show every extreme that they name: `spin`: every cell's three components form a unit vector. `demag_spectrum`: every component is unchanged when all three wave numbers are replaced by their negatives modulo 64, 64, 512.
All inputs are finite; a program needn't handle non-finite values. No bound on the sum of `region` on one device may be relied on, other than what follows from the above.
Results may differ from the reference program's by a relative error of at most 0.0003.
Values sent between devices are 32-bit elements; how exact they have to be, the bound alone decides.
No kernel may reach another device: no remote copies, remote signals or barrier semaphores. Data moves between devices by JAX's collectives and lax.ppermute only.
A program may use at most 64 MiB of HBM per device.

```python
import math
import jax
import jax.numpy as jnp

NZ = 32
MATERIALS = 4
NX = 32
NY = 256
LZ = 64
LX = 64
LY = 512


def draw_spin(key, part):
    first, second = jax.random.split(jax.random.fold_in(key, 11))
    height = jax.random.uniform(first, (NZ, NX, NY), jnp.float32, -1.0, 1.0)
    azimuth = jax.random.uniform(second, (NZ, NX, NY), jnp.float32, -math.pi, math.pi)
    radius = jnp.sqrt(jnp.maximum(1.0 - height * height, 0.0))
    return jnp.stack([radius * jnp.cos(azimuth), radius * jnp.sin(azimuth), height])


def mirror(values):
    return jnp.roll(jnp.flip(values, axis=(1, 2, 3)), (1, 1, 1), axis=(1, 2, 3))


def symbols(length):
    phase = jnp.arange(length).astype(jnp.float32) * (math.pi / length)
    return (2.0 * jnp.sin(2.0 * phase), 4.0 * jnp.sin(phase) * jnp.sin(phase))


def draw_demag_spectrum(key, part):
    first, second = jax.random.split(jax.random.fold_in(key, 23))
    odd_z, square_z = symbols(LZ)
    odd_x, square_x = symbols(LX)
    odd_y, square_y = symbols(LY)
    odd_z, square_z = (odd_z[:, None, None], square_z[:, None, None])
    odd_x, square_x = (odd_x[None, :, None], square_x[None, :, None])
    odd_y, square_y = (odd_y[None, None, :], square_y[None, None, :])
    denominator = square_x + square_y + square_z + 0.1
    base = jnp.stack([square_x + 0.0 * odd_y + 0.0 * odd_z, square_y + 0.0 * odd_x + 0.0 * odd_z, square_z + 0.0 * odd_x + 0.0 * odd_y, odd_x * odd_y + 0.0 * odd_z, odd_x * odd_z + 0.0 * odd_y, odd_y * odd_z + 0.0 * odd_x]) / denominator[None]
    gains = jax.random.uniform(first, (6, LZ, LX, LY), jnp.float32, 0.6, 1.4)
    noise = jax.random.uniform(second, (6, LZ, LX, LY), jnp.float32, -0.3, 0.3)
    values = base * gains + noise
    return jnp.clip(0.5 * (values + mirror(values)), -2.5, 2.5).astype(jnp.bfloat16)


def plant(values, key, low, largest):
    longest = values.shape.index(max(values.shape))
    spots = []
    for shift in (0, 1):
        where = [jax.random.randint(jax.random.fold_in(key, axis), (), 0, length) for axis, length in enumerate(values.shape)]
        where[longest] = (where[longest] + shift) % values.shape[longest]
        spots.append(tuple(where))
    return values.at[spots[0]].set(low).at[spots[1]].set(largest)


def scatter_about(stream_key, shape, width, most, kind=jnp.bfloat16):
    return jnp.clip(width * jax.random.normal(stream_key, shape, jnp.float32), -most, most).astype(kind)


def setup_inputs(seed: int = 0) -> dict:
    key_of = jax.random.split(jax.random.key(seed), 9)
    spin = draw_spin(jax.random.fold_in(key_of[8], 71), 0)
    region = plant((jax.random.randint(key_of[1], (NZ, NX, NY), 0, 8) < 7).astype(jnp.int32), jax.random.fold_in(key_of[1], 1), 0, 1)
    material = plant(jax.random.randint(key_of[2], (NZ, NX, NY), 0, MATERIALS), jax.random.fold_in(key_of[2], 1), 0, MATERIALS - 1).astype(jnp.int32)
    saturation = jnp.clip(jnp.exp(jax.random.uniform(key_of[3], (MATERIALS,), jnp.float32, math.log(0.5), math.log(2.0))), 0.5, 2.0)
    anisotropy = jnp.clip(jnp.exp(jax.random.uniform(key_of[4], (MATERIALS,), jnp.float32, math.log(0.2), math.log(1.0))), 0.2, 1.0)
    damping = jnp.clip(jnp.exp(jax.random.uniform(key_of[5], (MATERIALS,), jnp.float32, math.log(0.05), math.log(0.5))), 0.05, 0.5)
    applied = scatter_about(key_of[6], (3,), 1.0, 3.0, jnp.float32)
    demag_spectrum = draw_demag_spectrum(jax.random.fold_in(key_of[8], 71), 0)
    return dict(spin=spin, region=region, material=material, saturation=saturation, anisotropy=anisotropy, damping=damping, applied=applied, demag_spectrum=demag_spectrum)


exchange_coef = 0.3


def cross(left, right):
    return jnp.stack([left[1] * right[2] - left[2] * right[1],
                      left[2] * right[0] - left[0] * right[2],
                      left[0] * right[1] - left[1] * right[0]])


def reference(spin, region, material, saturation, anisotropy, damping, applied, demag_spectrum):
    magnet = region.astype(jnp.float32)
    direction = spin * magnet[None]
    sat_cell = saturation[material]
    anis_cell = anisotropy[material]
    damp_cell = damping[material]
    moment = direction * sat_cell[None]
    padded = jnp.pad(moment, ((0, 0), (0, NZ), (0, NX), (0, NY)))
    spectrum = jnp.fft.rfftn(padded, axes=(1, 2, 3))
    kernel = demag_spectrum.astype(jnp.float32)[:, :, :, :NY + 1]
    couplings = ((0, 3, 4), (3, 1, 5), (4, 5, 2))
    pieces = []
    for picks in couplings:
        mixed = kernel[picks[0]] * spectrum[0] + kernel[picks[1]] * spectrum[1] + kernel[picks[2]] * spectrum[2]
        inverse = jnp.fft.irfftn(mixed, s=(LZ, LX, LY), axes=(0, 1, 2))
        pieces.append(-inverse[:NZ, :NX, :NY])
    demag = jnp.stack(pieces)
    framed = jnp.pad(direction, ((0, 0), (1, 1), (1, 1), (1, 1)))
    weight = jnp.sum(framed * framed, axis=0)
    neighbours = (framed[:, 2:, 1:-1, 1:-1] + framed[:, :-2, 1:-1, 1:-1]
                  + framed[:, 1:-1, 2:, 1:-1] + framed[:, 1:-1, :-2, 1:-1]
                  + framed[:, 1:-1, 1:-1, 2:] + framed[:, 1:-1, 1:-1, :-2])
    present = (weight[2:, 1:-1, 1:-1] + weight[:-2, 1:-1, 1:-1]
               + weight[1:-1, 2:, 1:-1] + weight[1:-1, :-2, 1:-1]
               + weight[1:-1, 1:-1, 2:] + weight[1:-1, 1:-1, :-2])
    laplace = neighbours - present[None] * direction
    zeros = jnp.zeros_like(sat_cell)
    uniaxial = jnp.stack([zeros, zeros, 2.0 * anis_cell / sat_cell * direction[2]])
    field = exchange_coef * laplace / sat_cell[None] + demag + applied[:, None, None, None] + uniaxial
    torque = cross(direction, field)
    rate = -(torque + damp_cell[None] * cross(direction, torque)) / (1.0 + damp_cell * damp_cell)[None]
    return rate, demag
```

```python
from functools import partial
import math

import jax
import jax.numpy as jnp
import numpy as np
from jax import lax
from jax.experimental import pallas as pl
from jax.experimental.pallas import tpu as pltpu
from jax.sharding import PartitionSpec as P

exchange_coef = 0.3
highest = lax.Precision.HIGHEST


def extended(x, sides, width):
    for axis, dim in sides:
        peers, length = (lax.axis_size(axis), x.shape[dim])
        up = [(i, (i + 1) % peers) for i in range(peers - 1)]
        down = [(j, i) for i, j in up]
        last = lax.slice_in_dim(x, length - width, length, axis=dim)
        leading = lax.slice_in_dim(x, 0, width, axis=dim)
        before = lax.ppermute(last, axis, up)
        after = lax.ppermute(leading, axis, down)
        x = jnp.concatenate([before, x, after], axis=dim)
    return x


def phase_table(rows_count, cols_count, length, sign):
    left_index = lax.broadcasted_iota(jnp.int32, (rows_count, cols_count), 0)
    right_index = lax.broadcasted_iota(jnp.int32, (rows_count, cols_count), 1)
    angle = (left_index * right_index % length).astype(jnp.float32) * (2.0 * math.pi / length)
    return (jnp.cos(angle), sign * jnp.sin(angle))


def contract(pattern, phases, values):
    phase_re, phase_im = phases
    value_re, value_im = values
    product = partial(jnp.einsum, pattern, precision=highest)
    if value_im is None:
        return (product(phase_re, value_re), product(phase_im, value_re))
    return (
        product(phase_re, value_re) - product(phase_im, value_im),
        product(phase_re, value_im) + product(phase_im, value_re),
    )


def factors(half_size, at_end):
    if at_end:
        inner_size = math.gcd(half_size, 128)
    else:
        inner_size = max(
            (
                divisor
                for divisor in range(1, half_size + 1)
                if half_size % divisor == 0 and divisor * divisor <= 2 * half_size
            )
        )
    return (inner_size, 2 * half_size // inner_size)


def forward(values, at_end, natural):
    value_re, value_im = values
    extent = value_re.shape
    half_size = extent[1]
    length = 2 * half_size
    inner_size, outer_size = factors(half_size, at_end)
    tail_index = "" if at_end else "b"
    blocked = (extent[0], outer_size // 2, inner_size) + extent[2:]
    value_re = value_re.reshape(blocked)
    value_im = None if value_im is None else value_im.reshape(blocked)
    phases = phase_table(outer_size, outer_size // 2, outer_size, -1.0)
    work_re, work_im = contract(
        "kn,anp" + tail_index + "->akp" + tail_index, phases, (value_re, value_im)
    )
    twist_re, twist_im = phase_table(outer_size, inner_size, length, -1.0)
    if not at_end:
        twist_re, twist_im = (twist_re[:, :, None], twist_im[:, :, None])
    work_re, work_im = (
        work_re * twist_re - work_im * twist_im,
        work_re * twist_im + work_im * twist_re,
    )
    target = "ajk" if natural else "akj"
    phases = phase_table(inner_size, inner_size, inner_size, -1.0)
    out_re, out_im = contract(
        "jp,akp" + tail_index + "->" + target + tail_index, phases, (work_re, work_im)
    )
    merged = (extent[0], length) + extent[2:]
    return (out_re.reshape(merged), out_im.reshape(merged))


def inverse(values, at_end, natural, real_only):
    value_re, value_im = values
    extent = value_re.shape
    length = extent[1]
    half_size = length // 2
    inner_size, outer_size = factors(half_size, at_end)
    tail_index = "" if at_end else "b"
    if natural:
        blocked = (extent[0], inner_size, outer_size) + extent[2:]
        source = "ajk"
    else:
        blocked = (extent[0], outer_size, inner_size) + extent[2:]
        source = "akj"
    phases = phase_table(inner_size, inner_size, inner_size, 1.0)
    work_re, work_im = contract(
        "pj," + source + tail_index + "->akp" + tail_index,
        phases,
        (value_re.reshape(blocked), value_im.reshape(blocked)),
    )
    twist_re, twist_im = phase_table(outer_size, inner_size, length, 1.0)
    if not at_end:
        twist_re, twist_im = (twist_re[:, :, None], twist_im[:, :, None])
    work_re, work_im = (
        work_re * twist_re - work_im * twist_im,
        work_re * twist_im + work_im * twist_re,
    )
    phases = phase_table(outer_size // 2, outer_size, outer_size, 1.0)
    pattern = "nk,akp" + tail_index + "->anp" + tail_index
    scale = 1.0 / length
    merged = (extent[0], half_size) + extent[2:]
    if real_only:
        product = partial(jnp.einsum, pattern, precision=highest)
        result = product(phases[0], work_re) - product(phases[1], work_im)
        return result.reshape(merged) * scale
    out_re, out_im = contract(pattern, phases, (work_re, work_im))
    return (out_re.reshape(merged) * scale, out_im.reshape(merged) * scale)


def along_x(pieces):
    piece_re, piece_im = pieces
    members, planes, cells_x, cells_y = piece_re.shape
    extent = (members * planes, cells_x, cells_y)
    out_re, out_im = forward((piece_re.reshape(extent), piece_im.reshape(extent)), False, True)
    merged = (members, planes, 2 * cells_x, cells_y)
    return (out_re.reshape(merged), out_im.reshape(merged))


def along_y(pieces):
    piece_re, piece_im = pieces
    members, planes, rows_x, cells_y = piece_re.shape
    extent = (members * planes * rows_x, cells_y)
    out_re, out_im = forward((piece_re.reshape(extent), piece_im.reshape(extent)), True, False)
    merged = (members, planes, rows_x, 2 * cells_y)
    return (out_re.reshape(merged), out_im.reshape(merged))


def back_to_bricks(field_re, field_im):
    members, planes, rows_x, length_y = field_re.shape
    flattened = (members * planes * rows_x, length_y)
    grid_re, grid_im = inverse(
        (field_re.reshape(flattened), field_im.reshape(flattened)), True, False, False
    )
    merged = (members, planes, rows_x, length_y // 2)
    piece_re = lax.all_to_all(
        grid_re.reshape(merged), "narrow", split_axis=3, concat_axis=2, tiled=True
    )
    piece_im = lax.all_to_all(
        grid_im.reshape(merged), "narrow", split_axis=3, concat_axis=2, tiled=True
    )
    members, planes, length_x, cells_y = piece_re.shape
    extent = (members * planes, length_x, cells_y)
    out_re, out_im = inverse(
        (piece_re.reshape(extent), piece_im.reshape(extent)), False, True, False
    )
    invert_merged = (members, planes, length_x // 2, cells_y)
    columns = (out_re.reshape(invert_merged), out_im.reshape(invert_merged))
    piece_re, piece_im = lax.all_to_all(columns, "wide", split_axis=2, concat_axis=1, tiled=True)
    members, planes, cells_x, cells_y = piece_re.shape
    extent = (members, planes, cells_x * cells_y)
    result = inverse((piece_re.reshape(extent), piece_im.reshape(extent)), False, True, True)
    merged = (members, planes // 2, cells_x, cells_y)
    return result.reshape(merged)


def couple(kernel, values, picks):
    return -(
        kernel[picks[0]] * values[0] + kernel[picks[1]] * values[1] + kernel[picks[2]] * values[2]
    )


def cross(left, right):
    return jnp.stack(
        [
            left[1] * right[2] - left[2] * right[1],
            left[2] * right[0] - left[0] * right[2],
            left[0] * right[1] - left[1] * right[0],
        ]
    )


def general_shards(spin, region, material, saturation, anisotropy, damping, applied, demag_spectrum):
    magnet = region.astype(jnp.float32)
    direction = spin * magnet[None]
    species = saturation.shape[0]
    chosen = (
        material[None] == lax.broadcasted_iota(jnp.int32, (species,) + material.shape, 0)
    ).astype(jnp.float32)

    def lookup(entries):
        return jnp.sum(chosen * entries[:, None, None, None], axis=0)

    sat_cell = lookup(saturation)
    anis_cell = lookup(anisotropy)
    damp_cell = lookup(damping)
    moment = direction * sat_cell[None]
    components, layers, width_x, width_y = spin.shape
    flattened = moment.reshape(components, layers, width_x * width_y)
    spec_re, spec_im = forward((flattened, None), False, True)
    stacked = (components, 2 * layers, width_x, width_y)
    spectra = along_x(
        (
            lax.all_to_all(
                spec_re.reshape(stacked), "wide", split_axis=1, concat_axis=2, tiled=True
            ),
            lax.all_to_all(
                spec_im.reshape(stacked), "wide", split_axis=1, concat_axis=2, tiled=True
            ),
        )
    )
    spec_re, spec_im = along_y(
        lax.all_to_all(spectra, "narrow", split_axis=2, concat_axis=3, tiled=True)
    )
    parts, planes, rows_x, length_y = demag_spectrum.shape
    inner_size, outer_size = factors(length_y // 2, True)
    kernel = demag_spectrum.reshape(parts, planes, rows_x, inner_size, outer_size)
    kernel = (
        kernel.transpose(0, 1, 2, 4, 3).reshape(parts, planes, rows_x, length_y).astype(jnp.float32)
    )
    couplings = ((0, 3, 4), (3, 1, 5), (4, 5, 2))
    field_re = [couple(kernel, spec_re, picks) for picks in couplings]
    field_im = [couple(kernel, spec_im, picks) for picks in couplings]
    demag = back_to_bricks(jnp.stack(field_re), jnp.stack(field_im))
    framed = extended(direction, (("wide", 2), ("narrow", 3)), 1)
    framed = jnp.pad(framed, ((0, 0), (1, 1), (0, 0), (0, 0)))
    weight = jnp.sum(framed * framed, axis=0)
    neighbours = (
        framed[:, 2:, 1:-1, 1:-1]
        + framed[:, :-2, 1:-1, 1:-1]
        + framed[:, 1:-1, 2:, 1:-1]
        + framed[:, 1:-1, :-2, 1:-1]
        + framed[:, 1:-1, 1:-1, 2:]
        + framed[:, 1:-1, 1:-1, :-2]
    )
    present = (
        weight[2:, 1:-1, 1:-1]
        + weight[:-2, 1:-1, 1:-1]
        + weight[1:-1, 2:, 1:-1]
        + weight[1:-1, :-2, 1:-1]
        + weight[1:-1, 1:-1, 2:]
        + weight[1:-1, 1:-1, :-2]
    )
    laplace = neighbours - present[None] * direction
    zeros = jnp.zeros_like(sat_cell)
    uniaxial = jnp.stack([zeros, zeros, 2.0 * anis_cell / sat_cell * direction[2]])
    field = (
        exchange_coef * laplace / sat_cell[None] + demag + applied[:, None, None, None] + uniaxial
    )
    torque = cross(direction, field)
    rate = (
        -(torque + damp_cell[None] * cross(direction, torque)) / (1.0 + damp_cell * damp_cell)[None]
    )
    return (rate, demag)


def split_table(table):
    high = jnp.asarray(np.asarray(table, np.float32)).astype(jnp.bfloat16)
    high64 = np.asarray(np.asarray(table, np.float32).astype(high.dtype), np.float64)
    low = (table - high64).astype(np.float32).astype(high.dtype)
    return np.asarray(high64.astype(high.dtype)), low


class Plan:
    def __init__(self, wide, narrow, layers, width_x, width_y, planes, rows_x, length_y):
        self.wide, self.narrow = wide, narrow
        self.layers, self.width_x, self.width_y = layers, width_x, width_y
        self.planes, self.rows_x = planes, rows_x
        self.length_z, self.length_x, self.length_y = planes * wide, rows_x * narrow, length_y
        self.cells_x, self.cells_y = width_x * wide, width_y * narrow
        self.devices = wide * narrow
        self.special = self.narrow * (wide // 2) + 1

    def fits(self):
        return (
            self.narrow == 2
            and self.planes == 4
            and self.wide % 16 == 0
            and self.devices * 2 == self.length_z
            and self.length_z == 2 * self.layers
            and self.length_x == 2 * self.cells_x
            and self.length_y == 2 * self.cells_y
            and self.width_x == 2
            and self.width_y % 128 == 0
            and self.rows_x % 16 == 0
            and (self.layers * self.width_x) % 8 == 0
            and 6 * self.rows_x == 3 * self.layers * self.width_x
        )

    def wave(self):
        w, n = np.divmod(np.arange(self.devices), self.narrow)
        return self.planes * w + np.where(w < self.wide // 2, 1 + n, 1 - n)

    def thickness_tables(self):
        wave = self.wave()
        z = np.arange(self.layers)
        angle = 2.0 * np.pi * ((wave[:, None] * z[None]) % self.length_z) / self.length_z
        ahead = np.stack([np.cos(angle), -np.sin(angle)], 1)
        back = np.stack([2.0 * np.cos(angle), -2.0 * np.sin(angle)], 1)
        ahead[self.special, 1] = 1.0
        back[self.special, 0] = np.cos(angle[self.special])
        back[self.special, 1] = 1.0
        back *= -1.0 / (self.length_z * self.length_x * self.length_y)
        n = np.arange(self.devices) % self.narrow
        x = np.arange(self.width_x)
        sign = 1.0 - 2.0 * ((n[:, None] * x[None]) % 2)
        unit_c, unit_x = np.eye(3), np.eye(self.width_x)
        ahead = np.einsum("drz,dx,cb,xv->dcrxbzv", ahead, sign, unit_c, unit_x)
        back = np.einsum("drz,dx,cb,xv->bzvdcrx", back, sign, unit_c, unit_x)
        count = self.devices * 6 * self.width_x
        cells = 3 * self.layers * self.width_x
        return ahead.reshape(count, cells), back.reshape(cells, count)

    def lateral_tables(self):
        half = self.cells_y
        y, k = np.arange(half), np.arange(half)
        angle = 2.0 * np.pi * ((y[:, None] * k[None]) % self.length_y) / self.length_y
        cosine, sine = np.cos(angle), np.sin(angle)
        sine[:, 0] = 1.0 - 2.0 * (y % 2)
        ahead_y = np.concatenate([cosine, sine], 1)
        back_y = np.ascontiguousarray(ahead_y.T)
        x = (np.arange(self.wide)[None] * self.width_x + np.arange(self.width_x)[:, None]).reshape(-1)
        kx = np.arange(self.length_x)
        angle = 2.0 * np.pi * ((kx[:, None] * x[None]) % self.length_x) / self.length_x
        cosine, sine = np.cos(angle), np.sin(angle)
        ahead_x = np.concatenate([cosine, sine], 0)
        back_x = np.block([[cosine.T, -sine.T], [sine.T, cosine.T]])
        flip = np.zeros((half, half))
        flip[(half - k) % half, k] = 1.0
        return ahead_y, back_y, ahead_x, back_x, flip


def halves(value):
    high = value.astype(jnp.bfloat16)
    return high, (value - high.astype(jnp.float32)).astype(jnp.bfloat16)


def mul(left, right):
    return jnp.dot(left, right, preferred_element_type=jnp.float32)


def pick(material, entries, species):
    value = jnp.zeros(material.shape, jnp.float32)
    for s in range(species):
        value = jnp.where(material == s, entries[s], value)
    return value


def rows_of(plan):
    w, n = lax.axis_index("wide"), lax.axis_index("narrow")
    low = w < plan.wide // 2
    own = jnp.where(low, 1 + n, 1 - n)
    other = jnp.where(low, 2 - n, n)
    return w, n, own, other


def first_kernel(plan, species, spin, region, material, saturation, t_high, t_low, tensor,
                 out, up, down, swap, zero, turned, held, held0, sems):
    w, n, own, other = rows_of(plan)
    fetch = pltpu.make_async_copy(tensor.at[:, other], held, sems.at[0])
    fetch.start()
    fetch0 = pltpu.make_async_copy(tensor.at[:, 0], held0, sems.at[1])
    fetch0.start()
    cells = plan.layers * plan.width_x
    magnet = region[...].astype(jnp.float32)
    sat = pick(material[...], saturation, species)
    high, low = [], []
    for c in range(3):
        direction = spin[c * cells : (c + 1) * cells, :] * magnet
        turned[c * cells : (c + 1) * cells, :] = direction
        a, b = halves(direction * sat)
        high.append(a)
        low.append(b)
    high, low = jnp.concatenate(high, 0), jnp.concatenate(low, 0)
    out[...] = mul(t_high[...], high) + (mul(t_low[...], high) + mul(t_high[...], low))
    count = 3 * plan.layers
    up[...] = turned[pl.ds(1, count, stride=2), :]
    down[...] = turned[pl.ds(0, count, stride=2), :]
    swap[:, plan.length_y :] = turned[...]
    fetch.wait()
    fetch0.wait()
    for t in range(6):
        rows = slice(t * plan.rows_x, (t + 1) * plan.rows_x)
        swap[rows, : plan.length_y] = held[t].astype(jnp.float32)
    @pl.when(w == 0)
    def _():
        for t in range(6):
            rows = slice(t * plan.rows_x, (t + 1) * plan.rows_x)
            zero[rows, :] = held0[t].astype(jnp.float32)


def tensor_kernel(plan, swapped, zero_a, zero_b, flip, tensor, full, held, sems):
    w, n, own, other = rows_of(plan)
    fetch = pltpu.make_async_copy(tensor.at[:, own], held, sems.at[0])
    fetch.start()
    half, count = plan.cells_y, plan.rows_x
    special = jnp.logical_and(w == plan.wide // 2, n == 1)

    def place(slot, part, t, values):
        rows = slice(part * count, (part + 1) * count)
        full[slot, t, rows, :half] = values[:, :half].astype(jnp.float32)
        full[slot, t, rows, half:] = mul(values[:, half:].astype(jnp.bfloat16), flip[...])

    for t in range(6):
        place(0, 1, t, swapped[t * count : (t + 1) * count, : plan.length_y])
    @pl.when(special)
    def _():
        for t in range(6):
            place(1, 0, t, zero_b[t * count : (t + 1) * count, :])
            place(1, 1, t, zero_a[t * count : (t + 1) * count, :])
    fetch.wait()
    for t in range(6):
        place(0, 0, t, held[t])


COUPLINGS = ((0, 3, 4), (3, 1, 5), (4, 5, 2))


def plane_kernel(plan, got, y_high, y_low, x_ahead, xb_pair, xb_low, yb_high, yb_low, full,
                 out, mixed, packed, spread):
    w, n, own, other = rows_of(plan)
    special = jnp.logical_and(w == plan.wide // 2, n == 1)
    slot = special.astype(jnp.int32)
    lanes, half, wide = plan.width_y, plan.cells_y, plan.wide
    cells_x, length_x = plan.cells_x, plan.length_x
    block = 6 * plan.width_x
    per_c = 2 * cells_x
    narrow = plan.narrow
    lines = []
    for c in range(3):
        for j in range(2 * plan.width_x):
            row = c * 2 * plan.width_x + j
            lines.append(jnp.concatenate(
                [got[pl.ds(m * block + row, wide, stride=narrow * block), :] for m in range(narrow)], 1))
    lines = jnp.concatenate(lines, 0)
    high, low = halves(lines)
    waves = mul(high, y_high[...]) + (mul(low, y_high[...]) + mul(high, y_low[...]))
    for g in range(6):
        a, b = halves(waves[g * cells_x : (g + 1) * cells_x, :])
        mixed[g] = mul(x_ahead[...], jnp.concatenate([a, b, a], 0))
    step = 16
    for lane in range(0, half, 128):
        for row in range(0, length_x, step):
            left = slice(lane, lane + 128)
            right = slice(half + lane, half + lane + 128)
            cr, sr = slice(row, row + step), slice(length_x + row, length_x + row + step)
            fields = []
            for g in range(6):
                cp, sp = mixed[g, cr, left], mixed[g, sr, left]
                cq, sq = mixed[g, cr, right], mixed[g, sr, right]
                if lane == 0:
                    edge = lax.broadcasted_iota(jnp.int32, cp.shape, 1) == 0
                    cq0, sq0 = jnp.where(edge, 0.0, cq), jnp.where(edge, 0.0, sq)
                    fields.append((cp - sq0, -(sp + cq0),
                                   jnp.where(edge, cq, cp + sq), jnp.where(edge, -sq, cq - sp)))
                else:
                    fields.append((cp - sq, -(sp + cq), cp + sq, cq - sp))
            for i in range(3):
                sums = []
                for s, lanes_at in ((0, left), (2, right)):
                    real = imag = None
                    for j in range(3):
                        t = COUPLINGS[i][j]
                        ka = full[0, t, cr, lanes_at]
                        kb = full[slot, t, cr, lanes_at]
                        a, b = fields[2 * j], fields[2 * j + 1]
                        re = ka * a[s] - kb * b[s + 1]
                        im = ka * a[s + 1] + kb * b[s]
                        real = re if real is None else real + re
                        imag = im if imag is None else imag + im
                    sums.append((real, imag))
                (pr, pi), (mr, mi) = sums
                even_re, even_im, odd_re, odd_im = pr + mr, pi + mi, mi - pi, pr - mr
                if lane == 0:
                    even_re, even_im = jnp.where(edge, pr, even_re), jnp.where(edge, pi, even_im)
                    odd_re, odd_im = jnp.where(edge, mr, odd_re), jnp.where(edge, mi, odd_im)
                for value, at, lanes_at in (
                    (even_re, 0, left), (even_im, length_x, left),
                    (odd_re, 0, right), (odd_im, length_x, right),
                ):
                    a, b = halves(value)
                    packed[i, at + row : at + row + step, lanes_at] = a
                    packed[i, 2 * length_x + at + row : 2 * length_x + at + row + step, lanes_at] = b
    back = []
    for i in range(3):
        back.append(mul(xb_pair[...], packed[i]) + mul(xb_low[...], packed[i, : 2 * length_x, :]))
    high, low = halves(jnp.concatenate(back, 0))
    result = mul(high, yb_high[...]) + (mul(low, yb_high[...]) + mul(high, yb_low[...]))
    for c in range(3):
        for j in range(2 * plan.width_x):
            row = c * 2 * plan.width_x + j
            for m in range(narrow):
                out[pl.ds(m * block + row, wide, stride=narrow * block), :] = result[
                    row * wide : (row + 1) * wide, m * lanes : (m + 1) * lanes]


def local_kernel(plan, species, turned, side, before, after, material, saturation, anisotropy,
                 applied, out, woven):
    n = lax.axis_index("narrow")
    cells, layers = plan.layers * plan.width_x, plan.layers
    row = lax.broadcasted_iota(jnp.int32, (cells, plan.width_y), 0)
    col = lax.broadcasted_iota(jnp.int32, (cells, plan.width_y), 1)
    first, last = col == 0, col == plan.width_y - 1
    even = row % 2 == 0
    ahead = jnp.where(n == 0, 1.0, 0.0)
    sat = pick(material[...], saturation, species)
    anis = pick(material[...], anisotropy, species)
    sums, present, own = [], jnp.zeros((cells, plan.width_y), jnp.float32), []
    for c in range(3):
        d = turned[c * cells : (c + 1) * cells, :]
        s = side[c * cells : (c + 1) * cells, :]
        woven[pl.ds(0, layers, stride=2), :] = before[c * layers : (c + 1) * layers, :]
        woven[pl.ds(1, layers, stride=2), :] = after[c * layers : (c + 1) * layers, :]
        near = (
            jnp.where(row >= 2, pltpu.roll(d, 2, 0), 0.0),
            jnp.where(row < cells - 2, pltpu.roll(d, cells - 2, 0), 0.0),
            woven[...],
            jnp.where(even, pltpu.roll(d, cells - 1, 0), pltpu.roll(d, 1, 0)),
            pltpu.roll(jnp.where(first, s * ahead, d), plan.width_y - 1, 1),
            pltpu.roll(jnp.where(last, s * (1.0 - ahead), d), 1, 1),
        )
        total = near[0]
        present = present + near[0] * near[0]
        for v in near[1:]:
            total = total + v
            present = present + v * v
        sums.append(total)
        own.append(d)
    for c in range(3):
        field = exchange_coef * (sums[c] - present * own[c]) / sat + applied[c]
        if c == 2:
            field = field + 2.0 * anis / sat * own[2]
        out[c * cells : (c + 1) * cells, :] = field


def last_kernel(plan, species, got, t_high, t_low, base, turned, material, damping, rate, demag):
    cells = plan.layers * plan.width_x
    high, low = halves(got[...])
    demag[...] = mul(t_high[...], high) + (mul(t_low[...], high) + mul(t_high[...], low))
    damp = pick(material[...], damping, species)
    d = [turned[c * cells : (c + 1) * cells, :] for c in range(3)]
    f = [demag[c * cells : (c + 1) * cells, :] + base[c * cells : (c + 1) * cells, :] for c in range(3)]

    def turn(u, v):
        return [u[1] * v[2] - u[2] * v[1], u[2] * v[0] - u[0] * v[2], u[0] * v[1] - u[1] * v[0]]

    torque = turn(d, f)
    again = turn(d, torque)
    scale = -1.0 / (1.0 + damp * damp)
    for c in range(3):
        rate[c * cells : (c + 1) * cells, :] = (torque[c] + damp * again[c]) * scale


VMEM = pl.BlockSpec(memory_space=pltpu.VMEM)
SMEM = pl.BlockSpec(memory_space=pltpu.SMEM)
ANY = pl.BlockSpec(memory_space=pl.ANY)


def plane_shards(plan, spin, region, material, saturation, anisotropy, damping, applied, demag_spectrum):
    f32, bf16 = jnp.float32, jnp.bfloat16
    cells, lanes = plan.layers * plan.width_x, plan.width_y
    count, length_y, length_x = plan.devices * 6 * plan.width_x, plan.length_y, plan.length_x
    species = saturation.shape[0]
    shape = jax.ShapeDtypeStruct
    spin2 = spin.reshape(3 * cells, lanes)
    region2, material2 = region.reshape(cells, lanes), material.reshape(cells, lanes)
    ahead_z, back_z = plan.thickness_tables()
    ahead_y, back_y, ahead_x, back_x, flip = plan.lateral_tables()
    az, bz, ay, by = (split_table(t) for t in (ahead_z, back_z, ahead_y, back_y))
    ax, bx = split_table(ahead_x), split_table(back_x)
    x_ahead = np.concatenate([ax[0], ax[0], ax[1]], 1)
    xb_pair = np.concatenate([bx[0], bx[0]], 1)

    def call(body, out_shape, in_specs, out_specs, scratch, flops, limit=24 << 20):
        return pl.pallas_call(
            body, out_shape=out_shape, in_specs=in_specs, out_specs=out_specs, scratch_shapes=scratch,
            compiler_params=pltpu.CompilerParams(vmem_limit_bytes=limit),
            cost_estimate=pl.CostEstimate(flops=flops, bytes_accessed=1 << 20, transcendentals=0),
        )

    rows6 = 6 * plan.rows_x
    out, up, down, swap, zero, turned = call(
        partial(first_kernel, plan, species),
        (shape((count, lanes), f32), shape((3 * plan.layers, lanes), f32), shape((3 * plan.layers, lanes), f32),
         shape((rows6, length_y + lanes), f32), shape((rows6, length_y), f32), shape((3 * cells, lanes), f32)),
        [VMEM, VMEM, VMEM, SMEM, VMEM, VMEM, ANY],
        (VMEM,) * 6,
        [pltpu.VMEM((6, plan.rows_x, length_y), bf16), pltpu.VMEM((6, plan.rows_x, length_y), bf16),
         pltpu.SemaphoreType.DMA((2,))],
        1 << 28,
    )(spin2, region2, material2, saturation, jnp.asarray(az[0]), jnp.asarray(az[1]), demag_spectrum)

    both = ("wide", "narrow")
    swapped = lax.ppermute(swap, "narrow", [(0, 1), (1, 0)])
    zero_a = lax.ppermute(zero, both, [(0, plan.special)])
    zero_b = lax.ppermute(zero, both, [(1, plan.special)])
    blocks = (plan.devices, 3, 2 * plan.width_x, lanes)
    got = lax.all_to_all(out.reshape(blocks), both, 0, 0, tiled=True).reshape(count, lanes)

    full = call(
        partial(tensor_kernel, plan),
        shape((2, 6, length_x, length_y), f32),
        [VMEM, VMEM, VMEM, VMEM, ANY], VMEM,
        [pltpu.VMEM((6, plan.rows_x, length_y), bf16), pltpu.SemaphoreType.DMA((1,))],
        1 << 27,
    )(swapped, zero_a, zero_b, jnp.asarray(flip.astype(az[0].dtype)), demag_spectrum)

    sent = call(
        partial(plane_kernel, plan),
        shape((count, lanes), f32),
        [VMEM] * 9, VMEM,
        [pltpu.VMEM((6, 2 * length_x, length_y), f32), pltpu.VMEM((3, 4 * length_x, length_y), bf16),
         pltpu.VMEM((8, 128), f32)],
        1 << 29,
    )(got, jnp.asarray(ay[0]), jnp.asarray(ay[1]), jnp.asarray(x_ahead), jnp.asarray(xb_pair),
      jnp.asarray(bx[1]), jnp.asarray(by[0]), jnp.asarray(by[1]), full)

    back = lax.all_to_all(sent.reshape(blocks), both, 0, 0, tiled=True).reshape(count, lanes)
    rise = [(i, i + 1) for i in range(plan.wide - 1)]
    before = lax.ppermute(up, "wide", rise)
    after = lax.ppermute(down, "wide", [(j, i) for i, j in rise])
    base = pl.pallas_call(
        partial(local_kernel, plan, species),
        grid=(1,),
        out_shape=shape((3 * cells, lanes), f32),
        in_specs=[pl.BlockSpec((3 * cells, lanes), lambda i: (0, 0)),
                  pl.BlockSpec((3 * cells, lanes), lambda i: (0, length_y // lanes)),
                  pl.BlockSpec((3 * plan.layers, lanes), lambda i: (0, 0)),
                  pl.BlockSpec((3 * plan.layers, lanes), lambda i: (0, 0)),
                  pl.BlockSpec((cells, lanes), lambda i: (0, 0)), SMEM, SMEM, SMEM],
        out_specs=pl.BlockSpec((3 * cells, lanes), lambda i: (0, 0)),
        scratch_shapes=[pltpu.VMEM((cells, lanes), f32)],
        compiler_params=pltpu.CompilerParams(vmem_limit_bytes=16 << 20),
        cost_estimate=pl.CostEstimate(flops=1 << 22, bytes_accessed=1 << 19, transcendentals=0),
    )(turned, swapped, before, after, material2, saturation, anisotropy, applied)

    rate, demag = call(
        partial(last_kernel, plan, species),
        (shape((3 * cells, lanes), f32), shape((3 * cells, lanes), f32)),
        [VMEM] * 6 + [SMEM], (VMEM, VMEM), [], 1 << 28,
    )(back, jnp.asarray(bz[0]), jnp.asarray(bz[1]), base, turned, material2, damping)
    return rate.reshape(spin.shape), demag.reshape(spin.shape)


def shards(*args):
    spin, demag_spectrum = args[0], args[-1]
    components, layers, width_x, width_y = spin.shape
    parts, planes, rows_x, length_y = demag_spectrum.shape
    plan = Plan(lax.axis_size("wide"), lax.axis_size("narrow"), layers, width_x, width_y,
                planes, rows_x, length_y)
    if plan.fits():
        return plane_shards(plan, *args)
    return general_shards(*args)


def solution(mesh):
    placed = (
        P(None, None, "wide", "narrow"),
        P(None, "wide", "narrow"),
        P(None, "wide", "narrow"),
        P(),
        P(),
        P(),
        P(),
        P(None, "wide", "narrow", None),
    )
    return jax.shard_map(
        shards,
        mesh=mesh,
        in_specs=placed,
        out_specs=(P(None, None, "wide", "narrow"), P(None, None, "wide", "narrow")),
        check_vma=False,
    )
```

```python
from functools import partial
import math

import jax
import jax.numpy as jnp
import numpy as np
from jax import lax
from jax.experimental import pallas as pl
from jax.experimental.pallas import tpu as pltpu
from jax.sharding import PartitionSpec as P


exchange_coef = 0.3
highest = lax.Precision.HIGHEST


def extended(x, sides, width):
    for axis, dim in sides:
        peers, length = (lax.axis_size(axis), x.shape[dim])
        up = [(i, (i + 1) % peers) for i in range(peers - 1)]
        down = [(j, i) for i, j in up]
        last = lax.slice_in_dim(x, length - width, length, axis=dim)
        leading = lax.slice_in_dim(x, 0, width, axis=dim)
        before = lax.ppermute(last, axis, up)
        after = lax.ppermute(leading, axis, down)
        x = jnp.concatenate([before, x, after], axis=dim)
    return x


def phase_table(rows_count, cols_count, length, sign):
    left_index = lax.broadcasted_iota(jnp.int32, (rows_count, cols_count), 0)
    right_index = lax.broadcasted_iota(jnp.int32, (rows_count, cols_count), 1)
    angle = (left_index * right_index % length).astype(jnp.float32) * (2.0 * math.pi / length)
    return (jnp.cos(angle), sign * jnp.sin(angle))


def contract(pattern, phases, values):
    phase_re, phase_im = phases
    value_re, value_im = values
    product = partial(jnp.einsum, pattern, precision=highest)
    if value_im is None:
        return (product(phase_re, value_re), product(phase_im, value_re))
    return (
        product(phase_re, value_re) - product(phase_im, value_im),
        product(phase_re, value_im) + product(phase_im, value_re),
    )


def factors(half_size, at_end):
    if at_end:
        inner_size = math.gcd(half_size, 128)
    else:
        inner_size = max(
            (
                divisor
                for divisor in range(1, half_size + 1)
                if half_size % divisor == 0 and divisor * divisor <= 2 * half_size
            )
        )
    return (inner_size, 2 * half_size // inner_size)


def forward(values, at_end, natural):
    value_re, value_im = values
    extent = value_re.shape
    half_size = extent[1]
    length = 2 * half_size
    inner_size, outer_size = factors(half_size, at_end)
    tail_index = "" if at_end else "b"
    blocked = (extent[0], outer_size // 2, inner_size) + extent[2:]
    value_re = value_re.reshape(blocked)
    value_im = None if value_im is None else value_im.reshape(blocked)
    phases = phase_table(outer_size, outer_size // 2, outer_size, -1.0)
    work_re, work_im = contract(
        "kn,anp" + tail_index + "->akp" + tail_index, phases, (value_re, value_im)
    )
    twist_re, twist_im = phase_table(outer_size, inner_size, length, -1.0)
    if not at_end:
        twist_re, twist_im = (twist_re[:, :, None], twist_im[:, :, None])
    work_re, work_im = (
        work_re * twist_re - work_im * twist_im,
        work_re * twist_im + work_im * twist_re,
    )
    target = "ajk" if natural else "akj"
    phases = phase_table(inner_size, inner_size, inner_size, -1.0)
    out_re, out_im = contract(
        "jp,akp" + tail_index + "->" + target + tail_index, phases, (work_re, work_im)
    )
    merged = (extent[0], length) + extent[2:]
    return (out_re.reshape(merged), out_im.reshape(merged))


def inverse(values, at_end, natural, real_only):
    value_re, value_im = values
    extent = value_re.shape
    length = extent[1]
    half_size = length // 2
    inner_size, outer_size = factors(half_size, at_end)
    tail_index = "" if at_end else "b"
    if natural:
        blocked = (extent[0], inner_size, outer_size) + extent[2:]
        source = "ajk"
    else:
        blocked = (extent[0], outer_size, inner_size) + extent[2:]
        source = "akj"
    phases = phase_table(inner_size, inner_size, inner_size, 1.0)
    work_re, work_im = contract(
        "pj," + source + tail_index + "->akp" + tail_index,
        phases,
        (value_re.reshape(blocked), value_im.reshape(blocked)),
    )
    twist_re, twist_im = phase_table(outer_size, inner_size, length, 1.0)
    if not at_end:
        twist_re, twist_im = (twist_re[:, :, None], twist_im[:, :, None])
    work_re, work_im = (
        work_re * twist_re - work_im * twist_im,
        work_re * twist_im + work_im * twist_re,
    )
    phases = phase_table(outer_size // 2, outer_size, outer_size, 1.0)
    pattern = "nk,akp" + tail_index + "->anp" + tail_index
    scale = 1.0 / length
    merged = (extent[0], half_size) + extent[2:]
    if real_only:
        product = partial(jnp.einsum, pattern, precision=highest)
        result = product(phases[0], work_re) - product(phases[1], work_im)
        return result.reshape(merged) * scale
    out_re, out_im = contract(pattern, phases, (work_re, work_im))
    return (out_re.reshape(merged) * scale, out_im.reshape(merged) * scale)


def along_x(pieces):
    piece_re, piece_im = pieces
    members, planes, cells_x, cells_y = piece_re.shape
    extent = (members * planes, cells_x, cells_y)
    out_re, out_im = forward((piece_re.reshape(extent), piece_im.reshape(extent)), False, True)
    merged = (members, planes, 2 * cells_x, cells_y)
    return (out_re.reshape(merged), out_im.reshape(merged))


def along_y(pieces):
    piece_re, piece_im = pieces
    members, planes, rows_x, cells_y = piece_re.shape
    extent = (members * planes * rows_x, cells_y)
    out_re, out_im = forward((piece_re.reshape(extent), piece_im.reshape(extent)), True, False)
    merged = (members, planes, rows_x, 2 * cells_y)
    return (out_re.reshape(merged), out_im.reshape(merged))


def back_to_bricks(field_re, field_im):
    members, planes, rows_x, length_y = field_re.shape
    flattened = (members * planes * rows_x, length_y)
    grid_re, grid_im = inverse(
        (field_re.reshape(flattened), field_im.reshape(flattened)), True, False, False
    )
    merged = (members, planes, rows_x, length_y // 2)
    piece_re = lax.all_to_all(
        grid_re.reshape(merged), "narrow", split_axis=3, concat_axis=2, tiled=True
    )
    piece_im = lax.all_to_all(
        grid_im.reshape(merged), "narrow", split_axis=3, concat_axis=2, tiled=True
    )
    members, planes, length_x, cells_y = piece_re.shape
    extent = (members * planes, length_x, cells_y)
    out_re, out_im = inverse(
        (piece_re.reshape(extent), piece_im.reshape(extent)), False, True, False
    )
    invert_merged = (members, planes, length_x // 2, cells_y)
    columns = (out_re.reshape(invert_merged), out_im.reshape(invert_merged))
    piece_re, piece_im = lax.all_to_all(columns, "wide", split_axis=2, concat_axis=1, tiled=True)
    members, planes, cells_x, cells_y = piece_re.shape
    extent = (members, planes, cells_x * cells_y)
    result = inverse((piece_re.reshape(extent), piece_im.reshape(extent)), False, True, True)
    merged = (members, planes // 2, cells_x, cells_y)
    return result.reshape(merged)


def couple(kernel, values, picks):
    return -(
        kernel[picks[0]] * values[0] + kernel[picks[1]] * values[1] + kernel[picks[2]] * values[2]
    )


def cross(left, right):
    return jnp.stack(
        [
            left[1] * right[2] - left[2] * right[1],
            left[2] * right[0] - left[0] * right[2],
            left[0] * right[1] - left[1] * right[0],
        ]
    )


def general_shards(spin, region, material, saturation, anisotropy, damping, applied, demag_spectrum):
    magnet = region.astype(jnp.float32)
    direction = spin * magnet[None]
    species = saturation.shape[0]
    chosen = (
        material[None] == lax.broadcasted_iota(jnp.int32, (species,) + material.shape, 0)
    ).astype(jnp.float32)

    def lookup(entries):
        return jnp.sum(chosen * entries[:, None, None, None], axis=0)

    sat_cell = lookup(saturation)
    anis_cell = lookup(anisotropy)
    damp_cell = lookup(damping)
    moment = direction * sat_cell[None]
    components, layers, width_x, width_y = spin.shape
    flattened = moment.reshape(components, layers, width_x * width_y)
    spec_re, spec_im = forward((flattened, None), False, True)
    stacked = (components, 2 * layers, width_x, width_y)
    spectra = along_x(
        (
            lax.all_to_all(
                spec_re.reshape(stacked), "wide", split_axis=1, concat_axis=2, tiled=True
            ),
            lax.all_to_all(
                spec_im.reshape(stacked), "wide", split_axis=1, concat_axis=2, tiled=True
            ),
        )
    )
    spec_re, spec_im = along_y(
        lax.all_to_all(spectra, "narrow", split_axis=2, concat_axis=3, tiled=True)
    )
    parts, planes, rows_x, length_y = demag_spectrum.shape
    inner_size, outer_size = factors(length_y // 2, True)
    kernel = demag_spectrum.reshape(parts, planes, rows_x, inner_size, outer_size)
    kernel = (
        kernel.transpose(0, 1, 2, 4, 3).reshape(parts, planes, rows_x, length_y).astype(jnp.float32)
    )
    couplings = ((0, 3, 4), (3, 1, 5), (4, 5, 2))
    field_re = [couple(kernel, spec_re, picks) for picks in couplings]
    field_im = [couple(kernel, spec_im, picks) for picks in couplings]
    demag = back_to_bricks(jnp.stack(field_re), jnp.stack(field_im))
    framed = extended(direction, (("wide", 2), ("narrow", 3)), 1)
    framed = jnp.pad(framed, ((0, 0), (1, 1), (0, 0), (0, 0)))
    weight = jnp.sum(framed * framed, axis=0)
    neighbours = (
        framed[:, 2:, 1:-1, 1:-1]
        + framed[:, :-2, 1:-1, 1:-1]
        + framed[:, 1:-1, 2:, 1:-1]
        + framed[:, 1:-1, :-2, 1:-1]
        + framed[:, 1:-1, 1:-1, 2:]
        + framed[:, 1:-1, 1:-1, :-2]
    )
    present = (
        weight[2:, 1:-1, 1:-1]
        + weight[:-2, 1:-1, 1:-1]
        + weight[1:-1, 2:, 1:-1]
        + weight[1:-1, :-2, 1:-1]
        + weight[1:-1, 1:-1, 2:]
        + weight[1:-1, 1:-1, :-2]
    )
    laplace = neighbours - present[None] * direction
    zeros = jnp.zeros_like(sat_cell)
    uniaxial = jnp.stack([zeros, zeros, 2.0 * anis_cell / sat_cell * direction[2]])
    field = (
        exchange_coef * laplace / sat_cell[None] + demag + applied[:, None, None, None] + uniaxial
    )
    torque = cross(direction, field)
    rate = (
        -(torque + damp_cell[None] * cross(direction, torque)) / (1.0 + damp_cell * damp_cell)[None]
    )
    return (rate, demag)


def split_table(table):
    high = jnp.asarray(np.asarray(table, np.float32)).astype(jnp.bfloat16)
    high64 = np.asarray(np.asarray(table, np.float32).astype(high.dtype), np.float64)
    low = (table - high64).astype(np.float32).astype(high.dtype)
    return np.asarray(high64.astype(high.dtype)), low


class Plan:
    def __init__(self, wide, narrow, layers, width_x, width_y, planes, rows_x, length_y):
        self.wide, self.narrow = wide, narrow
        self.layers, self.width_x, self.width_y = layers, width_x, width_y
        self.planes, self.rows_x = planes, rows_x
        self.length_z, self.length_x, self.length_y = planes * wide, rows_x * narrow, length_y
        self.cells_x, self.cells_y = width_x * wide, width_y * narrow
        self.devices = wide * narrow
        self.special = self.narrow * (wide // 2) + 1

    def fits(self):
        return (
            self.narrow == 2
            and self.planes == 4
            and self.wide % 16 == 0
            and self.devices * 2 == self.length_z
            and self.length_z == 2 * self.layers
            and self.length_x == 2 * self.cells_x
            and self.length_y == 2 * self.cells_y
            and self.width_x == 2
            and self.width_y % 128 == 0
            and self.rows_x % 16 == 0
            and (self.layers * self.width_x) % 8 == 0
            and 6 * self.rows_x == 3 * self.layers * self.width_x
        )

    def wave(self):
        w, n = np.divmod(np.arange(self.devices), self.narrow)
        return self.planes * w + np.where(w < self.wide // 2, 1 + n, 1 - n)

    def thickness_tables(self):
        wave = self.wave()
        z = np.arange(self.layers)
        angle = 2.0 * np.pi * ((wave[:, None] * z[None]) % self.length_z) / self.length_z
        ahead = np.stack([np.cos(angle), -np.sin(angle)], 1)
        back = np.stack([2.0 * np.cos(angle), -2.0 * np.sin(angle)], 1)
        ahead[self.special, 1] = 1.0
        back[self.special, 0] = np.cos(angle[self.special])
        back[self.special, 1] = 1.0
        back *= -1.0 / (self.length_z * self.length_x * self.length_y)
        n = np.arange(self.devices) % self.narrow
        x = np.arange(self.width_x)
        sign = 1.0 - 2.0 * ((n[:, None] * x[None]) % 2)
        unit_c, unit_x = np.eye(3), np.eye(self.width_x)
        ahead = np.einsum("drz,dx,cb,xv->dcrxbzv", ahead, sign, unit_c, unit_x)
        back = np.einsum("drz,dx,cb,xv->bzvdcrx", back, sign, unit_c, unit_x)
        count = self.devices * 6 * self.width_x
        cells = 3 * self.layers * self.width_x
        return ahead.reshape(count, cells), back.reshape(cells, count)

    def lateral_tables(self):
        half = self.cells_y
        y, k = np.arange(half), np.arange(half)
        angle = 2.0 * np.pi * ((y[:, None] * k[None]) % self.length_y) / self.length_y
        cosine, sine = np.cos(angle), np.sin(angle)
        sine[:, 0] = 1.0 - 2.0 * (y % 2)
        ahead_y = np.concatenate([cosine, sine], 1)
        back_y = np.ascontiguousarray(ahead_y.T)
        x = (np.arange(self.wide)[None] * self.width_x + np.arange(self.width_x)[:, None]).reshape(-1)
        kx = np.arange(self.length_x)
        angle = 2.0 * np.pi * ((kx[:, None] * x[None]) % self.length_x) / self.length_x
        cosine, sine = np.cos(angle), np.sin(angle)
        ahead_x = np.concatenate([cosine, sine], 0)
        back_x = np.block([[cosine.T, -sine.T], [sine.T, cosine.T]])
        return ahead_y, back_y, ahead_x, back_x


def halves(value):
    high = value.astype(jnp.bfloat16)
    return high, (value - high.astype(jnp.float32)).astype(jnp.bfloat16)


def mul(left, right):
    return jnp.dot(left, right, preferred_element_type=jnp.float32)


def pick(material, entries, species):
    value = jnp.zeros(material.shape, jnp.float32)
    for s in range(species):
        value = jnp.where(material == s, entries[s], value)
    return value


def rows_of(plan):
    w, n = lax.axis_index("wide"), lax.axis_index("narrow")
    low = w < plan.wide // 2
    own = jnp.where(low, 1 + n, 1 - n)
    other = jnp.where(low, 2 - n, n)
    return w, n, own, other


def first_kernel(plan, species, spin_at, region_at, material_at, saturation_at, table_at, tensor,
                 out_at, near_at, next_at, swap_at, zero_at, edge_at, turned_at,
                 spin, region, material, saturation, table, held, held0,
                 out, near, next_, swap, zero, edge, turned, sems, done):
    w, _, _, other = rows_of(plan)
    count = plan.rows_x
    moves = [
        pltpu.make_async_copy(source, target, sems.at[k])
        for k, (source, target) in enumerate((
            (saturation_at, saturation), (material_at, material), (region_at, region), (spin_at, spin),
            (table_at, table), (tensor.at[:, other], held),
        ))
    ]
    for move in moves:
        move.start()
    fetch0 = pltpu.make_async_copy(tensor.at[:, 0], held0, sems.at[6])
    send0 = pltpu.make_async_copy(zero, zero_at, sems.at[7])

    @pl.when(w == 0)
    def _():
        fetch0.start()

    sent = []

    def send(source, target):
        move = pltpu.make_async_copy(source, target, done.at[len(sent)])
        move.start()
        sent.append(move)

    for move in moves[:4]:
        move.wait()
    cells = plan.layers * plan.width_x
    magnet = region[...].astype(jnp.float32)
    sat = pick(material[...], saturation, species)
    high, low = [], []
    for c in range(3):
        direction = spin[c * cells : (c + 1) * cells, :] * magnet
        turned[c * cells : (c + 1) * cells, :] = direction
        swap[c * cells : (c + 1) * cells, plan.length_y :] = direction
        a, b = halves(direction * sat)
        high.append(a)
        low.append(b)
    high, low = jnp.concatenate(high, 0), jnp.concatenate(low, 0)
    send(turned, turned_at)
    moves[5].wait()
    for t in range(6):
        rows = slice(t * count, (t + 1) * count)
        swap[rows, : plan.length_y] = held[t].astype(jnp.float32)
    send(swap, swap_at)
    moves[4].wait()
    lines = out.shape[0]
    t_high, t_low = table[:lines, :], table[lines:, :]
    out[...] = mul(t_high, high) + (mul(t_low, high) + mul(t_high, low))
    send(out, out_at)
    layers3 = 3 * plan.layers
    up, down = turned[pl.ds(1, layers3, stride=2), :], turned[pl.ds(0, layers3, stride=2), :]
    near[...] = jnp.where(w % 2 == 0, up, down)
    next_[...] = jnp.where(w % 2 == 0, down, up)
    send(near, near_at)
    send(next_, next_at)

    @pl.when(w == 0)
    def _():
        fetch0.wait()
        for t in range(6):
            zero[t * count : (t + 1) * count, :] = held0[t].astype(jnp.float32)
            edge[t : t + 1, :] = held0[t, 0:1, :].astype(jnp.float32)
        edge[6:8, :] = jnp.zeros((2, plan.length_y), jnp.float32)
        send0.start()
        last = pltpu.make_async_copy(edge, edge_at, sems.at[8])
        last.start()
        last.wait()
        send0.wait()

    for move in sent:
        move.wait()


def flip_of(half):
    sum_of = lax.broadcasted_iota(jnp.int32, (half, half), 0) + lax.broadcasted_iota(jnp.int32, (half, half), 1)
    return jnp.where((sum_of == half) | (sum_of == 0), 1.0, 0.0).astype(jnp.bfloat16)


def own_kernel(plan, tensor, table, full, held, sems):
    _, _, own, _ = rows_of(plan)
    fetch = pltpu.make_async_copy(tensor.at[:, own], held, sems.at[0])
    fetch.start()
    half = plan.cells_y
    flip = flip_of(half)
    fetch.wait()
    for t in range(6):
        values = held[t]
        full[t, :, :half] = values[:, :half].astype(jnp.float32)
        full[t, :, half:] = mul(values[:, half:], flip)


def far_kernel(plan, swapped, zero_at, edge_at, full, second, zero, edge, sems):
    w, n, _, _ = rows_of(plan)
    half, count = plan.cells_y, plan.rows_x
    flip = flip_of(half)
    for t in range(6):
        rows = slice(t * count, (t + 1) * count)
        full[t, :, :half] = swapped[rows, :half]
        full[t, :, half:] = mul(swapped[rows, half : 2 * half].astype(jnp.bfloat16), flip)

    @pl.when(jnp.logical_and(w == plan.wide // 2, n == 1))
    def _():
        moves = [pltpu.make_async_copy(zero_at, zero, sems.at[0]), pltpu.make_async_copy(edge_at, edge, sems.at[1])]
        for move in moves:
            move.start()
        for move in moves:
            move.wait()
        row = lax.broadcasted_iota(jnp.int32, (count, count), 0)
        col = lax.broadcasted_iota(jnp.int32, (count, count), 1)
        turn = jnp.where(row + col == count, 1.0, 0.0).astype(jnp.bfloat16)
        first = lax.broadcasted_iota(jnp.int32, (count, half), 0) == 0
        lane0 = lax.broadcasted_iota(jnp.int32, (count, half), 1) == 0
        edge_low = edge[:, :half]
        edge_high = mul(edge[:, half:].astype(jnp.bfloat16), flip)
        for t in range(6):
            rows = slice(t * count, (t + 1) * count)
            plus = zero[rows, :half]
            minus = mul(zero[rows, half:].astype(jnp.bfloat16), flip)
            second[t, :count, :half] = plus
            second[t, :count, half:] = minus
            swap_plus = mul(turn, jnp.where(lane0, plus, minus).astype(jnp.bfloat16))
            swap_minus = mul(turn, jnp.where(lane0, minus, plus).astype(jnp.bfloat16))
            second[t, count:, :half] = jnp.where(first, edge_low[t : t + 1, :], swap_plus)
            second[t, count:, half:] = jnp.where(first, edge_high[t : t + 1, :], swap_minus)


COUPLINGS = ((0, 3, 4), (3, 1, 5), (4, 5, 2))


def plane_kernel(plan, got, table, own_part, far_part, second, out, mixed, packed):
    w, n, _, _ = rows_of(plan)
    lanes, half, wide = plan.width_y, plan.cells_y, plan.wide
    cells_x, length_x = plan.cells_x, plan.length_x
    block = 6 * plan.width_x
    per_c = 2 * cells_x
    narrow = plan.narrow
    lines = []
    for c in range(3):
        for j in range(2 * plan.width_x):
            row = c * 2 * plan.width_x + j
            lines.append(jnp.concatenate(
                [got[pl.ds(m * block + row, wide, stride=narrow * block), :] for m in range(narrow)], 1))
    lines = jnp.concatenate(lines, 0)
    high, low = halves(lines)
    y_high, y_low = table[:half, :], table[half : 2 * half, :]
    base = 4 * half
    x_ahead = table[base : base + 2 * length_x, : 3 * cells_x]
    xb_pair = table[base : base + per_c, half : half + 4 * length_x]
    xb_low = table[base + per_c : base + 2 * per_c, half : half + 2 * length_x]
    waves = mul(high, y_high) + (mul(low, y_high) + mul(high, y_low))
    for g in range(6):
        a, b = halves(waves[g * cells_x : (g + 1) * cells_x, :])
        mixed[g] = mul(x_ahead, jnp.concatenate([a, b, a], 0))
    step = 16

    def couple(paired):
        for lane in range(0, half, 128):
            for row in range(0, length_x, step):
                left = slice(lane, lane + 128)
                right = slice(half + lane, half + lane + 128)
                cr, sr = slice(row, row + step), slice(length_x + row, length_x + row + step)
                part = own_part if row < plan.rows_x else far_part
                at = slice(row % plan.rows_x, row % plan.rows_x + step)
                fields = []
                for g in range(6):
                    cp, sp = mixed[g, cr, left], mixed[g, sr, left]
                    cq, sq = mixed[g, cr, right], mixed[g, sr, right]
                    if lane == 0:
                        edge = lax.broadcasted_iota(jnp.int32, cp.shape, 1) == 0
                        cq0, sq0 = jnp.where(edge, 0.0, cq), jnp.where(edge, 0.0, sq)
                        fields.append((cp - sq0, -(sp + cq0),
                                       jnp.where(edge, cq, cp + sq), jnp.where(edge, -sq, cq - sp)))
                    else:
                        fields.append((cp - sq, -(sp + cq), cp + sq, cq - sp))
                if not paired:
                    fields = [
                        (a[0] - b[1], a[1] + b[0], a[2] - b[3], a[3] + b[2])
                        for a, b in zip(fields[0::2], fields[1::2])
                    ]
                for i in range(3):
                    sums = []
                    for s, lanes_at in ((0, left), (2, right)):
                        real = imag = None
                        for j in range(3):
                            t = COUPLINGS[i][j]
                            ka = part[t, at, lanes_at]
                            if paired:
                                kb = second[t, cr, lanes_at]
                                a, b = fields[2 * j], fields[2 * j + 1]
                                re = ka * a[s] - kb * b[s + 1]
                                im = ka * a[s + 1] + kb * b[s]
                            else:
                                re, im = ka * fields[j][s], ka * fields[j][s + 1]
                            real = re if real is None else real + re
                            imag = im if imag is None else imag + im
                        sums.append((real, imag))
                    (pr, pi), (mr, mi) = sums
                    even_re, even_im, odd_re, odd_im = pr + mr, pi + mi, mi - pi, pr - mr
                    if lane == 0:
                        even_re, even_im = jnp.where(edge, pr, even_re), jnp.where(edge, pi, even_im)
                        odd_re, odd_im = jnp.where(edge, mr, odd_re), jnp.where(edge, mi, odd_im)
                    for value, base_at, lanes_at in (
                        (even_re, 0, left), (even_im, length_x, left),
                        (odd_re, 0, right), (odd_im, length_x, right),
                    ):
                        a, b = halves(value)
                        high_at, low_at = base_at + row, 2 * length_x + base_at + row
                        packed[i, high_at : high_at + step, lanes_at] = a
                        packed[i, low_at : low_at + step, lanes_at] = b

    special = jnp.logical_and(w == plan.wide // 2, n == 1)
    pl.when(special)(lambda: couple(True))
    pl.when(jnp.logical_not(special))(lambda: couple(False))
    back = []
    for i in range(3):
        back.append(mul(xb_pair, packed[i]) + mul(xb_low, packed[i, : 2 * length_x, :]))
    high, low = halves(jnp.concatenate(back, 0))
    result = None
    for k in (slice(0, half), slice(half, 2 * half)):
        yb_high, yb_low = table[2 * half : 3 * half, k], table[3 * half : 4 * half, k]
        part = mul(high[:, k], yb_high) + (mul(low[:, k], yb_high) + mul(high[:, k], yb_low))
        result = part if result is None else result + part
    for c in range(3):
        for j in range(2 * plan.width_x):
            row = c * 2 * plan.width_x + j
            for m in range(narrow):
                out[pl.ds(m * block + row, wide, stride=narrow * block), :] = result[
                    row * wide : (row + 1) * wide, m * lanes : (m + 1) * lanes]


def local_kernel(plan, species, turned, side, near, next_, material, saturation, anisotropy,
                 applied, table, out, woven):
    w, n = lax.axis_index("wide"), lax.axis_index("narrow")
    cells, layers = plan.layers * plan.width_x, plan.layers
    row = lax.broadcasted_iota(jnp.int32, (cells, plan.width_y), 0)
    col = lax.broadcasted_iota(jnp.int32, (cells, plan.width_y), 1)
    first, last = col == 0, col == plan.width_y - 1
    even = row % 2 == 0
    ahead = jnp.where(n == 0, 1.0, 0.0)
    sat = pick(material[...], saturation, species)
    anis = pick(material[...], anisotropy, species)
    sums, present, own = [], jnp.zeros((cells, plan.width_y), jnp.float32), []
    for c in range(3):
        d = turned[c * cells : (c + 1) * cells, :]
        s = side[c * cells : (c + 1) * cells, :]
        a, b = near[c * layers : (c + 1) * layers, :], next_[c * layers : (c + 1) * layers, :]
        woven[pl.ds(0, layers, stride=2), :] = jnp.where(w % 2 == 0, b, a)
        woven[pl.ds(1, layers, stride=2), :] = jnp.where(w % 2 == 0, a, b)
        beside = (
            jnp.where(row >= 2, pltpu.roll(d, 2, 0), 0.0),
            jnp.where(row < cells - 2, pltpu.roll(d, cells - 2, 0), 0.0),
            woven[...],
            jnp.where(even, pltpu.roll(d, cells - 1, 0), pltpu.roll(d, 1, 0)),
            pltpu.roll(jnp.where(first, s * ahead, d), plan.width_y - 1, 1),
            pltpu.roll(jnp.where(last, s * (1.0 - ahead), d), 1, 1),
        )
        total = beside[0]
        present = present + beside[0] * beside[0]
        for v in beside[1:]:
            total = total + v
            present = present + v * v
        sums.append(total)
        own.append(d)
    for c in range(3):
        field = exchange_coef * (sums[c] - present * own[c]) / sat + applied[c]
        if c == 2:
            field = field + 2.0 * anis / sat * own[2]
        out[c * cells : (c + 1) * cells, :] = field


def last_kernel(plan, species, got, table, base, turned, material, damping, rate, demag):
    cells = plan.layers * plan.width_x
    t_high, t_low = table[: 3 * cells, :], table[3 * cells :, :]
    high, low = halves(got[...])
    demag[...] = mul(t_high, high) + (mul(t_low, high) + mul(t_high, low))
    damp = pick(material[...], damping, species)
    d = [turned[c * cells : (c + 1) * cells, :] for c in range(3)]
    f = [demag[c * cells : (c + 1) * cells, :] + base[c * cells : (c + 1) * cells, :] for c in range(3)]

    def turn(u, v):
        return [u[1] * v[2] - u[2] * v[1], u[2] * v[0] - u[0] * v[2], u[0] * v[1] - u[1] * v[0]]

    torque = turn(d, f)
    again = turn(d, torque)
    scale = -1.0 / (1.0 + damp * damp)
    for c in range(3):
        rate[c * cells : (c + 1) * cells, :] = (torque[c] + damp * again[c]) * scale


LIMITS = (67043328, 24 << 20, 24 << 20, 16 << 20, 24 << 20)
VMEM = pl.BlockSpec(memory_space=pltpu.VMEM)
SMEM = pl.BlockSpec(memory_space=pltpu.SMEM)
HBM = pl.BlockSpec(memory_space=pltpu.HBM)


def plane_shards(plan, spin, region, material, saturation, anisotropy, damping, applied, demag_spectrum):
    f32, bf16 = jnp.float32, jnp.bfloat16
    cells, lanes = plan.layers * plan.width_x, plan.width_y
    count, length_y, length_x = plan.devices * 6 * plan.width_x, plan.length_y, plan.length_x
    species = saturation.shape[0]
    shape = jax.ShapeDtypeStruct
    spin2 = spin.reshape(3 * cells, lanes)
    region2, material2 = region.reshape(cells, lanes), material.reshape(cells, lanes)
    ahead_z, back_z = plan.thickness_tables()
    ahead_y, back_y, ahead_x, back_x = plan.lateral_tables()
    az, bz, ay, by = (split_table(t) for t in (ahead_z, back_z, ahead_y, back_y))
    ax, bx = split_table(ahead_x), split_table(back_x)
    x_ahead = np.concatenate([ax[0], ax[0], ax[1]], 1)
    xb_pair = np.concatenate([bx[0], bx[0]], 1)

    def call(body, out_shape, in_specs, out_specs, scratch, flops, limit=24 << 20):
        return pl.pallas_call(
            body, out_shape=out_shape, in_specs=in_specs, out_specs=out_specs, scratch_shapes=scratch,
            compiler_params=pltpu.CompilerParams(vmem_limit_bytes=limit),
            cost_estimate=pl.CostEstimate(flops=flops, bytes_accessed=1 << 20, transcendentals=0),
        )

    rows6 = 6 * plan.rows_x
    table_in, table_out = jnp.asarray(np.concatenate(az, 0)), jnp.asarray(np.concatenate(bz, 0))
    outs = ((count, lanes), (3 * plan.layers, lanes), (3 * plan.layers, lanes), (rows6, length_y + lanes),
            (rows6, length_y), (8, length_y), (3 * cells, lanes))
    out, near, next_, swap, zero, edge, turned = call(
        partial(first_kernel, plan, species),
        tuple(shape(o, f32) for o in outs), [HBM] * 6, (HBM,) * len(outs),
        [pltpu.VMEM((3 * cells, lanes), f32), pltpu.VMEM((cells, lanes), jnp.int32),
         pltpu.VMEM((cells, lanes), jnp.int32), pltpu.SMEM((species,), f32),
         pltpu.VMEM(table_in.shape, bf16),
         pltpu.VMEM((6, plan.rows_x, length_y), bf16), pltpu.VMEM((6, plan.rows_x, length_y), bf16)]
        + [pltpu.VMEM(o, f32) for o in outs]
        + [pltpu.SemaphoreType.DMA((9,)), pltpu.SemaphoreType.DMA((5,))],
        1 << 28, LIMITS[0],
    )(spin2, region2, material2, saturation, table_in, demag_spectrum)

    both = ("wide", "narrow")
    swapped = lax.ppermute(swap, "narrow", [(0, 1), (1, 0)])
    blocks = (plan.devices, 3, 2 * plan.width_x, lanes)
    got = lax.all_to_all(out.reshape(blocks), both, 0, 0, tiled=True).reshape(count, lanes)
    edge_a = lax.ppermute(edge, both, [(0, plan.special)])
    zero_b = lax.ppermute(zero, both, [(1, plan.special)])
    pairs = [(i ^ 1, i) for i in range(plan.wide)]
    near = lax.ppermute(near, "wide", pairs)
    pairs = [(i, j) for i in range(1, plan.wide - 1, 2) for i, j in ((i, i + 1), (i + 1, i))]
    next_ = lax.ppermute(next_, "wide", pairs)

    half = plan.cells_y
    folded = [np.concatenate([t[:half], t[half:]], 1) for t in by]
    small = np.zeros((2 * length_x, 2 * half), az[0].dtype)
    small[:, : 3 * plan.cells_x] = x_ahead
    small[: 2 * plan.cells_x, half : half + 4 * length_x] = xb_pair
    small[2 * plan.cells_x : 4 * plan.cells_x, half : half + 2 * length_x] = bx[1]
    table = jnp.asarray(np.concatenate([ay[0], ay[1], *folded, small], 0))

    own_part = call(
        partial(own_kernel, plan), shape((6, plan.rows_x, length_y), f32), [HBM, VMEM], VMEM,
        [pltpu.VMEM((6, plan.rows_x, length_y), bf16), pltpu.SemaphoreType.DMA((1,))], 1 << 26, LIMITS[1],
    )(demag_spectrum, table)
    far_part, second = call(
        partial(far_kernel, plan),
        (shape((6, plan.rows_x, length_y), f32), shape((6, length_x, length_y), f32)),
        [VMEM, HBM, HBM], (VMEM, VMEM),
        [pltpu.VMEM((rows6, length_y), f32), pltpu.VMEM((8, length_y), f32), pltpu.SemaphoreType.DMA((2,))],
        1 << 26, LIMITS[1],
    )(swapped, zero_b, edge_a)

    sent = call(
        partial(plane_kernel, plan),
        shape((count, lanes), f32),
        [VMEM] * 5, VMEM,
        [pltpu.VMEM((6, 2 * length_x, length_y), f32), pltpu.VMEM((3, 4 * length_x, length_y), bf16)],
        1 << 29, LIMITS[2],
    )(got, table, own_part, far_part, second)

    back = lax.all_to_all(sent.reshape(blocks), both, 0, 0, tiled=True).reshape(count, lanes)
    base = pl.pallas_call(
        partial(local_kernel, plan, species),
        grid=(1,),
        out_shape=shape((3 * cells, lanes), f32),
        in_specs=[pl.BlockSpec((3 * cells, lanes), lambda i: (0, 0)),
                  pl.BlockSpec((3 * cells, lanes), lambda i: (0, length_y // lanes)),
                  pl.BlockSpec((3 * plan.layers, lanes), lambda i: (0, 0)),
                  pl.BlockSpec((3 * plan.layers, lanes), lambda i: (0, 0)),
                  pl.BlockSpec((cells, lanes), lambda i: (0, 0)), SMEM, SMEM, SMEM, VMEM],
        out_specs=pl.BlockSpec((3 * cells, lanes), lambda i: (0, 0)),
        scratch_shapes=[pltpu.VMEM((cells, lanes), f32)],
        compiler_params=pltpu.CompilerParams(vmem_limit_bytes=LIMITS[3]),
        cost_estimate=pl.CostEstimate(flops=1 << 22, bytes_accessed=1 << 19, transcendentals=0),
    )(turned, swapped, near, next_, material2, saturation, anisotropy, applied, table_out)

    rate, demag = call(
        partial(last_kernel, plan, species),
        (shape((3 * cells, lanes), f32), shape((3 * cells, lanes), f32)),
        [VMEM] * 5 + [SMEM], (VMEM, VMEM), [], 1 << 28, LIMITS[4],
    )(back, table_out, base, turned, material2, damping)
    return rate.reshape(spin.shape), demag.reshape(spin.shape)


def shards(*args):
    spin, demag_spectrum = args[0], args[-1]
    _, layers, width_x, width_y = spin.shape
    _, planes, rows_x, length_y = demag_spectrum.shape
    plan = Plan(lax.axis_size("wide"), lax.axis_size("narrow"), layers, width_x, width_y,
                planes, rows_x, length_y)
    if plan.fits():
        return plane_shards(plan, *args)
    return general_shards(*args)


def solution(mesh):
    placed = (
        P(None, None, "wide", "narrow"),
        P(None, "wide", "narrow"),
        P(None, "wide", "narrow"),
        P(),
        P(),
        P(),
        P(),
        P(None, "wide", "narrow", None),
    )
    return jax.shard_map(
        shards,
        mesh=mesh,
        in_specs=placed,
        out_specs=(P(None, None, "wide", "narrow"), P(None, None, "wide", "narrow")),
        check_vma=False,
    )
```

```python
from functools import partial
import math

import jax
import jax.numpy as jnp
import numpy as np
from jax import lax
from jax.experimental import pallas as pl
from jax.experimental.pallas import tpu as pltpu
from jax.sharding import PartitionSpec as P


exchange_coef = 0.3
highest = lax.Precision.HIGHEST


def extended(x, sides, width):
    for axis, dim in sides:
        peers, length = (lax.axis_size(axis), x.shape[dim])
        up = [(i, (i + 1) % peers) for i in range(peers - 1)]
        down = [(j, i) for i, j in up]
        last = lax.slice_in_dim(x, length - width, length, axis=dim)
        leading = lax.slice_in_dim(x, 0, width, axis=dim)
        before = lax.ppermute(last, axis, up)
        after = lax.ppermute(leading, axis, down)
        x = jnp.concatenate([before, x, after], axis=dim)
    return x


def phase_table(rows_count, cols_count, length, sign):
    left_index = lax.broadcasted_iota(jnp.int32, (rows_count, cols_count), 0)
    right_index = lax.broadcasted_iota(jnp.int32, (rows_count, cols_count), 1)
    angle = (left_index * right_index % length).astype(jnp.float32) * (2.0 * math.pi / length)
    return (jnp.cos(angle), sign * jnp.sin(angle))


def contract(pattern, phases, values):
    phase_re, phase_im = phases
    value_re, value_im = values
    product = partial(jnp.einsum, pattern, precision=highest)
    if value_im is None:
        return (product(phase_re, value_re), product(phase_im, value_re))
    return (
        product(phase_re, value_re) - product(phase_im, value_im),
        product(phase_re, value_im) + product(phase_im, value_re),
    )


def factors(half_size, at_end):
    if at_end:
        inner_size = math.gcd(half_size, 128)
    else:
        inner_size = max(
            (
                divisor
                for divisor in range(1, half_size + 1)
                if half_size % divisor == 0 and divisor * divisor <= 2 * half_size
            )
        )
    return (inner_size, 2 * half_size // inner_size)


def forward(values, at_end, natural):
    value_re, value_im = values
    extent = value_re.shape
    half_size = extent[1]
    length = 2 * half_size
    inner_size, outer_size = factors(half_size, at_end)
    tail_index = "" if at_end else "b"
    blocked = (extent[0], outer_size // 2, inner_size) + extent[2:]
    value_re = value_re.reshape(blocked)
    value_im = None if value_im is None else value_im.reshape(blocked)
    phases = phase_table(outer_size, outer_size // 2, outer_size, -1.0)
    work_re, work_im = contract(
        "kn,anp" + tail_index + "->akp" + tail_index, phases, (value_re, value_im)
    )
    twist_re, twist_im = phase_table(outer_size, inner_size, length, -1.0)
    if not at_end:
        twist_re, twist_im = (twist_re[:, :, None], twist_im[:, :, None])
    work_re, work_im = (
        work_re * twist_re - work_im * twist_im,
        work_re * twist_im + work_im * twist_re,
    )
    target = "ajk" if natural else "akj"
    phases = phase_table(inner_size, inner_size, inner_size, -1.0)
    out_re, out_im = contract(
        "jp,akp" + tail_index + "->" + target + tail_index, phases, (work_re, work_im)
    )
    merged = (extent[0], length) + extent[2:]
    return (out_re.reshape(merged), out_im.reshape(merged))


def inverse(values, at_end, natural, real_only):
    value_re, value_im = values
    extent = value_re.shape
    length = extent[1]
    half_size = length // 2
    inner_size, outer_size = factors(half_size, at_end)
    tail_index = "" if at_end else "b"
    if natural:
        blocked = (extent[0], inner_size, outer_size) + extent[2:]
        source = "ajk"
    else:
        blocked = (extent[0], outer_size, inner_size) + extent[2:]
        source = "akj"
    phases = phase_table(inner_size, inner_size, inner_size, 1.0)
    work_re, work_im = contract(
        "pj," + source + tail_index + "->akp" + tail_index,
        phases,
        (value_re.reshape(blocked), value_im.reshape(blocked)),
    )
    twist_re, twist_im = phase_table(outer_size, inner_size, length, 1.0)
    if not at_end:
        twist_re, twist_im = (twist_re[:, :, None], twist_im[:, :, None])
    work_re, work_im = (
        work_re * twist_re - work_im * twist_im,
        work_re * twist_im + work_im * twist_re,
    )
    phases = phase_table(outer_size // 2, outer_size, outer_size, 1.0)
    pattern = "nk,akp" + tail_index + "->anp" + tail_index
    scale = 1.0 / length
    merged = (extent[0], half_size) + extent[2:]
    if real_only:
        product = partial(jnp.einsum, pattern, precision=highest)
        result = product(phases[0], work_re) - product(phases[1], work_im)
        return result.reshape(merged) * scale
    out_re, out_im = contract(pattern, phases, (work_re, work_im))
    return (out_re.reshape(merged) * scale, out_im.reshape(merged) * scale)


def along_x(pieces):
    piece_re, piece_im = pieces
    members, planes, cells_x, cells_y = piece_re.shape
    extent = (members * planes, cells_x, cells_y)
    out_re, out_im = forward((piece_re.reshape(extent), piece_im.reshape(extent)), False, True)
    merged = (members, planes, 2 * cells_x, cells_y)
    return (out_re.reshape(merged), out_im.reshape(merged))


def along_y(pieces):
    piece_re, piece_im = pieces
    members, planes, rows_x, cells_y = piece_re.shape
    extent = (members * planes * rows_x, cells_y)
    out_re, out_im = forward((piece_re.reshape(extent), piece_im.reshape(extent)), True, False)
    merged = (members, planes, rows_x, 2 * cells_y)
    return (out_re.reshape(merged), out_im.reshape(merged))


def back_to_bricks(field_re, field_im):
    members, planes, rows_x, length_y = field_re.shape
    flattened = (members * planes * rows_x, length_y)
    grid_re, grid_im = inverse(
        (field_re.reshape(flattened), field_im.reshape(flattened)), True, False, False
    )
    merged = (members, planes, rows_x, length_y // 2)
    piece_re = lax.all_to_all(
        grid_re.reshape(merged), "narrow", split_axis=3, concat_axis=2, tiled=True
    )
    piece_im = lax.all_to_all(
        grid_im.reshape(merged), "narrow", split_axis=3, concat_axis=2, tiled=True
    )
    members, planes, length_x, cells_y = piece_re.shape
    extent = (members * planes, length_x, cells_y)
    out_re, out_im = inverse(
        (piece_re.reshape(extent), piece_im.reshape(extent)), False, True, False
    )
    invert_merged = (members, planes, length_x // 2, cells_y)
    columns = (out_re.reshape(invert_merged), out_im.reshape(invert_merged))
    piece_re, piece_im = lax.all_to_all(columns, "wide", split_axis=2, concat_axis=1, tiled=True)
    members, planes, cells_x, cells_y = piece_re.shape
    extent = (members, planes, cells_x * cells_y)
    result = inverse((piece_re.reshape(extent), piece_im.reshape(extent)), False, True, True)
    merged = (members, planes // 2, cells_x, cells_y)
    return result.reshape(merged)


def couple(kernel, values, picks):
    return -(
        kernel[picks[0]] * values[0] + kernel[picks[1]] * values[1] + kernel[picks[2]] * values[2]
    )


def cross(left, right):
    return jnp.stack(
        [
            left[1] * right[2] - left[2] * right[1],
            left[2] * right[0] - left[0] * right[2],
            left[0] * right[1] - left[1] * right[0],
        ]
    )


def general_shards(spin, region, material, saturation, anisotropy, damping, applied, demag_spectrum):
    magnet = region.astype(jnp.float32)
    direction = spin * magnet[None]
    species = saturation.shape[0]
    chosen = (
        material[None] == lax.broadcasted_iota(jnp.int32, (species,) + material.shape, 0)
    ).astype(jnp.float32)

    def lookup(entries):
        return jnp.sum(chosen * entries[:, None, None, None], axis=0)

    sat_cell = lookup(saturation)
    anis_cell = lookup(anisotropy)
    damp_cell = lookup(damping)
    moment = direction * sat_cell[None]
    components, layers, width_x, width_y = spin.shape
    flattened = moment.reshape(components, layers, width_x * width_y)
    spec_re, spec_im = forward((flattened, None), False, True)
    stacked = (components, 2 * layers, width_x, width_y)
    spectra = along_x(
        (
            lax.all_to_all(
                spec_re.reshape(stacked), "wide", split_axis=1, concat_axis=2, tiled=True
            ),
            lax.all_to_all(
                spec_im.reshape(stacked), "wide", split_axis=1, concat_axis=2, tiled=True
            ),
        )
    )
    spec_re, spec_im = along_y(
        lax.all_to_all(spectra, "narrow", split_axis=2, concat_axis=3, tiled=True)
    )
    parts, planes, rows_x, length_y = demag_spectrum.shape
    inner_size, outer_size = factors(length_y // 2, True)
    kernel = demag_spectrum.reshape(parts, planes, rows_x, inner_size, outer_size)
    kernel = (
        kernel.transpose(0, 1, 2, 4, 3).reshape(parts, planes, rows_x, length_y).astype(jnp.float32)
    )
    couplings = ((0, 3, 4), (3, 1, 5), (4, 5, 2))
    field_re = [couple(kernel, spec_re, picks) for picks in couplings]
    field_im = [couple(kernel, spec_im, picks) for picks in couplings]
    demag = back_to_bricks(jnp.stack(field_re), jnp.stack(field_im))
    framed = extended(direction, (("wide", 2), ("narrow", 3)), 1)
    framed = jnp.pad(framed, ((0, 0), (1, 1), (0, 0), (0, 0)))
    weight = jnp.sum(framed * framed, axis=0)
    neighbours = (
        framed[:, 2:, 1:-1, 1:-1]
        + framed[:, :-2, 1:-1, 1:-1]
        + framed[:, 1:-1, 2:, 1:-1]
        + framed[:, 1:-1, :-2, 1:-1]
        + framed[:, 1:-1, 1:-1, 2:]
        + framed[:, 1:-1, 1:-1, :-2]
    )
    present = (
        weight[2:, 1:-1, 1:-1]
        + weight[:-2, 1:-1, 1:-1]
        + weight[1:-1, 2:, 1:-1]
        + weight[1:-1, :-2, 1:-1]
        + weight[1:-1, 1:-1, 2:]
        + weight[1:-1, 1:-1, :-2]
    )
    laplace = neighbours - present[None] * direction
    zeros = jnp.zeros_like(sat_cell)
    uniaxial = jnp.stack([zeros, zeros, 2.0 * anis_cell / sat_cell * direction[2]])
    field = (
        exchange_coef * laplace / sat_cell[None] + demag + applied[:, None, None, None] + uniaxial
    )
    torque = cross(direction, field)
    rate = (
        -(torque + damp_cell[None] * cross(direction, torque)) / (1.0 + damp_cell * damp_cell)[None]
    )
    return (rate, demag)


def split_table(table):
    high = jnp.asarray(np.asarray(table, np.float32)).astype(jnp.bfloat16)
    high64 = np.asarray(np.asarray(table, np.float32).astype(high.dtype), np.float64)
    low = (table - high64).astype(np.float32).astype(high.dtype)
    return np.asarray(high64.astype(high.dtype)), low


class Plan:
    def __init__(self, wide, narrow, layers, width_x, width_y, planes, rows_x, length_y):
        self.wide, self.narrow = wide, narrow
        self.layers, self.width_x, self.width_y = layers, width_x, width_y
        self.planes, self.rows_x = planes, rows_x
        self.length_z, self.length_x, self.length_y = planes * wide, rows_x * narrow, length_y
        self.cells_x, self.cells_y = width_x * wide, width_y * narrow
        self.devices = wide * narrow
        self.special = self.narrow * (wide // 2) + 1

    def fits(self):
        return (
            self.narrow == 2
            and self.planes == 4
            and self.wide % 16 == 0
            and self.devices * 2 == self.length_z
            and self.length_z == 2 * self.layers
            and self.length_x == 2 * self.cells_x
            and self.length_y == 2 * self.cells_y
            and self.width_x == 2
            and self.width_y % 128 == 0
            and self.rows_x % 16 == 0
            and (self.layers * self.width_x) % 8 == 0
            and 6 * self.rows_x == 3 * self.layers * self.width_x
        )

    def wave(self):
        w, n = np.divmod(np.arange(self.devices), self.narrow)
        return self.planes * w + np.where(w < self.wide // 2, 1 + n, 1 - n)

    def thickness_tables(self):
        wave = self.wave()
        z = np.arange(self.layers)
        angle = 2.0 * np.pi * ((wave[:, None] * z[None]) % self.length_z) / self.length_z
        ahead = np.stack([np.cos(angle), -np.sin(angle)], 1)
        back = np.stack([2.0 * np.cos(angle), -2.0 * np.sin(angle)], 1)
        ahead[self.special, 1] = 1.0
        back[self.special, 0] = np.cos(angle[self.special])
        back[self.special, 1] = 1.0
        back *= -1.0 / (self.length_z * self.length_x * self.length_y)
        n = np.arange(self.devices) % self.narrow
        x = np.arange(self.width_x)
        sign = 1.0 - 2.0 * ((n[:, None] * x[None]) % 2)
        unit_c, unit_x = np.eye(3), np.eye(self.width_x)
        ahead = np.einsum("drz,dx,cb,xv->dcrxbzv", ahead, sign, unit_c, unit_x)
        back = np.einsum("drz,dx,cb,xv->bzvdcrx", back, sign, unit_c, unit_x)
        count = self.devices * 6 * self.width_x
        cells = 3 * self.layers * self.width_x
        return ahead.reshape(count, cells), back.reshape(cells, count)

    def lateral_tables(self):
        half = self.cells_y
        y, k = np.arange(half), np.arange(half)
        angle = 2.0 * np.pi * ((y[:, None] * k[None]) % self.length_y) / self.length_y
        cosine, sine = np.cos(angle), np.sin(angle)
        sine[:, 0] = 1.0 - 2.0 * (y % 2)
        ahead_y = np.concatenate([cosine, sine], 1)
        x = (np.arange(self.wide)[None] * self.width_x + np.arange(self.width_x)[:, None]).reshape(-1)
        kx = np.arange(self.length_x)
        angle = 2.0 * np.pi * ((kx[:, None] * x[None]) % self.length_x) / self.length_x
        cosine, sine = np.cos(angle), np.sin(angle)
        ahead_x = np.concatenate([cosine, sine], 0)
        back_x = np.block([[cosine.T, -sine.T], [sine.T, cosine.T]])
        return ahead_y, ahead_x, back_x


def halves(value):
    high = value.astype(jnp.bfloat16)
    return high, (value - high.astype(jnp.float32)).astype(jnp.bfloat16)


def mul(left, right):
    return jnp.dot(left, right, preferred_element_type=jnp.float32)


def mul_back(left, right):
    return lax.dot_general(left, right, (((1,), (1,)), ((), ())), preferred_element_type=jnp.float32)


def pick(material, entries, species):
    value = jnp.zeros(material.shape, jnp.float32)
    for s in range(species):
        value = jnp.where(material == s, entries[s], value)
    return value


def rows_of(plan):
    w, n = lax.axis_index("wide"), lax.axis_index("narrow")
    low = w < plan.wide // 2
    own = jnp.where(low, 1 + n, 1 - n)
    other = jnp.where(low, 2 - n, n)
    return w, n, own, other


def first_kernel(plan, species, spin_at, region_at, material_at, saturation_at, table_at, tensor,
                 out_at, near_at, next_at, swap_at, lower_at, upper_at, turned_at, side_at, mine_at,
                 spin, region, material, saturation, table, held, held0,
                 out, near, next_, swap, lower, upper, turned, side, mine, sems, done):
    w, n, own, other = rows_of(plan)
    count = plan.rows_x
    moves = [
        pltpu.make_async_copy(source, target, sems.at[k])
        for k, (source, target) in enumerate((
            (saturation_at, saturation), (material_at, material), (region_at, region), (spin_at, spin),
            (table_at, table), (tensor.at[:, other], held), (tensor.at[:, own], mine),
        ))
    ]
    for move in moves:
        move.start()
    fetch0 = pltpu.make_async_copy(tensor.at[:, 0], held0, sems.at[7])

    @pl.when(w == 0)
    def _():
        fetch0.start()

    sent = []

    def send(source, target):
        move = pltpu.make_async_copy(source, target, done.at[len(sent)])
        move.start()
        sent.append(move)

    for move in moves[:4]:
        move.wait()
    cells = plan.layers * plan.width_x
    magnet = region[...].astype(jnp.float32)
    sat = pick(material[...], saturation, species)
    high, low = [], []
    for c in range(3):
        direction = spin[c * cells : (c + 1) * cells, :] * magnet
        turned[c * cells : (c + 1) * cells, :] = direction
        a, b = halves(direction * sat)
        high.append(a)
        low.append(b)
    high, low = jnp.concatenate(high, 0), jnp.concatenate(low, 0)
    send(turned, turned_at)
    moves[5].wait()
    for t in range(6):
        rows = slice(t * count, (t + 1) * count)
        swap[rows, : plan.length_y] = held[t].astype(jnp.float32)
    send(swap, swap_at)
    moves[6].wait()
    send(mine, mine_at)
    moves[4].wait()
    lines = out.shape[0]
    t_high, t_low = table[:lines, :], table[lines:, :]
    out[...] = mul(t_high, high) + (mul(t_low, high) + mul(t_high, low))
    send(out, out_at)
    layers3 = 3 * plan.layers
    up, down = turned[pl.ds(1, layers3, stride=2), :], turned[pl.ds(0, layers3, stride=2), :]
    near[...] = jnp.where(w % 2 == 0, up, down)
    next_[...] = jnp.where(w % 2 == 0, down, up)
    send(near, near_at)
    send(next_, next_at)
    column = lax.broadcasted_iota(jnp.int32, (8, plan.width_y), 1)
    chosen = jnp.where(column == jnp.where(n == 0, plan.width_y - 1, 0), 1.0, 0.0).astype(jnp.bfloat16)
    high = turned[...].astype(jnp.bfloat16)
    rest = turned[...] - high.astype(jnp.float32)
    middle, low = halves(rest)
    side[...] = mul_back(chosen, high) + mul_back(chosen, middle) + mul_back(chosen, low)
    send(side, side_at)

    @pl.when(w == 0)
    def _():
        fetch0.wait()
        cut = SPLIT * count
        lower[(6 - SPLIT) * count :, :] = jnp.zeros((8, plan.length_y), jnp.float32)
        upper[cut:, :] = jnp.zeros((8, plan.length_y), jnp.float32)
        for t in range(6):
            values, edge = held0[t].astype(jnp.float32), held0[t, 0:1, :].astype(jnp.float32)
            if t < SPLIT:
                upper[t * count : (t + 1) * count, :] = values
                lower[(6 - SPLIT) * count + t : (6 - SPLIT) * count + t + 1, :] = edge
            else:
                lower[(t - SPLIT) * count : (t - SPLIT + 1) * count, :] = values
                upper[cut + t : cut + t + 1, :] = edge
        sends = [pltpu.make_async_copy(lower, lower_at, sems.at[8]), pltpu.make_async_copy(upper, upper_at, sems.at[9])]
        for move in sends:
            move.start()
        for move in sends:
            move.wait()

    for move in sent:
        move.wait()


def flip_of(half):
    sum_of = lax.broadcasted_iota(jnp.int32, (half, half), 0) + lax.broadcasted_iota(jnp.int32, (half, half), 1)
    return jnp.where((sum_of == half) | (sum_of == 0), 1.0, 0.0).astype(jnp.bfloat16)


SPLIT = 3


def unfold_zero(plan, lower, upper, second, flip):
    half, count = plan.cells_y, plan.rows_x
    cut = SPLIT * count
    row = lax.broadcasted_iota(jnp.int32, (count, count), 0)
    col = lax.broadcasted_iota(jnp.int32, (count, count), 1)
    turn = jnp.where(row + col == count, 1.0, 0.0).astype(jnp.bfloat16)
    first = lax.broadcasted_iota(jnp.int32, (count, half), 0) == 0
    lane0 = lax.broadcasted_iota(jnp.int32, (count, half), 1) == 0
    tail_lower, tail_upper = (6 - SPLIT) * count, cut
    tail = jnp.concatenate([lower[tail_lower:, :], upper[tail_upper:, :]], 0)
    tail_flip = mul(tail[:, half:].astype(jnp.bfloat16), flip)
    for t in range(6):
        here, at, edge = (upper, t, t) if t < SPLIT else (lower, t - SPLIT, 8 + t)
        straight, mirrored = (slice(0, count), slice(count, 2 * count))[:: 1 if t < SPLIT else -1]
        rows = slice(at * count, (at + 1) * count)
        plus = here[rows, :half]
        minus = mul(here[rows, half:].astype(jnp.bfloat16), flip)
        second[t, straight, :half] = plus
        second[t, straight, half:] = minus
        swap_plus = mul(turn, jnp.where(lane0, plus, minus).astype(jnp.bfloat16))
        swap_minus = mul(turn, jnp.where(lane0, minus, plus).astype(jnp.bfloat16))
        second[t, mirrored, :half] = jnp.where(first, tail[edge : edge + 1, :half], swap_plus)
        second[t, mirrored, half:] = jnp.where(first, tail_flip[edge : edge + 1, :], swap_minus)


COUPLINGS = ((0, 3, 4), (3, 1, 5), (4, 5, 2))


def ready_kernel(table, mine, token):
    token[...] = table[:8, :128].astype(jnp.float32) + mine[0, :8, :128].astype(jnp.float32)


def plane_kernel(plan, got, table, mine, swapped, lower, upper, token, out, mixed, packed, parts, second):
    w, n, _, _ = rows_of(plan)
    lanes, half, wide = plan.width_y, plan.cells_y, plan.wide
    cells_x, length_x = plan.cells_x, plan.length_x
    block = 6 * plan.width_x
    per_c = 2 * cells_x
    narrow = plan.narrow
    lines = []
    for c in range(3):
        for j in range(2 * plan.width_x):
            row = c * 2 * plan.width_x + j
            lines.append(jnp.concatenate(
                [got[pl.ds(m * block + row, wide, stride=narrow * block), :] for m in range(narrow)], 1))
    lines = jnp.concatenate(lines, 0)
    high, low = halves(lines)
    y_high, y_low = table[:half, :], table[half : 2 * half, :]
    base = 2 * half
    x_ahead = table[base : base + 2 * length_x, : 3 * cells_x]
    xb_pair = table[base : base + per_c, half : half + 4 * length_x]
    xb_low = table[base + per_c : base + 2 * per_c, half : half + 2 * length_x]
    waves = mul(high, y_high) + (mul(low, y_high) + mul(high, y_low))
    flip = flip_of(half)
    count = plan.rows_x
    turned_mine = mul(jnp.concatenate([mine[t, :, half:] for t in range(6)], 0), flip)
    turned_far = mul(swapped[:, half : 2 * half].astype(jnp.bfloat16), flip)
    for t in range(6):
        rows = slice(t * count, (t + 1) * count)
        parts[t, :count, :half] = mine[t, :, :half].astype(jnp.float32)
        parts[t, :count, half:] = turned_mine[rows, :]
        parts[t, count:, :half] = swapped[rows, :half]
        parts[t, count:, half:] = turned_far[rows, :]
    for g in range(6):
        a, b = halves(waves[g * cells_x : (g + 1) * cells_x, :])
        mixed[g] = mul(x_ahead, jnp.concatenate([a, b, a], 0))
    step = 16

    def couple(paired):
        for lane in range(0, half, 128):
            for row in range(0, length_x, step):
                left = slice(lane, lane + 128)
                right = slice(half + lane, half + lane + 128)
                cr, sr = slice(row, row + step), slice(length_x + row, length_x + row + step)
                fields = []
                for g in range(6):
                    cp, sp = mixed[g, cr, left], mixed[g, sr, left]
                    cq, sq = mixed[g, cr, right], mixed[g, sr, right]
                    if lane == 0:
                        edge = lax.broadcasted_iota(jnp.int32, cp.shape, 1) == 0
                        cq0, sq0 = jnp.where(edge, 0.0, cq), jnp.where(edge, 0.0, sq)
                        fields.append((cp - sq0, -(sp + cq0),
                                       jnp.where(edge, cq, cp + sq), jnp.where(edge, -sq, cq - sp)))
                    else:
                        fields.append((cp - sq, -(sp + cq), cp + sq, cq - sp))
                if not paired:
                    fields = [
                        (a[0] - b[1], a[1] + b[0], a[2] - b[3], a[3] + b[2])
                        for a, b in zip(fields[0::2], fields[1::2])
                    ]
                for i in range(3):
                    sums = []
                    for s, lanes_at in ((0, left), (2, right)):
                        real = imag = None
                        for j in range(3):
                            t = COUPLINGS[i][j]
                            ka = parts[t, cr, lanes_at]
                            if paired:
                                kb = second[t, cr, lanes_at]
                                a, b = fields[2 * j], fields[2 * j + 1]
                                re = ka * a[s] - kb * b[s + 1]
                                im = ka * a[s + 1] + kb * b[s]
                            else:
                                re, im = ka * fields[j][s], ka * fields[j][s + 1]
                            real = re if real is None else real + re
                            imag = im if imag is None else imag + im
                        sums.append((real, imag))
                    (pr, pi), (mr, mi) = sums
                    even_re, even_im, odd_re, odd_im = pr + mr, pi + mi, mi - pi, pr - mr
                    if lane == 0:
                        even_re, even_im = jnp.where(edge, pr, even_re), jnp.where(edge, pi, even_im)
                        odd_re, odd_im = jnp.where(edge, mr, odd_re), jnp.where(edge, mi, odd_im)
                    for value, base_at, lanes_at in (
                        (even_re, 0, left), (even_im, length_x, left),
                        (odd_re, 0, right), (odd_im, length_x, right),
                    ):
                        a, b = halves(value)
                        high_at, low_at = base_at + row, 2 * length_x + base_at + row
                        packed[i, high_at : high_at + step, lanes_at] = a
                        packed[i, low_at : low_at + step, lanes_at] = b

    special = jnp.logical_and(w == plan.wide // 2, n == 1)

    @pl.when(special)
    def _():
        unfold_zero(plan, lower, upper, second, flip)
        couple(True)

    pl.when(jnp.logical_not(special))(lambda: couple(False))
    back = []
    for i in range(3):
        back.append(mul(xb_pair, packed[i]) + mul(xb_low, packed[i, : 2 * length_x, :]))
    high, low = halves(jnp.concatenate(back, 0))
    result = mul_back(high, y_high) + (mul_back(low, y_high) + mul_back(high, y_low))
    for c in range(3):
        for j in range(2 * plan.width_x):
            row = c * 2 * plan.width_x + j
            for m in range(narrow):
                out[pl.ds(m * block + row, wide, stride=narrow * block), :] = result[
                    row * wide : (row + 1) * wide, m * lanes : (m + 1) * lanes]


def local_kernel(plan, species, turned, side, near, next_, material, saturation, anisotropy,
                 damping, applied, table, out, damp, woven):
    w, n = lax.axis_index("wide"), lax.axis_index("narrow")
    cells, layers = plan.layers * plan.width_x, plan.layers
    row = lax.broadcasted_iota(jnp.int32, (cells, plan.width_y), 0)
    col = lax.broadcasted_iota(jnp.int32, (cells, plan.width_y), 1)
    first, last = col == 0, col == plan.width_y - 1
    even = row % 2 == 0
    ahead = jnp.where(n == 0, 1.0, 0.0)
    sat = pick(material[...], saturation, species)
    anis = pick(material[...], anisotropy, species)
    damp[...] = pick(material[...], damping, species)
    square = lax.broadcasted_iota(jnp.int32, (cells, cells), 0) == lax.broadcasted_iota(
        jnp.int32, (cells, cells), 1)
    sums, present, own = [], jnp.zeros((cells, plan.width_y), jnp.float32), []
    for c in range(3):
        d = turned[c * cells : (c + 1) * cells, :]
        line = jnp.broadcast_to(side[0:1, c * cells : (c + 1) * cells], (cells, cells))
        s = jnp.sum(jnp.where(square, line, 0.0), axis=1, keepdims=True)
        a, b = near[c * layers : (c + 1) * layers, :], next_[c * layers : (c + 1) * layers, :]
        woven[pl.ds(0, layers, stride=2), :] = jnp.where(w % 2 == 0, b, a)
        woven[pl.ds(1, layers, stride=2), :] = jnp.where(w % 2 == 0, a, b)
        beside = (
            jnp.where(row >= 2, pltpu.roll(d, 2, 0), 0.0),
            jnp.where(row < cells - 2, pltpu.roll(d, cells - 2, 0), 0.0),
            woven[...],
            jnp.where(even, pltpu.roll(d, cells - 1, 0), pltpu.roll(d, 1, 0)),
            pltpu.roll(jnp.where(first, s * ahead, d), plan.width_y - 1, 1),
            pltpu.roll(jnp.where(last, s * (1.0 - ahead), d), 1, 1),
        )
        total = beside[0]
        present = present + beside[0] * beside[0]
        for v in beside[1:]:
            total = total + v
            present = present + v * v
        sums.append(total)
        own.append(d)
    for c in range(3):
        field = exchange_coef * (sums[c] - present * own[c]) / sat + applied[c]
        if c == 2:
            field = field + 2.0 * anis / sat * own[2]
        out[c * cells : (c + 1) * cells, :] = field


def last_kernel(plan, got, table, base, turned, damping, rate_at, demag_at, rate, demag, sems):
    cells = plan.layers * plan.width_x
    t_high, t_low = table[: 3 * cells, :], table[3 * cells :, :]
    high, low = halves(got[...])
    demag[...] = mul(t_high, high) + (mul(t_low, high) + mul(t_high, low))
    moves = [pltpu.make_async_copy(demag, demag_at, sems.at[3])]
    moves[0].start()
    damp = damping[...]
    d = [turned[c * cells : (c + 1) * cells, :] for c in range(3)]
    f = [demag[c * cells : (c + 1) * cells, :] + base[c * cells : (c + 1) * cells, :] for c in range(3)]

    def turn(u, v):
        return [u[1] * v[2] - u[2] * v[1], u[2] * v[0] - u[0] * v[2], u[0] * v[1] - u[1] * v[0]]

    torque = turn(d, f)
    again = turn(d, torque)
    scale = -1.0 / (1.0 + damp * damp)
    for c in range(3):
        rows = pl.ds(c * cells, cells)
        rate[rows, :] = (torque[c] + damp * again[c]) * scale
        moves.append(pltpu.make_async_copy(rate.at[rows], rate_at.at[rows], sems.at[c]))
        moves[-1].start()
    for move in moves:
        move.wait()


LIMITS = (67043328, 4 << 20, 12 << 20, 4 << 20, 8 << 20)
VMEM = pl.BlockSpec(memory_space=pltpu.VMEM)
SMEM = pl.BlockSpec(memory_space=pltpu.SMEM)
HBM = pl.BlockSpec(memory_space=pltpu.HBM)


def plane_shards(plan, spin, region, material, saturation, anisotropy, damping, applied, demag_spectrum):
    f32, bf16 = jnp.float32, jnp.bfloat16
    cells, lanes = plan.layers * plan.width_x, plan.width_y
    count, length_y, length_x = plan.devices * 6 * plan.width_x, plan.length_y, plan.length_x
    species = saturation.shape[0]
    shape = jax.ShapeDtypeStruct
    spin2 = spin.reshape(3 * cells, lanes)
    region2, material2 = region.reshape(cells, lanes), material.reshape(cells, lanes)
    ahead_z, back_z = plan.thickness_tables()
    ahead_y, ahead_x, back_x = plan.lateral_tables()
    az, bz, ay = (split_table(t) for t in (ahead_z, back_z, ahead_y))
    ax, bx = split_table(ahead_x), split_table(back_x)
    x_ahead = np.concatenate([ax[0], ax[0], ax[1]], 1)
    xb_pair = np.concatenate([bx[0], bx[0]], 1)

    def call(body, out_shape, in_specs, out_specs, scratch, flops, limit=24 << 20):
        return pl.pallas_call(
            body, out_shape=out_shape, in_specs=in_specs, out_specs=out_specs, scratch_shapes=scratch,
            compiler_params=pltpu.CompilerParams(vmem_limit_bytes=limit),
            cost_estimate=pl.CostEstimate(flops=flops, bytes_accessed=1 << 20, transcendentals=0),
        )

    rows6 = 6 * plan.rows_x
    table_in, table_out = jnp.asarray(np.concatenate(az, 0)), jnp.asarray(np.concatenate(bz, 0))
    outs = ((count, lanes), (3 * plan.layers, lanes), (3 * plan.layers, lanes), (rows6, length_y),
            ((6 - SPLIT) * plan.rows_x + 8, length_y), (SPLIT * plan.rows_x + 8, length_y), (3 * cells, lanes),
            (8, 3 * cells))
    outs = tuple(shape(o, f32) for o in outs) + (shape((6, plan.rows_x, length_y), bf16),)
    out, near, next_, swap, lower, upper, turned, side, mine = call(
        partial(first_kernel, plan, species),
        outs, [HBM] * 6, (HBM,) * len(outs),
        [pltpu.VMEM((3 * cells, lanes), f32), pltpu.VMEM((cells, lanes), jnp.int32),
         pltpu.VMEM((cells, lanes), jnp.int32), pltpu.SMEM((species,), f32),
         pltpu.VMEM(table_in.shape, bf16),
         pltpu.VMEM((6, plan.rows_x, length_y), bf16), pltpu.VMEM((6, plan.rows_x, length_y), bf16)]
        + [pltpu.VMEM(o.shape, o.dtype) for o in outs]
        + [pltpu.SemaphoreType.DMA((10,)), pltpu.SemaphoreType.DMA((7,))],
        1 << 28, LIMITS[0],
    )(spin2, region2, material2, saturation, table_in, demag_spectrum)

    both = ("wide", "narrow")
    swapped = lax.ppermute(swap, "narrow", [(0, 1), (1, 0)])
    blocks = (plan.devices, 3, 2 * plan.width_x, lanes)
    got = lax.all_to_all(out.reshape(blocks), both, 0, 0, tiled=True).reshape(count, lanes)
    lower = lax.ppermute(lower, both, [(0, plan.special)])
    upper = lax.ppermute(upper, both, [(1, plan.special)])
    side = lax.ppermute(side, "narrow", [(0, 1), (1, 0)])
    pairs = [(i ^ 1, i) for i in range(plan.wide)]
    near = lax.ppermute(near, "wide", pairs)
    pairs = [(i, j) for i in range(1, plan.wide - 1, 2) for i, j in ((i, i + 1), (i + 1, i))]
    next_ = lax.ppermute(next_, "wide", pairs)

    half = plan.cells_y
    small = np.zeros((2 * length_x, 2 * half), az[0].dtype)
    small[:, : 3 * plan.cells_x] = x_ahead
    small[: 2 * plan.cells_x, half : half + 4 * length_x] = xb_pair
    small[2 * plan.cells_x : 4 * plan.cells_x, half : half + 2 * length_x] = bx[1]
    table = jnp.asarray(np.concatenate([ay[0], ay[1], small], 0))

    token = call(ready_kernel, shape((8, 128), f32), [VMEM, VMEM], VMEM, [], 1 << 20, LIMITS[1])(table, mine)
    sent = call(
        partial(plane_kernel, plan),
        shape((count, lanes), f32),
        [VMEM] * 7, VMEM,
        [pltpu.VMEM((6, 2 * length_x, length_y), f32), pltpu.VMEM((3, 4 * length_x, length_y), bf16),
         pltpu.VMEM((6, length_x, length_y), f32), pltpu.VMEM((6, length_x, length_y), f32)],
        1 << 29, LIMITS[2],
    )(got, table, mine, swapped, lower, upper, token)

    back = lax.all_to_all(sent.reshape(blocks), both, 0, 0, tiled=True).reshape(count, lanes)
    base, damp = call(
        partial(local_kernel, plan, species), (shape((3 * cells, lanes), f32), shape((cells, lanes), f32)),
        [VMEM] * 5 + [SMEM] * 4 + [VMEM], (VMEM, VMEM), [pltpu.VMEM((cells, lanes), f32)], 1 << 22, LIMITS[3],
    )(turned, side, near, next_, material2, saturation, anisotropy, damping, applied, table_out)

    rate, demag = call(
        partial(last_kernel, plan),
        (shape((3 * cells, lanes), f32), shape((3 * cells, lanes), f32)),
        [VMEM] * 5, (HBM, HBM),
        [pltpu.VMEM((3 * cells, lanes), f32), pltpu.VMEM((3 * cells, lanes), f32), pltpu.SemaphoreType.DMA((4,))],
        1 << 28, LIMITS[4],
    )(back, table_out, base, turned, damp)
    return rate.reshape(spin.shape), demag.reshape(spin.shape)


def shards(*args):
    spin, demag_spectrum = args[0], args[-1]
    _, layers, width_x, width_y = spin.shape
    _, planes, rows_x, length_y = demag_spectrum.shape
    plan = Plan(lax.axis_size("wide"), lax.axis_size("narrow"), layers, width_x, width_y,
                planes, rows_x, length_y)
    if plan.fits():
        return plane_shards(plan, *args)
    return general_shards(*args)


def solution(mesh):
    placed = (
        P(None, None, "wide", "narrow"),
        P(None, "wide", "narrow"),
        P(None, "wide", "narrow"),
        P(),
        P(),
        P(),
        P(),
        P(None, "wide", "narrow", None),
    )
    return jax.shard_map(
        shards,
        mesh=mesh,
        in_specs=placed,
        out_specs=(P(None, None, "wide", "narrow"), P(None, None, "wide", "narrow")),
        check_vma=False,
    )
```

```python
from functools import partial
import math

import jax
import jax.numpy as jnp
import numpy as np
from jax import lax
from jax.experimental import pallas as pl
from jax.experimental.pallas import tpu as pltpu
from jax.sharding import PartitionSpec as P


exchange_coef = 0.3
highest = lax.Precision.HIGHEST


def extended(x, sides, width):
    for axis, dim in sides:
        peers, length = (lax.axis_size(axis), x.shape[dim])
        up = [(i, (i + 1) % peers) for i in range(peers - 1)]
        down = [(j, i) for i, j in up]
        last = lax.slice_in_dim(x, length - width, length, axis=dim)
        leading = lax.slice_in_dim(x, 0, width, axis=dim)
        before = lax.ppermute(last, axis, up)
        after = lax.ppermute(leading, axis, down)
        x = jnp.concatenate([before, x, after], axis=dim)
    return x


def phase_table(rows_count, cols_count, length, sign):
    left_index = lax.broadcasted_iota(jnp.int32, (rows_count, cols_count), 0)
    right_index = lax.broadcasted_iota(jnp.int32, (rows_count, cols_count), 1)
    angle = (left_index * right_index % length).astype(jnp.float32) * (2.0 * math.pi / length)
    return (jnp.cos(angle), sign * jnp.sin(angle))


def contract(pattern, phases, values):
    phase_re, phase_im = phases
    value_re, value_im = values
    product = partial(jnp.einsum, pattern, precision=highest)
    if value_im is None:
        return (product(phase_re, value_re), product(phase_im, value_re))
    return (
        product(phase_re, value_re) - product(phase_im, value_im),
        product(phase_re, value_im) + product(phase_im, value_re),
    )


def factors(half_size, at_end):
    if at_end:
        inner_size = math.gcd(half_size, 128)
    else:
        inner_size = max(
            (
                divisor
                for divisor in range(1, half_size + 1)
                if half_size % divisor == 0 and divisor * divisor <= 2 * half_size
            )
        )
    return (inner_size, 2 * half_size // inner_size)


def forward(values, at_end, natural):
    value_re, value_im = values
    extent = value_re.shape
    half_size = extent[1]
    length = 2 * half_size
    inner_size, outer_size = factors(half_size, at_end)
    tail_index = "" if at_end else "b"
    blocked = (extent[0], outer_size // 2, inner_size) + extent[2:]
    value_re = value_re.reshape(blocked)
    value_im = None if value_im is None else value_im.reshape(blocked)
    phases = phase_table(outer_size, outer_size // 2, outer_size, -1.0)
    work_re, work_im = contract(
        "kn,anp" + tail_index + "->akp" + tail_index, phases, (value_re, value_im)
    )
    twist_re, twist_im = phase_table(outer_size, inner_size, length, -1.0)
    if not at_end:
        twist_re, twist_im = (twist_re[:, :, None], twist_im[:, :, None])
    work_re, work_im = (
        work_re * twist_re - work_im * twist_im,
        work_re * twist_im + work_im * twist_re,
    )
    target = "ajk" if natural else "akj"
    phases = phase_table(inner_size, inner_size, inner_size, -1.0)
    out_re, out_im = contract(
        "jp,akp" + tail_index + "->" + target + tail_index, phases, (work_re, work_im)
    )
    merged = (extent[0], length) + extent[2:]
    return (out_re.reshape(merged), out_im.reshape(merged))


def inverse(values, at_end, natural, real_only):
    value_re, value_im = values
    extent = value_re.shape
    length = extent[1]
    half_size = length // 2
    inner_size, outer_size = factors(half_size, at_end)
    tail_index = "" if at_end else "b"
    if natural:
        blocked = (extent[0], inner_size, outer_size) + extent[2:]
        source = "ajk"
    else:
        blocked = (extent[0], outer_size, inner_size) + extent[2:]
        source = "akj"
    phases = phase_table(inner_size, inner_size, inner_size, 1.0)
    work_re, work_im = contract(
        "pj," + source + tail_index + "->akp" + tail_index,
        phases,
        (value_re.reshape(blocked), value_im.reshape(blocked)),
    )
    twist_re, twist_im = phase_table(outer_size, inner_size, length, 1.0)
    if not at_end:
        twist_re, twist_im = (twist_re[:, :, None], twist_im[:, :, None])
    work_re, work_im = (
        work_re * twist_re - work_im * twist_im,
        work_re * twist_im + work_im * twist_re,
    )
    phases = phase_table(outer_size // 2, outer_size, outer_size, 1.0)
    pattern = "nk,akp" + tail_index + "->anp" + tail_index
    scale = 1.0 / length
    merged = (extent[0], half_size) + extent[2:]
    if real_only:
        product = partial(jnp.einsum, pattern, precision=highest)
        result = product(phases[0], work_re) - product(phases[1], work_im)
        return result.reshape(merged) * scale
    out_re, out_im = contract(pattern, phases, (work_re, work_im))
    return (out_re.reshape(merged) * scale, out_im.reshape(merged) * scale)


def along_x(pieces):
    piece_re, piece_im = pieces
    members, planes, cells_x, cells_y = piece_re.shape
    extent = (members * planes, cells_x, cells_y)
    out_re, out_im = forward((piece_re.reshape(extent), piece_im.reshape(extent)), False, True)
    merged = (members, planes, 2 * cells_x, cells_y)
    return (out_re.reshape(merged), out_im.reshape(merged))


def along_y(pieces):
    piece_re, piece_im = pieces
    members, planes, rows_x, cells_y = piece_re.shape
    extent = (members * planes * rows_x, cells_y)
    out_re, out_im = forward((piece_re.reshape(extent), piece_im.reshape(extent)), True, False)
    merged = (members, planes, rows_x, 2 * cells_y)
    return (out_re.reshape(merged), out_im.reshape(merged))


def back_to_bricks(field_re, field_im):
    members, planes, rows_x, length_y = field_re.shape
    flattened = (members * planes * rows_x, length_y)
    grid_re, grid_im = inverse(
        (field_re.reshape(flattened), field_im.reshape(flattened)), True, False, False
    )
    merged = (members, planes, rows_x, length_y // 2)
    piece_re = lax.all_to_all(
        grid_re.reshape(merged), "narrow", split_axis=3, concat_axis=2, tiled=True
    )
    piece_im = lax.all_to_all(
        grid_im.reshape(merged), "narrow", split_axis=3, concat_axis=2, tiled=True
    )
    members, planes, length_x, cells_y = piece_re.shape
    extent = (members * planes, length_x, cells_y)
    out_re, out_im = inverse(
        (piece_re.reshape(extent), piece_im.reshape(extent)), False, True, False
    )
    invert_merged = (members, planes, length_x // 2, cells_y)
    columns = (out_re.reshape(invert_merged), out_im.reshape(invert_merged))
    piece_re, piece_im = lax.all_to_all(columns, "wide", split_axis=2, concat_axis=1, tiled=True)
    members, planes, cells_x, cells_y = piece_re.shape
    extent = (members, planes, cells_x * cells_y)
    result = inverse((piece_re.reshape(extent), piece_im.reshape(extent)), False, True, True)
    merged = (members, planes // 2, cells_x, cells_y)
    return result.reshape(merged)


def couple(kernel, values, picks):
    return -(
        kernel[picks[0]] * values[0] + kernel[picks[1]] * values[1] + kernel[picks[2]] * values[2]
    )


def cross(left, right):
    return jnp.stack(
        [
            left[1] * right[2] - left[2] * right[1],
            left[2] * right[0] - left[0] * right[2],
            left[0] * right[1] - left[1] * right[0],
        ]
    )


def general_shards(spin, region, material, saturation, anisotropy, damping, applied, demag_spectrum):
    magnet = region.astype(jnp.float32)
    direction = spin * magnet[None]
    species = saturation.shape[0]
    chosen = (
        material[None] == lax.broadcasted_iota(jnp.int32, (species,) + material.shape, 0)
    ).astype(jnp.float32)

    def lookup(entries):
        return jnp.sum(chosen * entries[:, None, None, None], axis=0)

    sat_cell = lookup(saturation)
    anis_cell = lookup(anisotropy)
    damp_cell = lookup(damping)
    moment = direction * sat_cell[None]
    components, layers, width_x, width_y = spin.shape
    flattened = moment.reshape(components, layers, width_x * width_y)
    spec_re, spec_im = forward((flattened, None), False, True)
    stacked = (components, 2 * layers, width_x, width_y)
    spectra = along_x(
        (
            lax.all_to_all(
                spec_re.reshape(stacked), "wide", split_axis=1, concat_axis=2, tiled=True
            ),
            lax.all_to_all(
                spec_im.reshape(stacked), "wide", split_axis=1, concat_axis=2, tiled=True
            ),
        )
    )
    spec_re, spec_im = along_y(
        lax.all_to_all(spectra, "narrow", split_axis=2, concat_axis=3, tiled=True)
    )
    parts, planes, rows_x, length_y = demag_spectrum.shape
    inner_size, outer_size = factors(length_y // 2, True)
    kernel = demag_spectrum.reshape(parts, planes, rows_x, inner_size, outer_size)
    kernel = (
        kernel.transpose(0, 1, 2, 4, 3).reshape(parts, planes, rows_x, length_y).astype(jnp.float32)
    )
    couplings = ((0, 3, 4), (3, 1, 5), (4, 5, 2))
    field_re = [couple(kernel, spec_re, picks) for picks in couplings]
    field_im = [couple(kernel, spec_im, picks) for picks in couplings]
    demag = back_to_bricks(jnp.stack(field_re), jnp.stack(field_im))
    framed = extended(direction, (("wide", 2), ("narrow", 3)), 1)
    framed = jnp.pad(framed, ((0, 0), (1, 1), (0, 0), (0, 0)))
    weight = jnp.sum(framed * framed, axis=0)
    neighbours = (
        framed[:, 2:, 1:-1, 1:-1]
        + framed[:, :-2, 1:-1, 1:-1]
        + framed[:, 1:-1, 2:, 1:-1]
        + framed[:, 1:-1, :-2, 1:-1]
        + framed[:, 1:-1, 1:-1, 2:]
        + framed[:, 1:-1, 1:-1, :-2]
    )
    present = (
        weight[2:, 1:-1, 1:-1]
        + weight[:-2, 1:-1, 1:-1]
        + weight[1:-1, 2:, 1:-1]
        + weight[1:-1, :-2, 1:-1]
        + weight[1:-1, 1:-1, 2:]
        + weight[1:-1, 1:-1, :-2]
    )
    laplace = neighbours - present[None] * direction
    zeros = jnp.zeros_like(sat_cell)
    uniaxial = jnp.stack([zeros, zeros, 2.0 * anis_cell / sat_cell * direction[2]])
    field = (
        exchange_coef * laplace / sat_cell[None] + demag + applied[:, None, None, None] + uniaxial
    )
    torque = cross(direction, field)
    rate = (
        -(torque + damp_cell[None] * cross(direction, torque)) / (1.0 + damp_cell * damp_cell)[None]
    )
    return (rate, demag)


def split_table(table):
    high = jnp.asarray(np.asarray(table, np.float32)).astype(jnp.bfloat16)
    high64 = np.asarray(np.asarray(table, np.float32).astype(high.dtype), np.float64)
    low = (table - high64).astype(np.float32).astype(high.dtype)
    return np.asarray(high64.astype(high.dtype)), low


class Plan:
    def __init__(self, wide, narrow, layers, width_x, width_y, planes, rows_x, length_y):
        self.wide, self.narrow = wide, narrow
        self.layers, self.width_x, self.width_y = layers, width_x, width_y
        self.planes, self.rows_x = planes, rows_x
        self.length_z, self.length_x, self.length_y = planes * wide, rows_x * narrow, length_y
        self.cells_x, self.cells_y = width_x * wide, width_y * narrow
        self.devices = wide * narrow
        self.special = self.narrow * (wide // 2) + 1

    def fits(self):
        return (
            self.narrow == 2
            and self.planes == 4
            and self.wide % 16 == 0
            and self.devices * 2 == self.length_z
            and self.length_z == 2 * self.layers
            and self.length_x == 2 * self.cells_x
            and self.length_y == 2 * self.cells_y
            and self.width_x == 2
            and self.width_y % 128 == 0
            and self.rows_x % 16 == 0
            and (self.layers * self.width_x) % 8 == 0
            and 6 * self.rows_x == 3 * self.layers * self.width_x
        )

    def wave(self):
        w, n = np.divmod(np.arange(self.devices), self.narrow)
        return self.planes * w + np.where(w < self.wide // 2, 1 + n, 1 - n)

    def thickness_tables(self):
        wave = self.wave()
        z = np.arange(self.layers)
        angle = 2.0 * np.pi * ((wave[:, None] * z[None]) % self.length_z) / self.length_z
        ahead = np.stack([np.cos(angle), -np.sin(angle)], 1)
        back = np.stack([2.0 * np.cos(angle), -2.0 * np.sin(angle)], 1)
        ahead[self.special, 1] = 1.0
        back[self.special, 0] = np.cos(angle[self.special])
        back[self.special, 1] = 1.0
        back *= -1.0 / (self.length_z * self.length_x * self.length_y)
        n = np.arange(self.devices) % self.narrow
        x = np.arange(self.width_x)
        sign = 1.0 - 2.0 * ((n[:, None] * x[None]) % 2)
        unit_c, unit_x = np.eye(3), np.eye(self.width_x)
        ahead = np.einsum("drz,dx,xv->rxdzv", ahead, sign, unit_x)
        back = np.einsum("drz,dx,cb,xv->bzvdcrx", back, sign, unit_c, unit_x)
        count = self.devices * 6 * self.width_x
        cells = 3 * self.layers * self.width_x
        return ahead.reshape(count // 3, cells // 3), back.reshape(cells, count)

    def lateral_tables(self):
        half = self.cells_y
        y, k = np.arange(half), np.arange(half)
        angle = 2.0 * np.pi * ((y[:, None] * k[None]) % self.length_y) / self.length_y
        cosine, sine = np.cos(angle), np.sin(angle)
        sine[:, 0] = 1.0 - 2.0 * (y % 2)
        ahead_y = np.concatenate([cosine, sine], 1)
        x = (np.arange(self.wide)[None] * self.width_x + np.arange(self.width_x)[:, None]).reshape(-1)
        kx = np.arange(self.length_x)
        angle = 2.0 * np.pi * ((kx[:, None] * x[None]) % self.length_x) / self.length_x
        cosine, sine = np.cos(angle), np.sin(angle)
        ahead_x = np.concatenate([cosine, sine], 0)
        back_x = np.block([[cosine.T, -sine.T], [sine.T, cosine.T]])
        return ahead_y, ahead_x, back_x


def halves(value):
    high = value.astype(jnp.bfloat16)
    return high, (value - high.astype(jnp.float32)).astype(jnp.bfloat16)


def mul(left, right):
    return jnp.dot(left, right, preferred_element_type=jnp.float32)


def mul_back(left, right):
    return lax.dot_general(left, right, (((1,), (1,)), ((), ())), preferred_element_type=jnp.float32)


def pick(material, entries, species):
    value = jnp.zeros(material.shape, jnp.float32)
    for s in range(species):
        value = jnp.where(material == s, entries[s], value)
    return value


def rows_of(plan):
    w, n = lax.axis_index("wide"), lax.axis_index("narrow")
    low = w < plan.wide // 2
    own = jnp.where(low, 1 + n, 1 - n)
    other = jnp.where(low, 2 - n, n)
    return w, n, own, other


def first_kernel(plan, species, spin_at, region_at, material_at, saturation_at, table_at, tensor,
                 out_at, near_at, next_at, swap_at, lower_at, upper_at, turned_at, side_at,
                 spin, region, material, saturation, table, held, held0,
                 out, near, next_, swap, lower, upper, turned, side, sems, done):
    w, n, _, other = rows_of(plan)
    count = plan.rows_x
    moves = [
        pltpu.make_async_copy(source, target, sems.at[k])
        for k, (source, target) in enumerate((
            (saturation_at, saturation), (material_at, material), (region_at, region), (spin_at, spin),
            (table_at, table), (tensor.at[:, other], held),
        ))
    ]
    for move in moves:
        move.start()
    fetch0 = pltpu.make_async_copy(tensor.at[:, 0], held0, sems.at[7])

    @pl.when(w == 0)
    def _():
        fetch0.start()

    sent = []

    def send(source, target):
        move = pltpu.make_async_copy(source, target, done.at[len(sent)])
        move.start()
        sent.append(move)

    for move in moves[:4]:
        move.wait()
    cells = plan.layers * plan.width_x
    magnet = region[...].astype(jnp.float32)
    sat = pick(material[...], saturation, species)
    high, low = [], []
    for c in range(3):
        direction = spin[c * cells : (c + 1) * cells, :] * magnet
        turned[c * cells : (c + 1) * cells, :] = direction
        a, b = halves(direction * sat)
        high.append(a)
        low.append(b)
    high, low = jnp.concatenate(high, 1), jnp.concatenate(low, 1)
    send(turned, turned_at)
    moves[5].wait()
    for t in range(6):
        rows = slice(t * count, (t + 1) * count)
        swap[rows, : plan.length_y] = held[t].astype(jnp.float32)
    send(swap, swap_at)
    moves[4].wait()
    result = mul(table[...], jnp.concatenate([high, low, high], 0))
    group, lanes = plan.devices, plan.width_y
    for c in range(3):
        for j in range(2 * plan.width_x):
            out[pl.ds(c * 2 * plan.width_x + j, group, stride=6 * plan.width_x), :] = result[
                j * group : (j + 1) * group, c * lanes : (c + 1) * lanes]
    send(out, out_at)
    layers3 = 3 * plan.layers
    up, down = turned[pl.ds(1, layers3, stride=2), :], turned[pl.ds(0, layers3, stride=2), :]
    near[...] = jnp.where(w % 2 == 0, up, down)
    next_[...] = jnp.where(w % 2 == 0, down, up)
    send(near, near_at)
    send(next_, next_at)
    column = lax.broadcasted_iota(jnp.int32, (8, plan.width_y), 1)
    chosen = jnp.where(column == jnp.where(n == 0, plan.width_y - 1, 0), 1.0, 0.0).astype(jnp.bfloat16)
    high = turned[...].astype(jnp.bfloat16)
    rest = turned[...] - high.astype(jnp.float32)
    middle, low = halves(rest)
    side[...] = mul_back(chosen, high) + mul_back(chosen, middle) + mul_back(chosen, low)
    send(side, side_at)

    @pl.when(w == 0)
    def _():
        fetch0.wait()
        cut, half = SPLIT * count, plan.cells_y
        flip = flip_of(half)
        minus = mul(jnp.concatenate([held0[t, :, half:] for t in range(6)], 0), flip)
        lower[(6 - SPLIT) * count :, :] = jnp.zeros((8, plan.length_y), jnp.float32)
        upper[cut:, :] = jnp.zeros((8, plan.length_y), jnp.float32)
        for t in range(6):
            plus = held0[t, :, :half].astype(jnp.float32)
            values = jnp.concatenate([plus, minus[t * count : (t + 1) * count, :]], 1)
            edge = values[0:1, :]
            if t < SPLIT:
                upper[t * count : (t + 1) * count, :] = values
                lower[(6 - SPLIT) * count + t : (6 - SPLIT) * count + t + 1, :] = edge
            else:
                lower[(t - SPLIT) * count : (t - SPLIT + 1) * count, :] = values
                upper[cut + t : cut + t + 1, :] = edge
        sends = [pltpu.make_async_copy(lower, lower_at, sems.at[8]), pltpu.make_async_copy(upper, upper_at, sems.at[9])]
        for move in sends:
            move.start()
        for move in sends:
            move.wait()

    for move in sent:
        move.wait()


def flip_of(half):
    sum_of = lax.broadcasted_iota(jnp.int32, (half, half), 0) + lax.broadcasted_iota(jnp.int32, (half, half), 1)
    return jnp.where((sum_of == half) | (sum_of == 0), 1.0, 0.0).astype(jnp.bfloat16)


SPLIT = 3


def unfold_zero(plan, lower, upper, second):
    half, count = plan.cells_y, plan.rows_x
    row = lax.broadcasted_iota(jnp.int32, (count, count), 0)
    col = lax.broadcasted_iota(jnp.int32, (count, count), 1)
    turn = jnp.where(row + col == count, 1.0, 0.0).astype(jnp.bfloat16)
    first = lax.broadcasted_iota(jnp.int32, (count, 2 * half), 0) == 0
    lane0 = lax.broadcasted_iota(jnp.int32, (count, half), 1) == 0
    for t in range(6):
        here, at, there, edge = (
            (upper, t, lower, (6 - SPLIT) * count + t) if t < SPLIT else (lower, t - SPLIT, upper, SPLIT * count + t)
        )
        straight, mirrored = (slice(0, count), slice(count, 2 * count))[:: 1 if t < SPLIT else -1]
        rows = slice(at * count, (at + 1) * count)
        plus, minus = here[rows, :half], here[rows, half:]
        second[t, straight, :half] = plus
        second[t, straight, half:] = minus
        crossed = jnp.concatenate([jnp.where(lane0, plus, minus), jnp.where(lane0, minus, plus)], 1)
        crossed = mul(turn, crossed.astype(jnp.bfloat16))
        second[t, mirrored, :] = jnp.where(first, there[edge : edge + 1, :], crossed)


COUPLINGS = ((0, 3, 4), (3, 1, 5), (4, 5, 2))


def ready_kernel(plan, tensor, table_at, own_part, table):
    _, _, own, _ = rows_of(plan)
    half, count = plan.cells_y, plan.rows_x
    table[...] = table_at[...]
    turned = mul(jnp.concatenate([tensor[t, own, :, half:] for t in range(6)], 0), flip_of(half))
    for t in range(6):
        own_part[t, :, :half] = tensor[t, own, :, :half].astype(jnp.float32)
        own_part[t, :, half:] = turned[t * count : (t + 1) * count, :]


def ahead_kernel(plan, got, table, swapped, mixed, far_part):
    half, wide = plan.cells_y, plan.wide
    cells_x, length_x, narrow = plan.cells_x, plan.length_x, plan.narrow
    block = 6 * plan.width_x
    lines = []
    for c in range(3):
        for j in range(2 * plan.width_x):
            row = c * 2 * plan.width_x + j
            lines.append(jnp.concatenate(
                [got[pl.ds(m * block + row, wide, stride=narrow * block), :] for m in range(narrow)], 1))
    lines = jnp.concatenate(lines, 0)
    high, low = halves(lines)
    y_high, y_low = table[:half, :], table[half : 2 * half, :]
    x_ahead = table[2 * half : 2 * half + 2 * length_x, : 3 * cells_x]
    waves = mul(high, y_high) + (mul(low, y_high) + mul(high, y_low))
    flip = flip_of(half)
    count = plan.rows_x
    turned_far = mul(swapped[:, half : 2 * half].astype(jnp.bfloat16), flip)
    for t in range(6):
        rows = slice(t * count, (t + 1) * count)
        far_part[t, :, :half] = swapped[rows, :half]
        far_part[t, :, half:] = turned_far[rows, :]
    for g in range(6):
        a, b = halves(waves[g * cells_x : (g + 1) * cells_x, :])
        mixed[g] = mul(x_ahead, jnp.concatenate([a, b, a], 0))


def back_kernel(plan, mixed, own_part, far_part, table, lower, upper, out, packed, second):
    w, n, _, _ = rows_of(plan)
    lanes, half, wide = plan.width_y, plan.cells_y, plan.wide
    length_x, narrow = plan.length_x, plan.narrow
    block, per_c = 6 * plan.width_x, 2 * plan.cells_x
    y_high, y_low = table[:half, :], table[half : 2 * half, :]
    base = 2 * half
    xb_pair = table[base : base + per_c, half : half + 4 * length_x]
    xb_low = table[base + per_c : base + 2 * per_c, half : half + 2 * length_x]
    step = 16

    def couple(paired):
        for lane in range(0, half, 128):
            for row in range(0, length_x, step):
                left = slice(lane, lane + 128)
                right = slice(half + lane, half + lane + 128)
                cr, sr = slice(row, row + step), slice(length_x + row, length_x + row + step)
                part = own_part if row < plan.rows_x else far_part
                at = slice(row % plan.rows_x, row % plan.rows_x + step)
                fields = []
                for g in range(6):
                    cp, sp = mixed[g, cr, left], mixed[g, sr, left]
                    cq, sq = mixed[g, cr, right], mixed[g, sr, right]
                    if lane == 0:
                        edge = lax.broadcasted_iota(jnp.int32, cp.shape, 1) == 0
                        cq0, sq0 = jnp.where(edge, 0.0, cq), jnp.where(edge, 0.0, sq)
                        fields.append((cp - sq0, -(sp + cq0),
                                       jnp.where(edge, cq, cp + sq), jnp.where(edge, -sq, cq - sp)))
                    else:
                        fields.append((cp - sq, -(sp + cq), cp + sq, cq - sp))
                if not paired:
                    fields = [
                        (a[0] - b[1], a[1] + b[0], a[2] - b[3], a[3] + b[2])
                        for a, b in zip(fields[0::2], fields[1::2])
                    ]
                for i in range(3):
                    sums = []
                    for s, lanes_at in ((0, left), (2, right)):
                        real = imag = None
                        for j in range(3):
                            t = COUPLINGS[i][j]
                            ka = part[t, at, lanes_at]
                            if paired:
                                kb = second[t, cr, lanes_at]
                                a, b = fields[2 * j], fields[2 * j + 1]
                                re = ka * a[s] - kb * b[s + 1]
                                im = ka * a[s + 1] + kb * b[s]
                            else:
                                re, im = ka * fields[j][s], ka * fields[j][s + 1]
                            real = re if real is None else real + re
                            imag = im if imag is None else imag + im
                        sums.append((real, imag))
                    (pr, pi), (mr, mi) = sums
                    even_re, even_im, odd_re, odd_im = pr + mr, pi + mi, mi - pi, pr - mr
                    if lane == 0:
                        even_re, even_im = jnp.where(edge, pr, even_re), jnp.where(edge, pi, even_im)
                        odd_re, odd_im = jnp.where(edge, mr, odd_re), jnp.where(edge, mi, odd_im)
                    for value, base_at, lanes_at in (
                        (even_re, 0, left), (even_im, length_x, left),
                        (odd_re, 0, right), (odd_im, length_x, right),
                    ):
                        a, b = halves(value)
                        high_at, low_at = base_at + row, 2 * length_x + base_at + row
                        packed[i, high_at : high_at + step, lanes_at] = a
                        packed[i, low_at : low_at + step, lanes_at] = b

    special = jnp.logical_and(w == plan.wide // 2, n == 1)

    @pl.when(special)
    def _():
        unfold_zero(plan, lower, upper, second)
        couple(True)

    pl.when(jnp.logical_not(special))(lambda: couple(False))
    back = []
    for i in range(3):
        back.append(mul(xb_pair, packed[i]) + mul(xb_low, packed[i, : 2 * length_x, :]))
    high, low = halves(jnp.concatenate(back, 0))
    result = mul_back(high, y_high) + (mul_back(low, y_high) + mul_back(high, y_low))
    for c in range(3):
        for j in range(2 * plan.width_x):
            row = c * 2 * plan.width_x + j
            for m in range(narrow):
                out[pl.ds(m * block + row, wide, stride=narrow * block), :] = result[
                    row * wide : (row + 1) * wide, m * lanes : (m + 1) * lanes]


def local_kernel(plan, species, turned, side, near, next_, material, saturation, anisotropy,
                 damping, applied, table, out, damp, woven):
    w, n = lax.axis_index("wide"), lax.axis_index("narrow")
    cells, layers = plan.layers * plan.width_x, plan.layers
    row = lax.broadcasted_iota(jnp.int32, (cells, plan.width_y), 0)
    col = lax.broadcasted_iota(jnp.int32, (cells, plan.width_y), 1)
    first, last = col == 0, col == plan.width_y - 1
    even = row % 2 == 0
    ahead = jnp.where(n == 0, 1.0, 0.0)
    sat = pick(material[...], saturation, species)
    anis = pick(material[...], anisotropy, species)
    damp[...] = pick(material[...], damping, species)
    square = lax.broadcasted_iota(jnp.int32, (cells, cells), 0) == lax.broadcasted_iota(
        jnp.int32, (cells, cells), 1)
    sums, present, own = [], jnp.zeros((cells, plan.width_y), jnp.float32), []
    for c in range(3):
        d = turned[c * cells : (c + 1) * cells, :]
        line = jnp.broadcast_to(side[0:1, c * cells : (c + 1) * cells], (cells, cells))
        s = jnp.sum(jnp.where(square, line, 0.0), axis=1, keepdims=True)
        a, b = near[c * layers : (c + 1) * layers, :], next_[c * layers : (c + 1) * layers, :]
        woven[pl.ds(0, layers, stride=2), :] = jnp.where(w % 2 == 0, b, a)
        woven[pl.ds(1, layers, stride=2), :] = jnp.where(w % 2 == 0, a, b)
        beside = (
            jnp.where(row >= 2, pltpu.roll(d, 2, 0), 0.0),
            jnp.where(row < cells - 2, pltpu.roll(d, cells - 2, 0), 0.0),
            woven[...],
            jnp.where(even, pltpu.roll(d, cells - 1, 0), pltpu.roll(d, 1, 0)),
            pltpu.roll(jnp.where(first, s * ahead, d), plan.width_y - 1, 1),
            pltpu.roll(jnp.where(last, s * (1.0 - ahead), d), 1, 1),
        )
        total = beside[0]
        present = present + beside[0] * beside[0]
        for v in beside[1:]:
            total = total + v
            present = present + v * v
        sums.append(total)
        own.append(d)
    for c in range(3):
        field = exchange_coef * (sums[c] - present * own[c]) / sat + applied[c]
        if c == 2:
            field = field + 2.0 * anis / sat * own[2]
        out[c * cells : (c + 1) * cells, :] = field


def last_kernel(plan, got, table, base, turned, damping, rate_at, demag_at, rate, demag, sems):
    cells = plan.layers * plan.width_x
    t_high, t_low = table[: 3 * cells, :], table[3 * cells :, :]
    high, low = halves(got[...])
    demag[...] = mul(t_high, high) + (mul(t_low, high) + mul(t_high, low))
    moves = [pltpu.make_async_copy(demag, demag_at, sems.at[3])]
    moves[0].start()
    damp = damping[...]
    d = [turned[c * cells : (c + 1) * cells, :] for c in range(3)]
    f = [demag[c * cells : (c + 1) * cells, :] + base[c * cells : (c + 1) * cells, :] for c in range(3)]

    def turn(u, v):
        return [u[1] * v[2] - u[2] * v[1], u[2] * v[0] - u[0] * v[2], u[0] * v[1] - u[1] * v[0]]

    torque = turn(d, f)
    again = turn(d, torque)
    scale = -1.0 / (1.0 + damp * damp)
    for c in range(3):
        rows = pl.ds(c * cells, cells)
        rate[rows, :] = (torque[c] + damp * again[c]) * scale
        moves.append(pltpu.make_async_copy(rate.at[rows], rate_at.at[rows], sems.at[c]))
        moves[-1].start()
    for move in moves:
        move.wait()


LIMITS = (67043328, 8 << 20, 8 << 20, 4 << 20, 8 << 20)
VMEM = pl.BlockSpec(memory_space=pltpu.VMEM)
SMEM = pl.BlockSpec(memory_space=pltpu.SMEM)
HBM = pl.BlockSpec(memory_space=pltpu.HBM)


def plane_shards(plan, spin, region, material, saturation, anisotropy, damping, applied, demag_spectrum):
    f32, bf16 = jnp.float32, jnp.bfloat16
    cells, lanes = plan.layers * plan.width_x, plan.width_y
    count, length_y, length_x = plan.devices * 6 * plan.width_x, plan.length_y, plan.length_x
    species = saturation.shape[0]
    shape = jax.ShapeDtypeStruct
    spin2 = spin.reshape(3 * cells, lanes)
    region2, material2 = region.reshape(cells, lanes), material.reshape(cells, lanes)
    ahead_z, back_z = plan.thickness_tables()
    ahead_y, ahead_x, back_x = plan.lateral_tables()
    az, bz, ay = (split_table(t) for t in (ahead_z, back_z, ahead_y))
    ax, bx = split_table(ahead_x), split_table(back_x)
    x_ahead = np.concatenate([ax[0], ax[0], ax[1]], 1)
    xb_pair = np.concatenate([bx[0], bx[0]], 1)

    def call(body, out_shape, in_specs, out_specs, scratch, flops, limit=24 << 20):
        return pl.pallas_call(
            body, out_shape=out_shape, in_specs=in_specs, out_specs=out_specs, scratch_shapes=scratch,
            compiler_params=pltpu.CompilerParams(vmem_limit_bytes=limit),
            cost_estimate=pl.CostEstimate(flops=flops, bytes_accessed=1 << 20, transcendentals=0),
        )

    rows6 = 6 * plan.rows_x
    table_in = jnp.asarray(np.concatenate([az[0], az[0], az[1]], 1))
    table_out = jnp.asarray(np.concatenate(bz, 0))
    outs = ((count, lanes), (3 * plan.layers, lanes), (3 * plan.layers, lanes), (rows6, length_y),
            ((6 - SPLIT) * plan.rows_x + 8, length_y), (SPLIT * plan.rows_x + 8, length_y), (3 * cells, lanes),
            (8, 3 * cells))
    outs = tuple(shape(o, f32) for o in outs)
    half = plan.cells_y
    small = np.zeros((2 * length_x, 2 * half), ax[0].dtype)
    small[:, : 3 * plan.cells_x] = x_ahead
    small[: 2 * plan.cells_x, half : half + 4 * length_x] = xb_pair
    small[2 * plan.cells_x : 4 * plan.cells_x, half : half + 2 * length_x] = bx[1]
    table = jnp.asarray(np.concatenate([ay[0], ay[1], small], 0))

    out, near, next_, swap, lower, upper, turned, side = call(
        partial(first_kernel, plan, species),
        outs, [HBM] * 6, (HBM,) * len(outs),
        [pltpu.VMEM((3 * cells, lanes), f32), pltpu.VMEM((cells, lanes), jnp.int32),
         pltpu.VMEM((cells, lanes), jnp.int32), pltpu.SMEM((species,), f32),
         pltpu.VMEM(table_in.shape, bf16),
         pltpu.VMEM((6, plan.rows_x, length_y), bf16), pltpu.VMEM((6, plan.rows_x, length_y), bf16)]
        + [pltpu.VMEM(o.shape, o.dtype) for o in outs]
        + [pltpu.SemaphoreType.DMA((10,)), pltpu.SemaphoreType.DMA((6,))],
        1 << 28, LIMITS[0],
    )(spin2, region2, material2, saturation, table_in, demag_spectrum)

    both = ("wide", "narrow")
    swapped = lax.ppermute(swap, "narrow", [(0, 1), (1, 0)])
    blocks = (plan.devices, 3, 2 * plan.width_x, lanes)
    got = lax.all_to_all(out.reshape(blocks), both, 0, 0, tiled=True).reshape(count, lanes)
    lower = lax.ppermute(lower, both, [(0, plan.special)])
    upper = lax.ppermute(upper, both, [(1, plan.special)])
    side = lax.ppermute(side, "narrow", [(0, 1), (1, 0)])
    pairs = [(i ^ 1, i) for i in range(plan.wide)]
    near = lax.ppermute(near, "wide", pairs)
    pairs = [(i, j) for i in range(1, plan.wide - 1, 2) for i, j in ((i, i + 1), (i + 1, i))]
    next_ = lax.ppermute(next_, "wide", pairs)

    half_shape = shape((6, plan.rows_x, length_y), f32)
    own_part, table = call(
        partial(ready_kernel, plan), (half_shape, shape(table.shape, bf16)), [VMEM] * 2, (VMEM, VMEM), [],
        1 << 26, LIMITS[1],
    )(demag_spectrum, table)
    mixed, far_part = call(
        partial(ahead_kernel, plan), (shape((6, 2 * length_x, length_y), f32), half_shape),
        [VMEM] * 3, (VMEM, VMEM), [], 1 << 29, LIMITS[2],
    )(got, table, swapped)
    sent = call(
        partial(back_kernel, plan),
        shape((count, lanes), f32),
        [VMEM] * 6, VMEM,
        [pltpu.VMEM((3, 4 * length_x, length_y), bf16), pltpu.VMEM((6, length_x, length_y), f32)],
        1 << 29, LIMITS[2],
    )(mixed, own_part, far_part, table, lower, upper)

    back = lax.all_to_all(sent.reshape(blocks), both, 0, 0, tiled=True).reshape(count, lanes)
    base, damp = call(
        partial(local_kernel, plan, species), (shape((3 * cells, lanes), f32), shape((cells, lanes), f32)),
        [VMEM] * 5 + [SMEM] * 4 + [VMEM], (VMEM, VMEM), [pltpu.VMEM((cells, lanes), f32)], 1 << 22, LIMITS[3],
    )(turned, side, near, next_, material2, saturation, anisotropy, damping, applied, table_out)

    rate, demag = call(
        partial(last_kernel, plan),
        (shape((3 * cells, lanes), f32), shape((3 * cells, lanes), f32)),
        [VMEM] * 5, (HBM, HBM),
        [pltpu.VMEM((3 * cells, lanes), f32), pltpu.VMEM((3 * cells, lanes), f32), pltpu.SemaphoreType.DMA((4,))],
        1 << 28, LIMITS[4],
    )(back, table_out, base, turned, damp)
    return rate.reshape(spin.shape), demag.reshape(spin.shape)


def shards(*args):
    spin, demag_spectrum = args[0], args[-1]
    _, layers, width_x, width_y = spin.shape
    _, planes, rows_x, length_y = demag_spectrum.shape
    plan = Plan(lax.axis_size("wide"), lax.axis_size("narrow"), layers, width_x, width_y,
                planes, rows_x, length_y)
    if plan.fits():
        return plane_shards(plan, *args)
    return general_shards(*args)


def solution(mesh):
    placed = (
        P(None, None, "wide", "narrow"),
        P(None, "wide", "narrow"),
        P(None, "wide", "narrow"),
        P(),
        P(),
        P(),
        P(),
        P(None, "wide", "narrow", None),
    )
    return jax.shard_map(
        shards,
        mesh=mesh,
        in_specs=placed,
        out_specs=(P(None, None, "wide", "narrow"), P(None, None, "wide", "narrow")),
        check_vma=False,
    )
```

```python
from functools import partial
import math

import jax
import jax.numpy as jnp
import numpy as np
from jax import lax
from jax.experimental import pallas as pl
from jax.experimental.pallas import tpu as pltpu
from jax.sharding import PartitionSpec as P


exchange_coef = 0.3
highest = lax.Precision.HIGHEST


def extended(x, sides, width):
    for axis, dim in sides:
        peers, length = (lax.axis_size(axis), x.shape[dim])
        up = [(i, (i + 1) % peers) for i in range(peers - 1)]
        down = [(j, i) for i, j in up]
        last = lax.slice_in_dim(x, length - width, length, axis=dim)
        leading = lax.slice_in_dim(x, 0, width, axis=dim)
        before = lax.ppermute(last, axis, up)
        after = lax.ppermute(leading, axis, down)
        x = jnp.concatenate([before, x, after], axis=dim)
    return x


def phase_table(rows_count, cols_count, length, sign):
    left_index = lax.broadcasted_iota(jnp.int32, (rows_count, cols_count), 0)
    right_index = lax.broadcasted_iota(jnp.int32, (rows_count, cols_count), 1)
    angle = (left_index * right_index % length).astype(jnp.float32) * (2.0 * math.pi / length)
    return (jnp.cos(angle), sign * jnp.sin(angle))


def contract(pattern, phases, values):
    phase_re, phase_im = phases
    value_re, value_im = values
    product = partial(jnp.einsum, pattern, precision=highest)
    if value_im is None:
        return (product(phase_re, value_re), product(phase_im, value_re))
    return (
        product(phase_re, value_re) - product(phase_im, value_im),
        product(phase_re, value_im) + product(phase_im, value_re),
    )


def factors(half_size, at_end):
    if at_end:
        inner_size = math.gcd(half_size, 128)
    else:
        inner_size = max(
            (
                divisor
                for divisor in range(1, half_size + 1)
                if half_size % divisor == 0 and divisor * divisor <= 2 * half_size
            )
        )
    return (inner_size, 2 * half_size // inner_size)


def forward(values, at_end, natural):
    value_re, value_im = values
    extent = value_re.shape
    half_size = extent[1]
    length = 2 * half_size
    inner_size, outer_size = factors(half_size, at_end)
    tail_index = "" if at_end else "b"
    blocked = (extent[0], outer_size // 2, inner_size) + extent[2:]
    value_re = value_re.reshape(blocked)
    value_im = None if value_im is None else value_im.reshape(blocked)
    phases = phase_table(outer_size, outer_size // 2, outer_size, -1.0)
    work_re, work_im = contract(
        "kn,anp" + tail_index + "->akp" + tail_index, phases, (value_re, value_im)
    )
    twist_re, twist_im = phase_table(outer_size, inner_size, length, -1.0)
    if not at_end:
        twist_re, twist_im = (twist_re[:, :, None], twist_im[:, :, None])
    work_re, work_im = (
        work_re * twist_re - work_im * twist_im,
        work_re * twist_im + work_im * twist_re,
    )
    target = "ajk" if natural else "akj"
    phases = phase_table(inner_size, inner_size, inner_size, -1.0)
    out_re, out_im = contract(
        "jp,akp" + tail_index + "->" + target + tail_index, phases, (work_re, work_im)
    )
    merged = (extent[0], length) + extent[2:]
    return (out_re.reshape(merged), out_im.reshape(merged))


def inverse(values, at_end, natural, real_only):
    value_re, value_im = values
    extent = value_re.shape
    length = extent[1]
    half_size = length // 2
    inner_size, outer_size = factors(half_size, at_end)
    tail_index = "" if at_end else "b"
    if natural:
        blocked = (extent[0], inner_size, outer_size) + extent[2:]
        source = "ajk"
    else:
        blocked = (extent[0], outer_size, inner_size) + extent[2:]
        source = "akj"
    phases = phase_table(inner_size, inner_size, inner_size, 1.0)
    work_re, work_im = contract(
        "pj," + source + tail_index + "->akp" + tail_index,
        phases,
        (value_re.reshape(blocked), value_im.reshape(blocked)),
    )
    twist_re, twist_im = phase_table(outer_size, inner_size, length, 1.0)
    if not at_end:
        twist_re, twist_im = (twist_re[:, :, None], twist_im[:, :, None])
    work_re, work_im = (
        work_re * twist_re - work_im * twist_im,
        work_re * twist_im + work_im * twist_re,
    )
    phases = phase_table(outer_size // 2, outer_size, outer_size, 1.0)
    pattern = "nk,akp" + tail_index + "->anp" + tail_index
    scale = 1.0 / length
    merged = (extent[0], half_size) + extent[2:]
    if real_only:
        product = partial(jnp.einsum, pattern, precision=highest)
        result = product(phases[0], work_re) - product(phases[1], work_im)
        return result.reshape(merged) * scale
    out_re, out_im = contract(pattern, phases, (work_re, work_im))
    return (out_re.reshape(merged) * scale, out_im.reshape(merged) * scale)


def along_x(pieces):
    piece_re, piece_im = pieces
    members, planes, cells_x, cells_y = piece_re.shape
    extent = (members * planes, cells_x, cells_y)
    out_re, out_im = forward((piece_re.reshape(extent), piece_im.reshape(extent)), False, True)
    merged = (members, planes, 2 * cells_x, cells_y)
    return (out_re.reshape(merged), out_im.reshape(merged))


def along_y(pieces):
    piece_re, piece_im = pieces
    members, planes, rows_x, cells_y = piece_re.shape
    extent = (members * planes * rows_x, cells_y)
    out_re, out_im = forward((piece_re.reshape(extent), piece_im.reshape(extent)), True, False)
    merged = (members, planes, rows_x, 2 * cells_y)
    return (out_re.reshape(merged), out_im.reshape(merged))


def back_to_bricks(field_re, field_im):
    members, planes, rows_x, length_y = field_re.shape
    flattened = (members * planes * rows_x, length_y)
    grid_re, grid_im = inverse(
        (field_re.reshape(flattened), field_im.reshape(flattened)), True, False, False
    )
    merged = (members, planes, rows_x, length_y // 2)
    piece_re = lax.all_to_all(
        grid_re.reshape(merged), "narrow", split_axis=3, concat_axis=2, tiled=True
    )
    piece_im = lax.all_to_all(
        grid_im.reshape(merged), "narrow", split_axis=3, concat_axis=2, tiled=True
    )
    members, planes, length_x, cells_y = piece_re.shape
    extent = (members * planes, length_x, cells_y)
    out_re, out_im = inverse(
        (piece_re.reshape(extent), piece_im.reshape(extent)), False, True, False
    )
    invert_merged = (members, planes, length_x // 2, cells_y)
    columns = (out_re.reshape(invert_merged), out_im.reshape(invert_merged))
    piece_re, piece_im = lax.all_to_all(columns, "wide", split_axis=2, concat_axis=1, tiled=True)
    members, planes, cells_x, cells_y = piece_re.shape
    extent = (members, planes, cells_x * cells_y)
    result = inverse((piece_re.reshape(extent), piece_im.reshape(extent)), False, True, True)
    merged = (members, planes // 2, cells_x, cells_y)
    return result.reshape(merged)


def couple(kernel, values, picks):
    return -(
        kernel[picks[0]] * values[0] + kernel[picks[1]] * values[1] + kernel[picks[2]] * values[2]
    )


def cross(left, right):
    return jnp.stack(
        [
            left[1] * right[2] - left[2] * right[1],
            left[2] * right[0] - left[0] * right[2],
            left[0] * right[1] - left[1] * right[0],
        ]
    )


def general_shards(spin, region, material, saturation, anisotropy, damping, applied, demag_spectrum):
    magnet = region.astype(jnp.float32)
    direction = spin * magnet[None]
    species = saturation.shape[0]
    chosen = (
        material[None] == lax.broadcasted_iota(jnp.int32, (species,) + material.shape, 0)
    ).astype(jnp.float32)

    def lookup(entries):
        return jnp.sum(chosen * entries[:, None, None, None], axis=0)

    sat_cell = lookup(saturation)
    anis_cell = lookup(anisotropy)
    damp_cell = lookup(damping)
    moment = direction * sat_cell[None]
    components, layers, width_x, width_y = spin.shape
    flattened = moment.reshape(components, layers, width_x * width_y)
    spec_re, spec_im = forward((flattened, None), False, True)
    stacked = (components, 2 * layers, width_x, width_y)
    spectra = along_x(
        (
            lax.all_to_all(
                spec_re.reshape(stacked), "wide", split_axis=1, concat_axis=2, tiled=True
            ),
            lax.all_to_all(
                spec_im.reshape(stacked), "wide", split_axis=1, concat_axis=2, tiled=True
            ),
        )
    )
    spec_re, spec_im = along_y(
        lax.all_to_all(spectra, "narrow", split_axis=2, concat_axis=3, tiled=True)
    )
    parts, planes, rows_x, length_y = demag_spectrum.shape
    inner_size, outer_size = factors(length_y // 2, True)
    kernel = demag_spectrum.reshape(parts, planes, rows_x, inner_size, outer_size)
    kernel = (
        kernel.transpose(0, 1, 2, 4, 3).reshape(parts, planes, rows_x, length_y).astype(jnp.float32)
    )
    couplings = ((0, 3, 4), (3, 1, 5), (4, 5, 2))
    field_re = [couple(kernel, spec_re, picks) for picks in couplings]
    field_im = [couple(kernel, spec_im, picks) for picks in couplings]
    demag = back_to_bricks(jnp.stack(field_re), jnp.stack(field_im))
    framed = extended(direction, (("wide", 2), ("narrow", 3)), 1)
    framed = jnp.pad(framed, ((0, 0), (1, 1), (0, 0), (0, 0)))
    weight = jnp.sum(framed * framed, axis=0)
    neighbours = (
        framed[:, 2:, 1:-1, 1:-1]
        + framed[:, :-2, 1:-1, 1:-1]
        + framed[:, 1:-1, 2:, 1:-1]
        + framed[:, 1:-1, :-2, 1:-1]
        + framed[:, 1:-1, 1:-1, 2:]
        + framed[:, 1:-1, 1:-1, :-2]
    )
    present = (
        weight[2:, 1:-1, 1:-1]
        + weight[:-2, 1:-1, 1:-1]
        + weight[1:-1, 2:, 1:-1]
        + weight[1:-1, :-2, 1:-1]
        + weight[1:-1, 1:-1, 2:]
        + weight[1:-1, 1:-1, :-2]
    )
    laplace = neighbours - present[None] * direction
    zeros = jnp.zeros_like(sat_cell)
    uniaxial = jnp.stack([zeros, zeros, 2.0 * anis_cell / sat_cell * direction[2]])
    field = (
        exchange_coef * laplace / sat_cell[None] + demag + applied[:, None, None, None] + uniaxial
    )
    torque = cross(direction, field)
    rate = (
        -(torque + damp_cell[None] * cross(direction, torque)) / (1.0 + damp_cell * damp_cell)[None]
    )
    return (rate, demag)


def split_table(table):
    high = jnp.asarray(np.asarray(table, np.float32)).astype(jnp.bfloat16)
    high64 = np.asarray(np.asarray(table, np.float32).astype(high.dtype), np.float64)
    low = (table - high64).astype(np.float32).astype(high.dtype)
    return np.asarray(high64.astype(high.dtype)), low


class Plan:
    def __init__(self, wide, narrow, layers, width_x, width_y, planes, rows_x, length_y):
        self.wide, self.narrow = wide, narrow
        self.layers, self.width_x, self.width_y = layers, width_x, width_y
        self.planes, self.rows_x = planes, rows_x
        self.length_z, self.length_x, self.length_y = planes * wide, rows_x * narrow, length_y
        self.cells_x, self.cells_y = width_x * wide, width_y * narrow
        self.devices = wide * narrow
        self.special, self.holder = 1, self.narrow * (wide // 2)

    def fits(self):
        return (
            self.narrow == 2
            and self.planes == 4
            and self.wide % 16 == 0
            and self.devices * 2 == self.length_z
            and self.length_z == 2 * self.layers
            and self.length_x == 2 * self.cells_x
            and self.length_y == 2 * self.cells_y
            and self.width_x == 2
            and self.width_y % 128 == 0
            and self.rows_x % 16 == 0
            and (self.layers * self.width_x) % 8 == 0
            and 6 * self.rows_x == 3 * self.layers * self.width_x
        )

    def wave(self):
        w, n = np.divmod(np.arange(self.devices), self.narrow)
        return self.planes * w + np.where(w < self.wide // 2, 1 - n, 1 + n)

    def thickness_tables(self):
        wave = self.wave()
        z = np.arange(self.layers)
        angle = 2.0 * np.pi * ((wave[:, None] * z[None]) % self.length_z) / self.length_z
        ahead = np.stack([np.cos(angle), -np.sin(angle)], 1)
        back = np.stack([2.0 * np.cos(angle), -2.0 * np.sin(angle)], 1)
        middle = 1.0 - 2.0 * (z % 2)
        ahead[self.special, 1] = middle
        back[self.special, 0] = 1.0
        back[self.special, 1] = middle
        back *= -1.0 / (self.length_z * self.length_x * self.length_y)
        n = np.arange(self.devices) % self.narrow
        x = np.arange(self.width_x)
        sign = 1.0 - 2.0 * ((n[:, None] * x[None]) % 2)
        unit_c, unit_x = np.eye(3), np.eye(self.width_x)
        ahead = np.einsum("drz,dx,xv->rxdzv", ahead, sign, unit_x)
        back = np.einsum("drz,dx,cb,xv->bzvdcrx", back, sign, unit_c, unit_x)
        count = self.devices * 6 * self.width_x
        cells = 3 * self.layers * self.width_x
        return ahead.reshape(count // 3, cells // 3), back.reshape(cells, count)

    def lateral_tables(self):
        half = self.cells_y
        y, k = np.arange(half), np.arange(half)
        angle = 2.0 * np.pi * ((y[:, None] * k[None]) % self.length_y) / self.length_y
        cosine, sine = np.cos(angle), np.sin(angle)
        sine[:, 0] = 1.0 - 2.0 * (y % 2)
        ahead_y = np.concatenate([cosine, sine], 1)
        x = (np.arange(self.wide)[None] * self.width_x + np.arange(self.width_x)[:, None]).reshape(-1)
        kx = np.arange(self.length_x)
        angle = 2.0 * np.pi * ((kx[:, None] * x[None]) % self.length_x) / self.length_x
        cosine, sine = np.cos(angle), np.sin(angle)
        ahead_x = np.concatenate([cosine, sine], 0)
        back_x = np.block([[cosine.T, -sine.T], [sine.T, cosine.T]])
        return ahead_y, ahead_x, back_x


def halves(value):
    high = value.astype(jnp.bfloat16)
    return high, (value - high.astype(jnp.float32)).astype(jnp.bfloat16)


def mul(left, right):
    return jnp.dot(left, right, preferred_element_type=jnp.float32)


def mul_back(left, right):
    return lax.dot_general(left, right, (((1,), (1,)), ((), ())), preferred_element_type=jnp.float32)


def pick(material, entries, species):
    value = jnp.zeros(material.shape, jnp.float32)
    for s in range(species):
        value = jnp.where(material == s, entries[s], value)
    return value


def rows_of(plan):
    w, n = lax.axis_index("wide"), lax.axis_index("narrow")
    low = w >= plan.wide // 2
    own = jnp.where(low, 1 + n, 1 - n)
    other = jnp.where(low, 2 - n, n)
    return w, n, own, other


def first_kernel(plan, species, spin_at, region_at, material_at, saturation_at, table_at, tensor,
                 out_at, near_at, next_at, swap_at, lower_at, upper_at, turned_at, side_at,
                 spin, region, material, saturation, table, held, held0,
                 out, near, next_, swap, lower, upper, turned, side, sems, done):
    w, n, _, other = rows_of(plan)
    count = plan.rows_x
    moves = [
        pltpu.make_async_copy(source, target, sems.at[k])
        for k, (source, target) in enumerate((
            (saturation_at, saturation), (material_at, material), (region_at, region), (spin_at, spin),
            (table_at, table), (tensor.at[:, other], held),
        ))
    ]
    for move in moves:
        move.start()
    fetch0 = pltpu.make_async_copy(tensor.at[:, 0], held0, sems.at[7])

    @pl.when(w == plan.wide // 2)
    def _():
        fetch0.start()

    sent = []

    def send(source, target):
        move = pltpu.make_async_copy(source, target, done.at[len(sent)])
        move.start()
        sent.append(move)

    for move in moves[:4]:
        move.wait()
    cells = plan.layers * plan.width_x
    magnet = region[...].astype(jnp.float32)
    sat = pick(material[...], saturation, species)
    high, low = [], []
    for c in range(3):
        direction = spin[c * cells : (c + 1) * cells, :] * magnet
        turned[c * cells : (c + 1) * cells, :] = direction
        a, b = halves(direction * sat)
        high.append(a)
        low.append(b)
    high, low = jnp.concatenate(high, 1), jnp.concatenate(low, 1)
    send(turned, turned_at)
    moves[5].wait()
    for t in range(6):
        rows = slice(t * count, (t + 1) * count)
        swap[rows, : plan.length_y] = held[t].astype(jnp.float32)
    send(swap, swap_at)
    moves[4].wait()
    result = mul(table[...], jnp.concatenate([high, low, high], 0))
    group, lanes = plan.devices, plan.width_y
    for c in range(3):
        for j in range(2 * plan.width_x):
            out[pl.ds(c * 2 * plan.width_x + j, group, stride=6 * plan.width_x), :] = result[
                j * group : (j + 1) * group, c * lanes : (c + 1) * lanes]
    send(out, out_at)
    layers3 = 3 * plan.layers
    up, down = turned[pl.ds(1, layers3, stride=2), :], turned[pl.ds(0, layers3, stride=2), :]
    near[...] = jnp.where(w % 2 == 0, up, down)
    next_[...] = jnp.where(w % 2 == 0, down, up)
    send(near, near_at)
    send(next_, next_at)
    column = lax.broadcasted_iota(jnp.int32, (8, plan.width_y), 1)
    chosen = jnp.where(column == jnp.where(n == 0, plan.width_y - 1, 0), 1.0, 0.0).astype(jnp.bfloat16)
    high = turned[...].astype(jnp.bfloat16)
    rest = turned[...] - high.astype(jnp.float32)
    middle, low = halves(rest)
    side[...] = mul_back(chosen, high) + mul_back(chosen, middle) + mul_back(chosen, low)
    send(side, side_at)

    @pl.when(w == plan.wide // 2)
    def _():
        fetch0.wait()
        cut, half = SPLIT * count, plan.cells_y
        flip = flip_of(half)
        minus = mul(jnp.concatenate([held0[t, :, half:] for t in range(6)], 0), flip)
        lower[(6 - SPLIT) * count :, :] = jnp.zeros((8, plan.length_y), jnp.float32)
        upper[cut:, :] = jnp.zeros((8, plan.length_y), jnp.float32)
        for t in range(6):
            plus = held0[t, :, :half].astype(jnp.float32)
            values = jnp.concatenate([plus, minus[t * count : (t + 1) * count, :]], 1)
            edge = values[0:1, :]
            if t < SPLIT:
                upper[t * count : (t + 1) * count, :] = values
                lower[(6 - SPLIT) * count + t : (6 - SPLIT) * count + t + 1, :] = edge
            else:
                lower[(t - SPLIT) * count : (t - SPLIT + 1) * count, :] = values
                upper[cut + t : cut + t + 1, :] = edge
        sends = [pltpu.make_async_copy(lower, lower_at, sems.at[8]), pltpu.make_async_copy(upper, upper_at, sems.at[9])]
        for move in sends:
            move.start()
        for move in sends:
            move.wait()

    for move in sent:
        move.wait()


def flip_of(half):
    sum_of = lax.broadcasted_iota(jnp.int32, (half, half), 0) + lax.broadcasted_iota(jnp.int32, (half, half), 1)
    return jnp.where((sum_of == half) | (sum_of == 0), 1.0, 0.0).astype(jnp.bfloat16)


SPLIT = 3


def unfold_zero(plan, lower, upper, second):
    half, count = plan.cells_y, plan.rows_x
    row = lax.broadcasted_iota(jnp.int32, (count, count), 0)
    col = lax.broadcasted_iota(jnp.int32, (count, count), 1)
    turn = jnp.where(row + col == count, 1.0, 0.0).astype(jnp.bfloat16)
    first = lax.broadcasted_iota(jnp.int32, (count, 2 * half), 0) == 0
    lane0 = lax.broadcasted_iota(jnp.int32, (count, half), 1) == 0
    for t in range(6):
        here, at, there, edge = (
            (upper, t, lower, (6 - SPLIT) * count + t) if t < SPLIT else (lower, t - SPLIT, upper, SPLIT * count + t)
        )
        straight, mirrored = (slice(0, count), slice(count, 2 * count))[:: 1 if t < SPLIT else -1]
        rows = slice(at * count, (at + 1) * count)
        plus, minus = here[rows, :half], here[rows, half:]
        second[t, straight, :half] = plus
        second[t, straight, half:] = minus
        crossed = jnp.concatenate([jnp.where(lane0, plus, minus), jnp.where(lane0, minus, plus)], 1)
        crossed = mul(turn, crossed.astype(jnp.bfloat16))
        second[t, mirrored, :] = jnp.where(first, there[edge : edge + 1, :], crossed)


COUPLINGS = ((0, 3, 4), (3, 1, 5), (4, 5, 2))


def ready_kernel(plan, tensor, table_at, own_part, table):
    _, _, own, _ = rows_of(plan)
    half, count = plan.cells_y, plan.rows_x
    table[...] = table_at[...]
    turned = mul(jnp.concatenate([tensor[t, own, :, half:] for t in range(6)], 0), flip_of(half))
    for t in range(6):
        own_part[t, :, :half] = tensor[t, own, :, :half].astype(jnp.float32)
        own_part[t, :, half:] = turned[t * count : (t + 1) * count, :]


def ahead_kernel(plan, got, table, swapped, mixed, far_part):
    half, wide = plan.cells_y, plan.wide
    cells_x, length_x, narrow = plan.cells_x, plan.length_x, plan.narrow
    block = 6 * plan.width_x
    lines = []
    for c in range(3):
        for j in range(2 * plan.width_x):
            row = c * 2 * plan.width_x + j
            lines.append(jnp.concatenate(
                [got[pl.ds(m * block + row, wide, stride=narrow * block), :] for m in range(narrow)], 1))
    lines = jnp.concatenate(lines, 0)
    high, low = halves(lines)
    y_high, y_low = table[:half, :], table[half : 2 * half, :]
    x_ahead = table[2 * half : 2 * half + 2 * length_x, : 3 * cells_x]
    waves = mul(high, y_high) + (mul(low, y_high) + mul(high, y_low))
    flip = flip_of(half)
    count = plan.rows_x
    turned_far = mul(swapped[:, half : 2 * half].astype(jnp.bfloat16), flip)
    for t in range(6):
        rows = slice(t * count, (t + 1) * count)
        far_part[t, :, :half] = swapped[rows, :half]
        far_part[t, :, half:] = turned_far[rows, :]
    for g in range(6):
        a, b = halves(waves[g * cells_x : (g + 1) * cells_x, :])
        mixed[g] = mul(x_ahead, jnp.concatenate([a, b, a], 0))


def back_kernel(plan, mixed, own_part, far_part, table, lower, upper, out, packed, second):
    w, n, _, _ = rows_of(plan)
    lanes, half, wide = plan.width_y, plan.cells_y, plan.wide
    length_x, narrow = plan.length_x, plan.narrow
    block, per_c = 6 * plan.width_x, 2 * plan.cells_x
    y_high, y_low = table[:half, :], table[half : 2 * half, :]
    base = 2 * half
    xb_pair = table[base : base + per_c, half : half + 4 * length_x]
    xb_low = table[base + per_c : base + 2 * per_c, half : half + 2 * length_x]
    step = 16

    def couple(paired):
        for lane in range(0, half, 128):
            for row in range(0, length_x, step):
                left = slice(lane, lane + 128)
                right = slice(half + lane, half + lane + 128)
                cr, sr = slice(row, row + step), slice(length_x + row, length_x + row + step)
                part = own_part if row < plan.rows_x else far_part
                at = slice(row % plan.rows_x, row % plan.rows_x + step)
                fields = []
                for g in range(6):
                    cp, sp = mixed[g, cr, left], mixed[g, sr, left]
                    cq, sq = mixed[g, cr, right], mixed[g, sr, right]
                    if lane == 0:
                        edge = lax.broadcasted_iota(jnp.int32, cp.shape, 1) == 0
                        cq0, sq0 = jnp.where(edge, 0.0, cq), jnp.where(edge, 0.0, sq)
                        fields.append((cp - sq0, -(sp + cq0),
                                       jnp.where(edge, cq, cp + sq), jnp.where(edge, -sq, cq - sp)))
                    else:
                        fields.append((cp - sq, -(sp + cq), cp + sq, cq - sp))
                if not paired:
                    fields = [
                        (a[0] - b[1], a[1] + b[0], a[2] - b[3], a[3] + b[2])
                        for a, b in zip(fields[0::2], fields[1::2])
                    ]
                for i in range(3):
                    sums = []
                    for s, lanes_at in ((0, left), (2, right)):
                        real = imag = None
                        for j in range(3):
                            t = COUPLINGS[i][j]
                            ka = part[t, at, lanes_at]
                            if paired:
                                kb = second[t, cr, lanes_at]
                                a, b = fields[2 * j], fields[2 * j + 1]
                                re = ka * a[s] - kb * b[s + 1]
                                im = ka * a[s + 1] + kb * b[s]
                            else:
                                re, im = ka * fields[j][s], ka * fields[j][s + 1]
                            real = re if real is None else real + re
                            imag = im if imag is None else imag + im
                        sums.append((real, imag))
                    (pr, pi), (mr, mi) = sums
                    even_re, even_im, odd_re, odd_im = pr + mr, pi + mi, mi - pi, pr - mr
                    if lane == 0:
                        even_re, even_im = jnp.where(edge, pr, even_re), jnp.where(edge, pi, even_im)
                        odd_re, odd_im = jnp.where(edge, mr, odd_re), jnp.where(edge, mi, odd_im)
                    for value, base_at, lanes_at in (
                        (even_re, 0, left), (even_im, length_x, left),
                        (odd_re, 0, right), (odd_im, length_x, right),
                    ):
                        a, b = halves(value)
                        high_at, low_at = base_at + row, 2 * length_x + base_at + row
                        packed[i, high_at : high_at + step, lanes_at] = a
                        packed[i, low_at : low_at + step, lanes_at] = b

    special = jnp.logical_and(w == 0, n == 1)

    @pl.when(special)
    def _():
        unfold_zero(plan, lower, upper, second)
        couple(True)

    pl.when(jnp.logical_not(special))(lambda: couple(False))
    back = []
    for i in range(3):
        back.append(mul(xb_pair, packed[i]) + mul(xb_low, packed[i, : 2 * length_x, :]))
    high, low = halves(jnp.concatenate(back, 0))
    result = mul_back(high, y_high) + (mul_back(low, y_high) + mul_back(high, y_low))
    for c in range(3):
        for j in range(2 * plan.width_x):
            row = c * 2 * plan.width_x + j
            for m in range(narrow):
                out[pl.ds(m * block + row, wide, stride=narrow * block), :] = result[
                    row * wide : (row + 1) * wide, m * lanes : (m + 1) * lanes]


def local_kernel(plan, species, turned, side, near, next_, material, saturation, anisotropy,
                 damping, applied, table, out, damp, woven):
    w, n = lax.axis_index("wide"), lax.axis_index("narrow")
    cells, layers = plan.layers * plan.width_x, plan.layers
    row = lax.broadcasted_iota(jnp.int32, (cells, plan.width_y), 0)
    col = lax.broadcasted_iota(jnp.int32, (cells, plan.width_y), 1)
    first, last = col == 0, col == plan.width_y - 1
    even = row % 2 == 0
    ahead = jnp.where(n == 0, 1.0, 0.0)
    sat = pick(material[...], saturation, species)
    anis = pick(material[...], anisotropy, species)
    damp[...] = pick(material[...], damping, species)
    square = lax.broadcasted_iota(jnp.int32, (cells, cells), 0) == lax.broadcasted_iota(
        jnp.int32, (cells, cells), 1)
    sums, present, own = [], jnp.zeros((cells, plan.width_y), jnp.float32), []
    for c in range(3):
        d = turned[c * cells : (c + 1) * cells, :]
        line = jnp.broadcast_to(side[0:1, c * cells : (c + 1) * cells], (cells, cells))
        s = jnp.sum(jnp.where(square, line, 0.0), axis=1, keepdims=True)
        a, b = near[c * layers : (c + 1) * layers, :], next_[c * layers : (c + 1) * layers, :]
        woven[pl.ds(0, layers, stride=2), :] = jnp.where(w % 2 == 0, b, a)
        woven[pl.ds(1, layers, stride=2), :] = jnp.where(w % 2 == 0, a, b)
        beside = (
            jnp.where(row >= 2, pltpu.roll(d, 2, 0), 0.0),
            jnp.where(row < cells - 2, pltpu.roll(d, cells - 2, 0), 0.0),
            woven[...],
            jnp.where(even, pltpu.roll(d, cells - 1, 0), pltpu.roll(d, 1, 0)),
            pltpu.roll(jnp.where(first, s * ahead, d), plan.width_y - 1, 1),
            pltpu.roll(jnp.where(last, s * (1.0 - ahead), d), 1, 1),
        )
        total = beside[0]
        present = present + beside[0] * beside[0]
        for v in beside[1:]:
            total = total + v
            present = present + v * v
        sums.append(total)
        own.append(d)
    for c in range(3):
        field = exchange_coef * (sums[c] - present * own[c]) / sat + applied[c]
        if c == 2:
            field = field + 2.0 * anis / sat * own[2]
        out[c * cells : (c + 1) * cells, :] = field


def last_kernel(plan, got, table, base, turned, damping, rate_at, demag_at, rate, demag, sems):
    cells = plan.layers * plan.width_x
    t_high, t_low = table[: 3 * cells, :], table[3 * cells :, :]
    high, low = halves(got[...])
    demag[...] = mul(t_high, high) + (mul(t_low, high) + mul(t_high, low))
    moves = [pltpu.make_async_copy(demag, demag_at, sems.at[3])]
    moves[0].start()
    damp = damping[...]
    d = [turned[c * cells : (c + 1) * cells, :] for c in range(3)]
    f = [demag[c * cells : (c + 1) * cells, :] + base[c * cells : (c + 1) * cells, :] for c in range(3)]

    def turn(u, v):
        return [u[1] * v[2] - u[2] * v[1], u[2] * v[0] - u[0] * v[2], u[0] * v[1] - u[1] * v[0]]

    torque = turn(d, f)
    again = turn(d, torque)
    scale = -1.0 / (1.0 + damp * damp)
    for c in range(3):
        rows = pl.ds(c * cells, cells)
        rate[rows, :] = (torque[c] + damp * again[c]) * scale
        moves.append(pltpu.make_async_copy(rate.at[rows], rate_at.at[rows], sems.at[c]))
        moves[-1].start()
    for move in moves:
        move.wait()


LIMITS = (67043328, 8 << 20, 8 << 20, 4 << 20, 8 << 20)
VMEM = pl.BlockSpec(memory_space=pltpu.VMEM)
SMEM = pl.BlockSpec(memory_space=pltpu.SMEM)
HBM = pl.BlockSpec(memory_space=pltpu.HBM)


def plane_shards(plan, spin, region, material, saturation, anisotropy, damping, applied, demag_spectrum):
    f32, bf16 = jnp.float32, jnp.bfloat16
    cells, lanes = plan.layers * plan.width_x, plan.width_y
    count, length_y, length_x = plan.devices * 6 * plan.width_x, plan.length_y, plan.length_x
    species = saturation.shape[0]
    shape = jax.ShapeDtypeStruct
    spin2 = spin.reshape(3 * cells, lanes)
    region2, material2 = region.reshape(cells, lanes), material.reshape(cells, lanes)
    ahead_z, back_z = plan.thickness_tables()
    ahead_y, ahead_x, back_x = plan.lateral_tables()
    az, bz, ay = (split_table(t) for t in (ahead_z, back_z, ahead_y))
    ax, bx = split_table(ahead_x), split_table(back_x)
    x_ahead = np.concatenate([ax[0], ax[0], ax[1]], 1)
    xb_pair = np.concatenate([bx[0], bx[0]], 1)

    def call(body, out_shape, in_specs, out_specs, scratch, flops, limit=24 << 20):
        return pl.pallas_call(
            body, out_shape=out_shape, in_specs=in_specs, out_specs=out_specs, scratch_shapes=scratch,
            compiler_params=pltpu.CompilerParams(vmem_limit_bytes=limit),
            cost_estimate=pl.CostEstimate(flops=flops, bytes_accessed=1 << 20, transcendentals=0),
        )

    rows6 = 6 * plan.rows_x
    table_in = jnp.asarray(np.concatenate([az[0], az[0], az[1]], 1))
    table_out = jnp.asarray(np.concatenate(bz, 0))
    outs = ((count, lanes), (3 * plan.layers, lanes), (3 * plan.layers, lanes), (rows6, length_y),
            ((6 - SPLIT) * plan.rows_x + 8, length_y), (SPLIT * plan.rows_x + 8, length_y), (3 * cells, lanes),
            (8, 3 * cells))
    outs = tuple(shape(o, f32) for o in outs)
    half = plan.cells_y
    small = np.zeros((2 * length_x, 2 * half), ax[0].dtype)
    small[:, : 3 * plan.cells_x] = x_ahead
    small[: 2 * plan.cells_x, half : half + 4 * length_x] = xb_pair
    small[2 * plan.cells_x : 4 * plan.cells_x, half : half + 2 * length_x] = bx[1]
    table = jnp.asarray(np.concatenate([ay[0], ay[1], small], 0))

    out, near, next_, swap, lower, upper, turned, side = call(
        partial(first_kernel, plan, species),
        outs, [HBM] * 6, (HBM,) * len(outs),
        [pltpu.VMEM((3 * cells, lanes), f32), pltpu.VMEM((cells, lanes), jnp.int32),
         pltpu.VMEM((cells, lanes), jnp.int32), pltpu.SMEM((species,), f32),
         pltpu.VMEM(table_in.shape, bf16),
         pltpu.VMEM((6, plan.rows_x, length_y), bf16), pltpu.VMEM((6, plan.rows_x, length_y), bf16)]
        + [pltpu.VMEM(o.shape, o.dtype) for o in outs]
        + [pltpu.SemaphoreType.DMA((10,)), pltpu.SemaphoreType.DMA((6,))],
        1 << 28, LIMITS[0],
    )(spin2, region2, material2, saturation, table_in, demag_spectrum)

    both = ("wide", "narrow")
    swapped = lax.ppermute(swap, "narrow", [(0, 1), (1, 0)])
    blocks = (plan.devices, 3, 2 * plan.width_x, lanes)
    got = lax.all_to_all(out.reshape(blocks), both, 0, 0, tiled=True).reshape(count, lanes)
    lower = lax.ppermute(lower, both, [(plan.holder, plan.special)])
    upper = lax.ppermute(upper, both, [(plan.holder + 1, plan.special)])
    side = lax.ppermute(side, "narrow", [(0, 1), (1, 0)])
    pairs = [(i ^ 1, i) for i in range(plan.wide)]
    near = lax.ppermute(near, "wide", pairs)
    pairs = [(i, j) for i in range(1, plan.wide - 1, 2) for i, j in ((i, i + 1), (i + 1, i))]
    next_ = lax.ppermute(next_, "wide", pairs)

    half_shape = shape((6, plan.rows_x, length_y), f32)
    own_part, table = call(
        partial(ready_kernel, plan), (half_shape, shape(table.shape, bf16)), [VMEM] * 2, (VMEM, VMEM), [],
        1 << 26, LIMITS[1],
    )(demag_spectrum, table)
    mixed, far_part = call(
        partial(ahead_kernel, plan), (shape((6, 2 * length_x, length_y), f32), half_shape),
        [VMEM] * 3, (VMEM, VMEM), [], 1 << 29, LIMITS[2],
    )(got, table, swapped)
    sent = call(
        partial(back_kernel, plan),
        shape((count, lanes), f32),
        [VMEM] * 6, VMEM,
        [pltpu.VMEM((3, 4 * length_x, length_y), bf16), pltpu.VMEM((6, length_x, length_y), f32)],
        1 << 29, LIMITS[2],
    )(mixed, own_part, far_part, table, lower, upper)

    back = lax.all_to_all(sent.reshape(blocks), both, 0, 0, tiled=True).reshape(count, lanes)
    base, damp = call(
        partial(local_kernel, plan, species), (shape((3 * cells, lanes), f32), shape((cells, lanes), f32)),
        [VMEM] * 5 + [SMEM] * 4 + [VMEM], (VMEM, VMEM), [pltpu.VMEM((cells, lanes), f32)], 1 << 22, LIMITS[3],
    )(turned, side, near, next_, material2, saturation, anisotropy, damping, applied, table_out)

    rate, demag = call(
        partial(last_kernel, plan),
        (shape((3 * cells, lanes), f32), shape((3 * cells, lanes), f32)),
        [VMEM] * 5, (HBM, HBM),
        [pltpu.VMEM((3 * cells, lanes), f32), pltpu.VMEM((3 * cells, lanes), f32), pltpu.SemaphoreType.DMA((4,))],
        1 << 28, LIMITS[4],
    )(back, table_out, base, turned, damp)
    return rate.reshape(spin.shape), demag.reshape(spin.shape)


def shards(*args):
    spin, demag_spectrum = args[0], args[-1]
    _, layers, width_x, width_y = spin.shape
    _, planes, rows_x, length_y = demag_spectrum.shape
    plan = Plan(lax.axis_size("wide"), lax.axis_size("narrow"), layers, width_x, width_y,
                planes, rows_x, length_y)
    if plan.fits():
        return plane_shards(plan, *args)
    return general_shards(*args)


def solution(mesh):
    placed = (
        P(None, None, "wide", "narrow"),
        P(None, "wide", "narrow"),
        P(None, "wide", "narrow"),
        P(),
        P(),
        P(),
        P(),
        P(None, "wide", "narrow", None),
    )
    return jax.shard_map(
        shards,
        mesh=mesh,
        in_specs=placed,
        out_specs=(P(None, None, "wide", "narrow"), P(None, None, "wide", "narrow")),
        check_vma=False,
    )
```

```python
from functools import partial
import math

import jax
import jax.numpy as jnp
import numpy as np
from jax import lax
from jax.experimental import pallas as pl
from jax.experimental.pallas import tpu as pltpu
from jax.sharding import PartitionSpec as P


exchange_coef = 0.3
highest = lax.Precision.HIGHEST


def extended(x, sides, width):
    for axis, dim in sides:
        peers, length = (lax.axis_size(axis), x.shape[dim])
        up = [(i, (i + 1) % peers) for i in range(peers - 1)]
        down = [(j, i) for i, j in up]
        last = lax.slice_in_dim(x, length - width, length, axis=dim)
        leading = lax.slice_in_dim(x, 0, width, axis=dim)
        before = lax.ppermute(last, axis, up)
        after = lax.ppermute(leading, axis, down)
        x = jnp.concatenate([before, x, after], axis=dim)
    return x


def phase_table(rows_count, cols_count, length, sign):
    left_index = lax.broadcasted_iota(jnp.int32, (rows_count, cols_count), 0)
    right_index = lax.broadcasted_iota(jnp.int32, (rows_count, cols_count), 1)
    angle = (left_index * right_index % length).astype(jnp.float32) * (2.0 * math.pi / length)
    return (jnp.cos(angle), sign * jnp.sin(angle))


def contract(pattern, phases, values):
    phase_re, phase_im = phases
    value_re, value_im = values
    product = partial(jnp.einsum, pattern, precision=highest)
    if value_im is None:
        return (product(phase_re, value_re), product(phase_im, value_re))
    return (
        product(phase_re, value_re) - product(phase_im, value_im),
        product(phase_re, value_im) + product(phase_im, value_re),
    )


def factors(half_size, at_end):
    if at_end:
        inner_size = math.gcd(half_size, 128)
    else:
        inner_size = max(
            (
                divisor
                for divisor in range(1, half_size + 1)
                if half_size % divisor == 0 and divisor * divisor <= 2 * half_size
            )
        )
    return (inner_size, 2 * half_size // inner_size)


def forward(values, at_end, natural):
    value_re, value_im = values
    extent = value_re.shape
    half_size = extent[1]
    length = 2 * half_size
    inner_size, outer_size = factors(half_size, at_end)
    tail_index = "" if at_end else "b"
    blocked = (extent[0], outer_size // 2, inner_size) + extent[2:]
    value_re = value_re.reshape(blocked)
    value_im = None if value_im is None else value_im.reshape(blocked)
    phases = phase_table(outer_size, outer_size // 2, outer_size, -1.0)
    work_re, work_im = contract(
        "kn,anp" + tail_index + "->akp" + tail_index, phases, (value_re, value_im)
    )
    twist_re, twist_im = phase_table(outer_size, inner_size, length, -1.0)
    if not at_end:
        twist_re, twist_im = (twist_re[:, :, None], twist_im[:, :, None])
    work_re, work_im = (
        work_re * twist_re - work_im * twist_im,
        work_re * twist_im + work_im * twist_re,
    )
    target = "ajk" if natural else "akj"
    phases = phase_table(inner_size, inner_size, inner_size, -1.0)
    out_re, out_im = contract(
        "jp,akp" + tail_index + "->" + target + tail_index, phases, (work_re, work_im)
    )
    merged = (extent[0], length) + extent[2:]
    return (out_re.reshape(merged), out_im.reshape(merged))


def inverse(values, at_end, natural, real_only):
    value_re, value_im = values
    extent = value_re.shape
    length = extent[1]
    half_size = length // 2
    inner_size, outer_size = factors(half_size, at_end)
    tail_index = "" if at_end else "b"
    if natural:
        blocked = (extent[0], inner_size, outer_size) + extent[2:]
        source = "ajk"
    else:
        blocked = (extent[0], outer_size, inner_size) + extent[2:]
        source = "akj"
    phases = phase_table(inner_size, inner_size, inner_size, 1.0)
    work_re, work_im = contract(
        "pj," + source + tail_index + "->akp" + tail_index,
        phases,
        (value_re.reshape(blocked), value_im.reshape(blocked)),
    )
    twist_re, twist_im = phase_table(outer_size, inner_size, length, 1.0)
    if not at_end:
        twist_re, twist_im = (twist_re[:, :, None], twist_im[:, :, None])
    work_re, work_im = (
        work_re * twist_re - work_im * twist_im,
        work_re * twist_im + work_im * twist_re,
    )
    phases = phase_table(outer_size // 2, outer_size, outer_size, 1.0)
    pattern = "nk,akp" + tail_index + "->anp" + tail_index
    scale = 1.0 / length
    merged = (extent[0], half_size) + extent[2:]
    if real_only:
        product = partial(jnp.einsum, pattern, precision=highest)
        result = product(phases[0], work_re) - product(phases[1], work_im)
        return result.reshape(merged) * scale
    out_re, out_im = contract(pattern, phases, (work_re, work_im))
    return (out_re.reshape(merged) * scale, out_im.reshape(merged) * scale)


def along_x(pieces):
    piece_re, piece_im = pieces
    members, planes, cells_x, cells_y = piece_re.shape
    extent = (members * planes, cells_x, cells_y)
    out_re, out_im = forward((piece_re.reshape(extent), piece_im.reshape(extent)), False, True)
    merged = (members, planes, 2 * cells_x, cells_y)
    return (out_re.reshape(merged), out_im.reshape(merged))


def along_y(pieces):
    piece_re, piece_im = pieces
    members, planes, rows_x, cells_y = piece_re.shape
    extent = (members * planes * rows_x, cells_y)
    out_re, out_im = forward((piece_re.reshape(extent), piece_im.reshape(extent)), True, False)
    merged = (members, planes, rows_x, 2 * cells_y)
    return (out_re.reshape(merged), out_im.reshape(merged))


def back_to_bricks(field_re, field_im):
    members, planes, rows_x, length_y = field_re.shape
    flattened = (members * planes * rows_x, length_y)
    grid_re, grid_im = inverse(
        (field_re.reshape(flattened), field_im.reshape(flattened)), True, False, False
    )
    merged = (members, planes, rows_x, length_y // 2)
    piece_re = lax.all_to_all(
        grid_re.reshape(merged), "narrow", split_axis=3, concat_axis=2, tiled=True
    )
    piece_im = lax.all_to_all(
        grid_im.reshape(merged), "narrow", split_axis=3, concat_axis=2, tiled=True
    )
    members, planes, length_x, cells_y = piece_re.shape
    extent = (members * planes, length_x, cells_y)
    out_re, out_im = inverse(
        (piece_re.reshape(extent), piece_im.reshape(extent)), False, True, False
    )
    invert_merged = (members, planes, length_x // 2, cells_y)
    columns = (out_re.reshape(invert_merged), out_im.reshape(invert_merged))
    piece_re, piece_im = lax.all_to_all(columns, "wide", split_axis=2, concat_axis=1, tiled=True)
    members, planes, cells_x, cells_y = piece_re.shape
    extent = (members, planes, cells_x * cells_y)
    result = inverse((piece_re.reshape(extent), piece_im.reshape(extent)), False, True, True)
    merged = (members, planes // 2, cells_x, cells_y)
    return result.reshape(merged)


def couple(kernel, values, picks):
    return -(
        kernel[picks[0]] * values[0] + kernel[picks[1]] * values[1] + kernel[picks[2]] * values[2]
    )


def cross(left, right):
    return jnp.stack(
        [
            left[1] * right[2] - left[2] * right[1],
            left[2] * right[0] - left[0] * right[2],
            left[0] * right[1] - left[1] * right[0],
        ]
    )


def general_shards(spin, region, material, saturation, anisotropy, damping, applied, demag_spectrum):
    magnet = region.astype(jnp.float32)
    direction = spin * magnet[None]
    species = saturation.shape[0]
    chosen = (
        material[None] == lax.broadcasted_iota(jnp.int32, (species,) + material.shape, 0)
    ).astype(jnp.float32)

    def lookup(entries):
        return jnp.sum(chosen * entries[:, None, None, None], axis=0)

    sat_cell = lookup(saturation)
    anis_cell = lookup(anisotropy)
    damp_cell = lookup(damping)
    moment = direction * sat_cell[None]
    components, layers, width_x, width_y = spin.shape
    flattened = moment.reshape(components, layers, width_x * width_y)
    spec_re, spec_im = forward((flattened, None), False, True)
    stacked = (components, 2 * layers, width_x, width_y)
    spectra = along_x(
        (
            lax.all_to_all(
                spec_re.reshape(stacked), "wide", split_axis=1, concat_axis=2, tiled=True
            ),
            lax.all_to_all(
                spec_im.reshape(stacked), "wide", split_axis=1, concat_axis=2, tiled=True
            ),
        )
    )
    spec_re, spec_im = along_y(
        lax.all_to_all(spectra, "narrow", split_axis=2, concat_axis=3, tiled=True)
    )
    parts, planes, rows_x, length_y = demag_spectrum.shape
    inner_size, outer_size = factors(length_y // 2, True)
    kernel = demag_spectrum.reshape(parts, planes, rows_x, inner_size, outer_size)
    kernel = (
        kernel.transpose(0, 1, 2, 4, 3).reshape(parts, planes, rows_x, length_y).astype(jnp.float32)
    )
    couplings = ((0, 3, 4), (3, 1, 5), (4, 5, 2))
    field_re = [couple(kernel, spec_re, picks) for picks in couplings]
    field_im = [couple(kernel, spec_im, picks) for picks in couplings]
    demag = back_to_bricks(jnp.stack(field_re), jnp.stack(field_im))
    framed = extended(direction, (("wide", 2), ("narrow", 3)), 1)
    framed = jnp.pad(framed, ((0, 0), (1, 1), (0, 0), (0, 0)))
    weight = jnp.sum(framed * framed, axis=0)
    neighbours = (
        framed[:, 2:, 1:-1, 1:-1]
        + framed[:, :-2, 1:-1, 1:-1]
        + framed[:, 1:-1, 2:, 1:-1]
        + framed[:, 1:-1, :-2, 1:-1]
        + framed[:, 1:-1, 1:-1, 2:]
        + framed[:, 1:-1, 1:-1, :-2]
    )
    present = (
        weight[2:, 1:-1, 1:-1]
        + weight[:-2, 1:-1, 1:-1]
        + weight[1:-1, 2:, 1:-1]
        + weight[1:-1, :-2, 1:-1]
        + weight[1:-1, 1:-1, 2:]
        + weight[1:-1, 1:-1, :-2]
    )
    laplace = neighbours - present[None] * direction
    zeros = jnp.zeros_like(sat_cell)
    uniaxial = jnp.stack([zeros, zeros, 2.0 * anis_cell / sat_cell * direction[2]])
    field = (
        exchange_coef * laplace / sat_cell[None] + demag + applied[:, None, None, None] + uniaxial
    )
    torque = cross(direction, field)
    rate = (
        -(torque + damp_cell[None] * cross(direction, torque)) / (1.0 + damp_cell * damp_cell)[None]
    )
    return (rate, demag)


def split_table(table):
    high = jnp.asarray(np.asarray(table, np.float32)).astype(jnp.bfloat16)
    high64 = np.asarray(np.asarray(table, np.float32).astype(high.dtype), np.float64)
    low = (table - high64).astype(np.float32).astype(high.dtype)
    return np.asarray(high64.astype(high.dtype)), low


class Plan:
    def __init__(self, wide, narrow, layers, width_x, width_y, planes, rows_x, length_y):
        self.wide, self.narrow = wide, narrow
        self.layers, self.width_x, self.width_y = layers, width_x, width_y
        self.planes, self.rows_x = planes, rows_x
        self.length_z, self.length_x, self.length_y = planes * wide, rows_x * narrow, length_y
        self.cells_x, self.cells_y = width_x * wide, width_y * narrow
        self.devices = wide * narrow
        self.special, self.holder = 1, self.narrow * (wide // 2)

    def fits(self):
        return (
            self.narrow == 2
            and self.planes == 4
            and self.wide % 16 == 0
            and self.devices * 2 == self.length_z
            and self.length_z == 2 * self.layers
            and self.length_x == 2 * self.cells_x
            and self.length_y == 2 * self.cells_y
            and self.width_x == 2
            and self.width_y % 128 == 0
            and self.rows_x % 16 == 0
            and 6 * self.cells_x <= self.cells_y
            and (self.layers * self.width_x) % 8 == 0
            and 6 * self.rows_x == 3 * self.layers * self.width_x
        )

    def wave(self):
        w, n = np.divmod(np.arange(self.devices), self.narrow)
        return self.planes * w + np.where(w < self.wide // 2, 1 - n, 1 + n)

    def thickness_tables(self):
        wave = self.wave()
        z = np.arange(self.layers)
        angle = 2.0 * np.pi * ((wave[:, None] * z[None]) % self.length_z) / self.length_z
        ahead = np.stack([np.cos(angle), -np.sin(angle)], 1)
        back = np.stack([2.0 * np.cos(angle), -2.0 * np.sin(angle)], 1)
        middle = 1.0 - 2.0 * (z % 2)
        ahead[self.special, 1] = middle
        back[self.special, 0] = 1.0
        back[self.special, 1] = middle
        back *= -1.0 / (self.length_z * self.length_x * self.length_y)
        n = np.arange(self.devices) % self.narrow
        x = np.arange(self.width_x)
        sign = 1.0 - 2.0 * ((n[:, None] * x[None]) % 2)
        unit_c, unit_x = np.eye(3), np.eye(self.width_x)
        ahead = np.einsum("drz,dx,xv->rxdzv", ahead, sign, unit_x)
        back = np.einsum("drz,dx,cb,xv->bzvdcrx", back, sign, unit_c, unit_x)
        count = self.devices * 6 * self.width_x
        cells = 3 * self.layers * self.width_x
        return ahead.reshape(count // 3, cells // 3), back.reshape(cells, count)

    def lateral_tables(self):
        half = self.cells_y
        y, k = np.arange(half), np.arange(half)
        angle = 2.0 * np.pi * ((y[:, None] * k[None]) % self.length_y) / self.length_y
        cosine, sine = np.cos(angle), np.sin(angle)
        sine[:, 0] = 1.0 - 2.0 * (y % 2)
        ahead_y = np.concatenate([cosine, sine], 1)
        x = (np.arange(self.wide)[None] * self.width_x + np.arange(self.width_x)[:, None]).reshape(-1)
        kx = np.arange(self.length_x)
        angle = 2.0 * np.pi * ((kx[:, None] * x[None]) % self.length_x) / self.length_x
        cosine, sine = np.cos(angle), np.sin(angle)
        ahead_x = np.block([[cosine, sine], [-sine, cosine]])
        back_x = np.block([[cosine.T, -sine.T], [sine.T, cosine.T]])
        return ahead_y, ahead_x, back_x


def halves(value):
    high = value.astype(jnp.bfloat16)
    return high, (value - high.astype(jnp.float32)).astype(jnp.bfloat16)


def mul(left, right):
    return jnp.dot(left, right, preferred_element_type=jnp.float32)


def mul_back(left, right):
    return lax.dot_general(left, right, (((1,), (1,)), ((), ())), preferred_element_type=jnp.float32)


def pick(material, entries, species):
    value = jnp.zeros(material.shape, jnp.float32)
    for s in range(species):
        value = jnp.where(material == s, entries[s], value)
    return value


def rows_of(plan):
    w, n = lax.axis_index("wide"), lax.axis_index("narrow")
    low = w >= plan.wide // 2
    own = jnp.where(low, 1 + n, 1 - n)
    other = jnp.where(low, 2 - n, n)
    return w, n, own, other


def first_kernel(plan, species, spin_at, region_at, material_at, saturation_at, table_at, tensor,
                 out_at, near_at, next_at, swap_at, lower_at, upper_at, turned_at, side_at,
                 spin, region, material, saturation, table, held, held0,
                 out, near, next_, swap, lower, upper, turned, side, sems, done):
    w, n, _, other = rows_of(plan)
    count = plan.rows_x
    moves = [
        pltpu.make_async_copy(source, target, sems.at[k])
        for k, (source, target) in enumerate((
            (saturation_at, saturation), (material_at, material), (region_at, region), (spin_at, spin),
            (table_at, table), (tensor.at[:, other], held),
        ))
    ]
    for move in moves:
        move.start()
    fetch0 = pltpu.make_async_copy(tensor.at[:, 0], held0, sems.at[7])

    @pl.when(w == plan.wide // 2)
    def _():
        fetch0.start()

    sent = []

    def send(source, target):
        move = pltpu.make_async_copy(source, target, done.at[len(sent)])
        move.start()
        sent.append(move)

    for move in moves[:4]:
        move.wait()
    cells = plan.layers * plan.width_x
    magnet = region[...].astype(jnp.float32)
    sat = pick(material[...], saturation, species)
    high, low = [], []
    for c in range(3):
        direction = spin[c * cells : (c + 1) * cells, :] * magnet
        turned[c * cells : (c + 1) * cells, :] = direction
        a, b = halves(direction * sat)
        high.append(a)
        low.append(b)
    high, low = jnp.concatenate(high, 1), jnp.concatenate(low, 1)
    send(turned, turned_at)
    moves[5].wait()
    for t in range(6):
        rows = slice(t * count, (t + 1) * count)
        swap[rows, : plan.length_y] = held[t].astype(jnp.float32)
    send(swap, swap_at)
    moves[4].wait()
    result = mul(table[...], jnp.concatenate([high, low, high], 0))
    group, lanes = plan.devices, plan.width_y
    for c in range(3):
        for j in range(2 * plan.width_x):
            out[pl.ds(c * 2 * plan.width_x + j, group, stride=6 * plan.width_x), :] = result[
                j * group : (j + 1) * group, c * lanes : (c + 1) * lanes]
    send(out, out_at)
    layers3 = 3 * plan.layers
    up, down = turned[pl.ds(1, layers3, stride=2), :], turned[pl.ds(0, layers3, stride=2), :]
    near[...] = jnp.where(w % 2 == 0, up, down)
    next_[...] = jnp.where(w % 2 == 0, down, up)
    send(near, near_at)
    send(next_, next_at)
    column = lax.broadcasted_iota(jnp.int32, (8, plan.width_y), 1)
    chosen = jnp.where(column == jnp.where(n == 0, plan.width_y - 1, 0), 1.0, 0.0).astype(jnp.bfloat16)
    high = turned[...].astype(jnp.bfloat16)
    rest = turned[...] - high.astype(jnp.float32)
    middle, low = halves(rest)
    side[...] = mul_back(chosen, high) + mul_back(chosen, middle) + mul_back(chosen, low)
    send(side, side_at)

    @pl.when(w == plan.wide // 2)
    def _():
        fetch0.wait()
        cut, half = SPLIT * count, plan.cells_y
        flip = flip_of(half)
        minus = mul(jnp.concatenate([held0[t, :, half:] for t in range(6)], 0), flip)
        lower[(6 - SPLIT) * count :, :] = jnp.zeros((8, plan.length_y), jnp.float32)
        upper[cut:, :] = jnp.zeros((8, plan.length_y), jnp.float32)
        for t in range(6):
            plus = held0[t, :, :half].astype(jnp.float32)
            values = jnp.concatenate([plus, minus[t * count : (t + 1) * count, :]], 1)
            edge = values[0:1, :]
            if t < SPLIT:
                upper[t * count : (t + 1) * count, :] = values
                lower[(6 - SPLIT) * count + t : (6 - SPLIT) * count + t + 1, :] = edge
            else:
                lower[(t - SPLIT) * count : (t - SPLIT + 1) * count, :] = values
                upper[cut + t : cut + t + 1, :] = edge
        sends = [pltpu.make_async_copy(lower, lower_at, sems.at[8]), pltpu.make_async_copy(upper, upper_at, sems.at[9])]
        for move in sends:
            move.start()
        for move in sends:
            move.wait()

    for move in sent:
        move.wait()


def flip_of(half):
    sum_of = lax.broadcasted_iota(jnp.int32, (half, half), 0) + lax.broadcasted_iota(jnp.int32, (half, half), 1)
    return jnp.where((sum_of == half) | (sum_of == 0), 1.0, 0.0).astype(jnp.bfloat16)


SPLIT = 3


def unfold_zero(plan, lower, upper, second):
    half, count = plan.cells_y, plan.rows_x
    row = lax.broadcasted_iota(jnp.int32, (count, count), 0)
    col = lax.broadcasted_iota(jnp.int32, (count, count), 1)
    turn = jnp.where(row + col == count, 1.0, 0.0).astype(jnp.bfloat16)
    first = lax.broadcasted_iota(jnp.int32, (count, 2 * half), 0) == 0
    lane0 = lax.broadcasted_iota(jnp.int32, (count, half), 1) == 0
    for t in range(6):
        here, at, there, edge = (
            (upper, t, lower, (6 - SPLIT) * count + t) if t < SPLIT else (lower, t - SPLIT, upper, SPLIT * count + t)
        )
        straight, mirrored = (slice(0, count), slice(count, 2 * count))[:: 1 if t < SPLIT else -1]
        rows = slice(at * count, (at + 1) * count)
        plus, minus = here[rows, :half], here[rows, half:]
        second[t, straight, :half] = plus
        second[t, straight, half:] = minus
        crossed = jnp.concatenate([jnp.where(lane0, plus, minus), jnp.where(lane0, minus, plus)], 1)
        crossed = mul(turn, crossed.astype(jnp.bfloat16))
        second[t, mirrored, :] = jnp.where(first, there[edge : edge + 1, :], crossed)


COUPLINGS = ((0, 3, 4), (3, 1, 5), (4, 5, 2))


def ready_kernel(plan, tensor, table_at, own_part, table):
    _, _, own, _ = rows_of(plan)
    half, count = plan.cells_y, plan.rows_x
    table[...] = table_at[...]
    turned = mul(jnp.concatenate([tensor[t, own, :, half:] for t in range(6)], 0), flip_of(half))
    for t in range(6):
        own_part[t, :, :half] = tensor[t, own, :, :half].astype(jnp.float32)
        own_part[t, :, half:] = turned[t * count : (t + 1) * count, :]


def ahead_kernel(plan, got, table, swapped, mixed, far_part):
    w, n, _, _ = rows_of(plan)
    half, wide = plan.cells_y, plan.wide
    cells_x, length_x, narrow = plan.cells_x, plan.length_x, plan.narrow
    block = 6 * plan.width_x
    lines = []
    for c in range(3):
        for j in range(2 * plan.width_x):
            row = c * 2 * plan.width_x + j
            lines.append(jnp.concatenate(
                [got[pl.ds(m * block + row, wide, stride=narrow * block), :] for m in range(narrow)], 1))
    lines = jnp.concatenate(lines, 0)
    high, low = halves(lines)
    y_high, y_low = table[:half, :], table[half : 2 * half, :]
    x_ahead = table[2 * half : 2 * half + 2 * length_x, : 6 * cells_x]
    waves = mul(high, y_high) + (mul(low, y_high) + mul(high, y_low))
    flip = flip_of(half)
    count = plan.rows_x
    turned_far = mul(swapped[:, half : 2 * half].astype(jnp.bfloat16), flip)
    for t in range(6):
        rows = slice(t * count, (t + 1) * count)
        far_part[t, :, :half] = swapped[rows, :half]
        far_part[t, :, half:] = turned_far[rows, :]
    edge = lax.broadcasted_iota(jnp.int32, (cells_x, half), 1) == 0
    parts = [(waves[g * cells_x : (g + 1) * cells_x, :half], waves[g * cells_x : (g + 1) * cells_x, half:])
             for g in range(6)]

    def stage(g, real, imag):
        (pr, qr), (pi, qi) = real, imag
        plus = jnp.where(edge, pr, pr + qi), jnp.where(edge, pi, pi - qr)
        minus = jnp.where(edge, qr, pr - qi), jnp.where(edge, qi, pi + qr)
        stack = jnp.concatenate([jnp.concatenate([p, m], 1) for p, m in zip(plus, minus)], 0)
        a, b = halves(stack)
        mixed[g] = mul(x_ahead, jnp.concatenate([a, b, a], 0))

    special = jnp.logical_and(w == 0, n == 1)

    @pl.when(special)
    def _():
        none = jnp.zeros((cells_x, half), jnp.float32)
        for g in range(6):
            stage(g, parts[g], (none, none))

    @pl.when(jnp.logical_not(special))
    def _():
        for c in range(3):
            stage(c, parts[2 * c], parts[2 * c + 1])


def back_kernel(plan, mixed, own_part, far_part, table, lower, upper, out, packed, second):
    w, n, _, _ = rows_of(plan)
    lanes, half, wide = plan.width_y, plan.cells_y, plan.wide
    length_x, narrow = plan.length_x, plan.narrow
    block, per_c = 6 * plan.width_x, 2 * plan.cells_x
    y_high, y_low = table[:half, :], table[half : 2 * half, :]
    base = 2 * half
    xb_pair = table[base : base + per_c, half : half + 4 * length_x]
    xb_low = table[base + per_c : base + 2 * per_c, half : half + 2 * length_x]
    step = 16

    def couple(paired):
        for lane in range(0, half, 128):
            for row in range(0, length_x, step):
                left = slice(lane, lane + 128)
                right = slice(half + lane, half + lane + 128)
                cr, sr = slice(row, row + step), slice(length_x + row, length_x + row + step)
                part = own_part if row < plan.rows_x else far_part
                at = slice(row % plan.rows_x, row % plan.rows_x + step)
                if lane == 0:
                    edge = lax.broadcasted_iota(jnp.int32, (step, 128), 1) == 0
                fields = [
                    (mixed[g, cr, left], mixed[g, sr, left], mixed[g, cr, right], mixed[g, sr, right])
                    for g in range(6 if paired else 3)
                ]
                for i in range(3):
                    sums = []
                    for s, lanes_at in ((0, left), (2, right)):
                        real = imag = None
                        for j in range(3):
                            t = COUPLINGS[i][j]
                            ka = part[t, at, lanes_at]
                            if paired:
                                kb = second[t, cr, lanes_at]
                                a, b = fields[2 * j], fields[2 * j + 1]
                                re = ka * a[s] - kb * b[s + 1]
                                im = ka * a[s + 1] + kb * b[s]
                            else:
                                re, im = ka * fields[j][s], ka * fields[j][s + 1]
                            real = re if real is None else real + re
                            imag = im if imag is None else imag + im
                        sums.append((real, imag))
                    (pr, pi), (mr, mi) = sums
                    even_re, even_im, odd_re, odd_im = pr + mr, pi + mi, mi - pi, pr - mr
                    if lane == 0:
                        even_re, even_im = jnp.where(edge, pr, even_re), jnp.where(edge, pi, even_im)
                        odd_re, odd_im = jnp.where(edge, mr, odd_re), jnp.where(edge, mi, odd_im)
                    for value, base_at, lanes_at in (
                        (even_re, 0, left), (even_im, length_x, left),
                        (odd_re, 0, right), (odd_im, length_x, right),
                    ):
                        a, b = halves(value)
                        high_at, low_at = base_at + row, 2 * length_x + base_at + row
                        packed[i, high_at : high_at + step, lanes_at] = a
                        packed[i, low_at : low_at + step, lanes_at] = b

    special = jnp.logical_and(w == 0, n == 1)

    @pl.when(special)
    def _():
        unfold_zero(plan, lower, upper, second)
        couple(True)

    pl.when(jnp.logical_not(special))(lambda: couple(False))
    back = []
    for i in range(3):
        back.append(mul(xb_pair, packed[i]) + mul(xb_low, packed[i, : 2 * length_x, :]))
    high, low = halves(jnp.concatenate(back, 0))
    result = mul_back(high, y_high) + (mul_back(low, y_high) + mul_back(high, y_low))
    for c in range(3):
        for j in range(2 * plan.width_x):
            row = c * 2 * plan.width_x + j
            for m in range(narrow):
                out[pl.ds(m * block + row, wide, stride=narrow * block), :] = result[
                    row * wide : (row + 1) * wide, m * lanes : (m + 1) * lanes]


def local_kernel(plan, species, turned, side, near, next_, material, saturation, anisotropy,
                 damping, applied, table, out, damp, woven):
    w, n = lax.axis_index("wide"), lax.axis_index("narrow")
    cells, layers = plan.layers * plan.width_x, plan.layers
    row = lax.broadcasted_iota(jnp.int32, (cells, plan.width_y), 0)
    col = lax.broadcasted_iota(jnp.int32, (cells, plan.width_y), 1)
    first, last = col == 0, col == plan.width_y - 1
    even = row % 2 == 0
    ahead = jnp.where(n == 0, 1.0, 0.0)
    sat = pick(material[...], saturation, species)
    anis = pick(material[...], anisotropy, species)
    damp[...] = pick(material[...], damping, species)
    square = lax.broadcasted_iota(jnp.int32, (cells, cells), 0) == lax.broadcasted_iota(
        jnp.int32, (cells, cells), 1)
    sums, present, own = [], jnp.zeros((cells, plan.width_y), jnp.float32), []
    for c in range(3):
        d = turned[c * cells : (c + 1) * cells, :]
        line = jnp.broadcast_to(side[0:1, c * cells : (c + 1) * cells], (cells, cells))
        s = jnp.sum(jnp.where(square, line, 0.0), axis=1, keepdims=True)
        a, b = near[c * layers : (c + 1) * layers, :], next_[c * layers : (c + 1) * layers, :]
        woven[pl.ds(0, layers, stride=2), :] = jnp.where(w % 2 == 0, b, a)
        woven[pl.ds(1, layers, stride=2), :] = jnp.where(w % 2 == 0, a, b)
        beside = (
            jnp.where(row >= 2, pltpu.roll(d, 2, 0), 0.0),
            jnp.where(row < cells - 2, pltpu.roll(d, cells - 2, 0), 0.0),
            woven[...],
            jnp.where(even, pltpu.roll(d, cells - 1, 0), pltpu.roll(d, 1, 0)),
            pltpu.roll(jnp.where(first, s * ahead, d), plan.width_y - 1, 1),
            pltpu.roll(jnp.where(last, s * (1.0 - ahead), d), 1, 1),
        )
        total = beside[0]
        present = present + beside[0] * beside[0]
        for v in beside[1:]:
            total = total + v
            present = present + v * v
        sums.append(total)
        own.append(d)
    for c in range(3):
        field = exchange_coef * (sums[c] - present * own[c]) / sat + applied[c]
        if c == 2:
            field = field + 2.0 * anis / sat * own[2]
        out[c * cells : (c + 1) * cells, :] = field


def last_kernel(plan, got, table, base, turned, damping, rate_at, demag_at, rate, demag, sems):
    cells = plan.layers * plan.width_x
    t_high, t_low = table[: 3 * cells, :], table[3 * cells :, :]
    high, low = halves(got[...])
    demag[...] = mul(t_high, high) + (mul(t_low, high) + mul(t_high, low))
    moves = [pltpu.make_async_copy(demag, demag_at, sems.at[3])]
    moves[0].start()
    damp = damping[...]
    d = [turned[c * cells : (c + 1) * cells, :] for c in range(3)]
    f = [demag[c * cells : (c + 1) * cells, :] + base[c * cells : (c + 1) * cells, :] for c in range(3)]

    def turn(u, v):
        return [u[1] * v[2] - u[2] * v[1], u[2] * v[0] - u[0] * v[2], u[0] * v[1] - u[1] * v[0]]

    torque = turn(d, f)
    again = turn(d, torque)
    scale = -1.0 / (1.0 + damp * damp)
    for c in range(3):
        rows = pl.ds(c * cells, cells)
        rate[rows, :] = (torque[c] + damp * again[c]) * scale
        moves.append(pltpu.make_async_copy(rate.at[rows], rate_at.at[rows], sems.at[c]))
        moves[-1].start()
    for move in moves:
        move.wait()


LIMITS = (67043328, 8 << 20, 8 << 20, 4 << 20, 8 << 20)
VMEM = pl.BlockSpec(memory_space=pltpu.VMEM)
SMEM = pl.BlockSpec(memory_space=pltpu.SMEM)
HBM = pl.BlockSpec(memory_space=pltpu.HBM)


def plane_shards(plan, spin, region, material, saturation, anisotropy, damping, applied, demag_spectrum):
    f32, bf16 = jnp.float32, jnp.bfloat16
    cells, lanes = plan.layers * plan.width_x, plan.width_y
    count, length_y, length_x = plan.devices * 6 * plan.width_x, plan.length_y, plan.length_x
    species = saturation.shape[0]
    shape = jax.ShapeDtypeStruct
    spin2 = spin.reshape(3 * cells, lanes)
    region2, material2 = region.reshape(cells, lanes), material.reshape(cells, lanes)
    ahead_z, back_z = plan.thickness_tables()
    ahead_y, ahead_x, back_x = plan.lateral_tables()
    az, bz, ay = (split_table(t) for t in (ahead_z, back_z, ahead_y))
    ax, bx = split_table(ahead_x), split_table(back_x)
    x_ahead = np.concatenate([ax[0], ax[0], ax[1]], 1)
    xb_pair = np.concatenate([bx[0], bx[0]], 1)

    def call(body, out_shape, in_specs, out_specs, scratch, flops, limit=24 << 20):
        return pl.pallas_call(
            body, out_shape=out_shape, in_specs=in_specs, out_specs=out_specs, scratch_shapes=scratch,
            compiler_params=pltpu.CompilerParams(vmem_limit_bytes=limit),
            cost_estimate=pl.CostEstimate(flops=flops, bytes_accessed=1 << 20, transcendentals=0),
        )

    rows6 = 6 * plan.rows_x
    table_in = jnp.asarray(np.concatenate([az[0], az[0], az[1]], 1))
    table_out = jnp.asarray(np.concatenate(bz, 0))
    outs = ((count, lanes), (3 * plan.layers, lanes), (3 * plan.layers, lanes), (rows6, length_y),
            ((6 - SPLIT) * plan.rows_x + 8, length_y), (SPLIT * plan.rows_x + 8, length_y), (3 * cells, lanes),
            (8, 3 * cells))
    outs = tuple(shape(o, f32) for o in outs)
    half = plan.cells_y
    small = np.zeros((2 * length_x, 2 * half), ax[0].dtype)
    small[:, : 6 * plan.cells_x] = x_ahead
    small[: 2 * plan.cells_x, half : half + 4 * length_x] = xb_pair
    small[2 * plan.cells_x : 4 * plan.cells_x, half : half + 2 * length_x] = bx[1]
    table = jnp.asarray(np.concatenate([ay[0], ay[1], small], 0))

    out, near, next_, swap, lower, upper, turned, side = call(
        partial(first_kernel, plan, species),
        outs, [HBM] * 6, (HBM,) * len(outs),
        [pltpu.VMEM((3 * cells, lanes), f32), pltpu.VMEM((cells, lanes), jnp.int32),
         pltpu.VMEM((cells, lanes), jnp.int32), pltpu.SMEM((species,), f32),
         pltpu.VMEM(table_in.shape, bf16),
         pltpu.VMEM((6, plan.rows_x, length_y), bf16), pltpu.VMEM((6, plan.rows_x, length_y), bf16)]
        + [pltpu.VMEM(o.shape, o.dtype) for o in outs]
        + [pltpu.SemaphoreType.DMA((10,)), pltpu.SemaphoreType.DMA((6,))],
        1 << 28, LIMITS[0],
    )(spin2, region2, material2, saturation, table_in, demag_spectrum)

    both = ("wide", "narrow")
    swapped = lax.ppermute(swap, "narrow", [(0, 1), (1, 0)])
    blocks = (plan.devices, 3, 2 * plan.width_x, lanes)
    got = lax.all_to_all(out.reshape(blocks), both, 0, 0, tiled=True).reshape(count, lanes)
    lower = lax.ppermute(lower, both, [(plan.holder, plan.special)])
    upper = lax.ppermute(upper, both, [(plan.holder + 1, plan.special)])
    side = lax.ppermute(side, "narrow", [(0, 1), (1, 0)])
    pairs = [(i ^ 1, i) for i in range(plan.wide)]
    near = lax.ppermute(near, "wide", pairs)
    pairs = [(i, j) for i in range(1, plan.wide - 1, 2) for i, j in ((i, i + 1), (i + 1, i))]
    next_ = lax.ppermute(next_, "wide", pairs)

    half_shape = shape((6, plan.rows_x, length_y), f32)
    own_part, table = call(
        partial(ready_kernel, plan), (half_shape, shape(table.shape, bf16)), [VMEM] * 2, (VMEM, VMEM), [],
        1 << 26, LIMITS[1],
    )(demag_spectrum, table)
    mixed, far_part = call(
        partial(ahead_kernel, plan), (shape((6, 2 * length_x, length_y), f32), half_shape),
        [VMEM] * 3, (VMEM, VMEM), [], 1 << 29, LIMITS[2],
    )(got, table, swapped)
    sent = call(
        partial(back_kernel, plan),
        shape((count, lanes), f32),
        [VMEM] * 6, VMEM,
        [pltpu.VMEM((3, 4 * length_x, length_y), bf16), pltpu.VMEM((6, length_x, length_y), f32)],
        1 << 29, LIMITS[2],
    )(mixed, own_part, far_part, table, lower, upper)

    back = lax.all_to_all(sent.reshape(blocks), both, 0, 0, tiled=True).reshape(count, lanes)
    base, damp = call(
        partial(local_kernel, plan, species), (shape((3 * cells, lanes), f32), shape((cells, lanes), f32)),
        [VMEM] * 5 + [SMEM] * 4 + [VMEM], (VMEM, VMEM), [pltpu.VMEM((cells, lanes), f32)], 1 << 22, LIMITS[3],
    )(turned, side, near, next_, material2, saturation, anisotropy, damping, applied, table_out)

    rate, demag = call(
        partial(last_kernel, plan),
        (shape((3 * cells, lanes), f32), shape((3 * cells, lanes), f32)),
        [VMEM] * 5, (HBM, HBM),
        [pltpu.VMEM((3 * cells, lanes), f32), pltpu.VMEM((3 * cells, lanes), f32), pltpu.SemaphoreType.DMA((4,))],
        1 << 28, LIMITS[4],
    )(back, table_out, base, turned, damp)
    return rate.reshape(spin.shape), demag.reshape(spin.shape)


def shards(*args):
    spin, demag_spectrum = args[0], args[-1]
    _, layers, width_x, width_y = spin.shape
    _, planes, rows_x, length_y = demag_spectrum.shape
    plan = Plan(lax.axis_size("wide"), lax.axis_size("narrow"), layers, width_x, width_y,
                planes, rows_x, length_y)
    if plan.fits():
        return plane_shards(plan, *args)
    return general_shards(*args)


def solution(mesh):
    placed = (
        P(None, None, "wide", "narrow"),
        P(None, "wide", "narrow"),
        P(None, "wide", "narrow"),
        P(),
        P(),
        P(),
        P(),
        P(None, "wide", "narrow", None),
    )
    return jax.shard_map(
        shards,
        mesh=mesh,
        in_specs=placed,
        out_specs=(P(None, None, "wide", "narrow"), P(None, None, "wide", "narrow")),
        check_vma=False,
    )
```

```python
from functools import partial
import math

import jax
import jax.numpy as jnp
import numpy as np
from jax import lax
from jax.experimental import pallas as pl
from jax.experimental.pallas import tpu as pltpu
from jax.sharding import PartitionSpec as P


exchange_coef = 0.3
highest = lax.Precision.HIGHEST


def extended(x, sides, width):
    for axis, dim in sides:
        peers, length = (lax.axis_size(axis), x.shape[dim])
        up = [(i, (i + 1) % peers) for i in range(peers - 1)]
        down = [(j, i) for i, j in up]
        last = lax.slice_in_dim(x, length - width, length, axis=dim)
        leading = lax.slice_in_dim(x, 0, width, axis=dim)
        before = lax.ppermute(last, axis, up)
        after = lax.ppermute(leading, axis, down)
        x = jnp.concatenate([before, x, after], axis=dim)
    return x


def phase_table(rows_count, cols_count, length, sign):
    left_index = lax.broadcasted_iota(jnp.int32, (rows_count, cols_count), 0)
    right_index = lax.broadcasted_iota(jnp.int32, (rows_count, cols_count), 1)
    angle = (left_index * right_index % length).astype(jnp.float32) * (2.0 * math.pi / length)
    return (jnp.cos(angle), sign * jnp.sin(angle))


def contract(pattern, phases, values):
    phase_re, phase_im = phases
    value_re, value_im = values
    product = partial(jnp.einsum, pattern, precision=highest)
    if value_im is None:
        return (product(phase_re, value_re), product(phase_im, value_re))
    return (
        product(phase_re, value_re) - product(phase_im, value_im),
        product(phase_re, value_im) + product(phase_im, value_re),
    )


def factors(half_size, at_end):
    if at_end:
        inner_size = math.gcd(half_size, 128)
    else:
        inner_size = max(
            (
                divisor
                for divisor in range(1, half_size + 1)
                if half_size % divisor == 0 and divisor * divisor <= 2 * half_size
            )
        )
    return (inner_size, 2 * half_size // inner_size)


def forward(values, at_end, natural):
    value_re, value_im = values
    extent = value_re.shape
    half_size = extent[1]
    length = 2 * half_size
    inner_size, outer_size = factors(half_size, at_end)
    tail_index = "" if at_end else "b"
    blocked = (extent[0], outer_size // 2, inner_size) + extent[2:]
    value_re = value_re.reshape(blocked)
    value_im = None if value_im is None else value_im.reshape(blocked)
    phases = phase_table(outer_size, outer_size // 2, outer_size, -1.0)
    work_re, work_im = contract(
        "kn,anp" + tail_index + "->akp" + tail_index, phases, (value_re, value_im)
    )
    twist_re, twist_im = phase_table(outer_size, inner_size, length, -1.0)
    if not at_end:
        twist_re, twist_im = (twist_re[:, :, None], twist_im[:, :, None])
    work_re, work_im = (
        work_re * twist_re - work_im * twist_im,
        work_re * twist_im + work_im * twist_re,
    )
    target = "ajk" if natural else "akj"
    phases = phase_table(inner_size, inner_size, inner_size, -1.0)
    out_re, out_im = contract(
        "jp,akp" + tail_index + "->" + target + tail_index, phases, (work_re, work_im)
    )
    merged = (extent[0], length) + extent[2:]
    return (out_re.reshape(merged), out_im.reshape(merged))


def inverse(values, at_end, natural, real_only):
    value_re, value_im = values
    extent = value_re.shape
    length = extent[1]
    half_size = length // 2
    inner_size, outer_size = factors(half_size, at_end)
    tail_index = "" if at_end else "b"
    if natural:
        blocked = (extent[0], inner_size, outer_size) + extent[2:]
        source = "ajk"
    else:
        blocked = (extent[0], outer_size, inner_size) + extent[2:]
        source = "akj"
    phases = phase_table(inner_size, inner_size, inner_size, 1.0)
    work_re, work_im = contract(
        "pj," + source + tail_index + "->akp" + tail_index,
        phases,
        (value_re.reshape(blocked), value_im.reshape(blocked)),
    )
    twist_re, twist_im = phase_table(outer_size, inner_size, length, 1.0)
    if not at_end:
        twist_re, twist_im = (twist_re[:, :, None], twist_im[:, :, None])
    work_re, work_im = (
        work_re * twist_re - work_im * twist_im,
        work_re * twist_im + work_im * twist_re,
    )
    phases = phase_table(outer_size // 2, outer_size, outer_size, 1.0)
    pattern = "nk,akp" + tail_index + "->anp" + tail_index
    scale = 1.0 / length
    merged = (extent[0], half_size) + extent[2:]
    if real_only:
        product = partial(jnp.einsum, pattern, precision=highest)
        result = product(phases[0], work_re) - product(phases[1], work_im)
        return result.reshape(merged) * scale
    out_re, out_im = contract(pattern, phases, (work_re, work_im))
    return (out_re.reshape(merged) * scale, out_im.reshape(merged) * scale)


def along_x(pieces):
    piece_re, piece_im = pieces
    members, planes, cells_x, cells_y = piece_re.shape
    extent = (members * planes, cells_x, cells_y)
    out_re, out_im = forward((piece_re.reshape(extent), piece_im.reshape(extent)), False, True)
    merged = (members, planes, 2 * cells_x, cells_y)
    return (out_re.reshape(merged), out_im.reshape(merged))


def along_y(pieces):
    piece_re, piece_im = pieces
    members, planes, rows_x, cells_y = piece_re.shape
    extent = (members * planes * rows_x, cells_y)
    out_re, out_im = forward((piece_re.reshape(extent), piece_im.reshape(extent)), True, False)
    merged = (members, planes, rows_x, 2 * cells_y)
    return (out_re.reshape(merged), out_im.reshape(merged))


def back_to_bricks(field_re, field_im):
    members, planes, rows_x, length_y = field_re.shape
    flattened = (members * planes * rows_x, length_y)
    grid_re, grid_im = inverse(
        (field_re.reshape(flattened), field_im.reshape(flattened)), True, False, False
    )
    merged = (members, planes, rows_x, length_y // 2)
    piece_re = lax.all_to_all(
        grid_re.reshape(merged), "narrow", split_axis=3, concat_axis=2, tiled=True
    )
    piece_im = lax.all_to_all(
        grid_im.reshape(merged), "narrow", split_axis=3, concat_axis=2, tiled=True
    )
    members, planes, length_x, cells_y = piece_re.shape
    extent = (members * planes, length_x, cells_y)
    out_re, out_im = inverse(
        (piece_re.reshape(extent), piece_im.reshape(extent)), False, True, False
    )
    invert_merged = (members, planes, length_x // 2, cells_y)
    columns = (out_re.reshape(invert_merged), out_im.reshape(invert_merged))
    piece_re, piece_im = lax.all_to_all(columns, "wide", split_axis=2, concat_axis=1, tiled=True)
    members, planes, cells_x, cells_y = piece_re.shape
    extent = (members, planes, cells_x * cells_y)
    result = inverse((piece_re.reshape(extent), piece_im.reshape(extent)), False, True, True)
    merged = (members, planes // 2, cells_x, cells_y)
    return result.reshape(merged)


def couple(kernel, values, picks):
    return -(
        kernel[picks[0]] * values[0] + kernel[picks[1]] * values[1] + kernel[picks[2]] * values[2]
    )


def cross(left, right):
    return jnp.stack(
        [
            left[1] * right[2] - left[2] * right[1],
            left[2] * right[0] - left[0] * right[2],
            left[0] * right[1] - left[1] * right[0],
        ]
    )


def general_shards(spin, region, material, saturation, anisotropy, damping, applied, demag_spectrum):
    magnet = region.astype(jnp.float32)
    direction = spin * magnet[None]
    species = saturation.shape[0]
    chosen = (
        material[None] == lax.broadcasted_iota(jnp.int32, (species,) + material.shape, 0)
    ).astype(jnp.float32)

    def lookup(entries):
        return jnp.sum(chosen * entries[:, None, None, None], axis=0)

    sat_cell = lookup(saturation)
    anis_cell = lookup(anisotropy)
    damp_cell = lookup(damping)
    moment = direction * sat_cell[None]
    components, layers, width_x, width_y = spin.shape
    flattened = moment.reshape(components, layers, width_x * width_y)
    spec_re, spec_im = forward((flattened, None), False, True)
    stacked = (components, 2 * layers, width_x, width_y)
    spectra = along_x(
        (
            lax.all_to_all(
                spec_re.reshape(stacked), "wide", split_axis=1, concat_axis=2, tiled=True
            ),
            lax.all_to_all(
                spec_im.reshape(stacked), "wide", split_axis=1, concat_axis=2, tiled=True
            ),
        )
    )
    spec_re, spec_im = along_y(
        lax.all_to_all(spectra, "narrow", split_axis=2, concat_axis=3, tiled=True)
    )
    parts, planes, rows_x, length_y = demag_spectrum.shape
    inner_size, outer_size = factors(length_y // 2, True)
    kernel = demag_spectrum.reshape(parts, planes, rows_x, inner_size, outer_size)
    kernel = (
        kernel.transpose(0, 1, 2, 4, 3).reshape(parts, planes, rows_x, length_y).astype(jnp.float32)
    )
    couplings = ((0, 3, 4), (3, 1, 5), (4, 5, 2))
    field_re = [couple(kernel, spec_re, picks) for picks in couplings]
    field_im = [couple(kernel, spec_im, picks) for picks in couplings]
    demag = back_to_bricks(jnp.stack(field_re), jnp.stack(field_im))
    framed = extended(direction, (("wide", 2), ("narrow", 3)), 1)
    framed = jnp.pad(framed, ((0, 0), (1, 1), (0, 0), (0, 0)))
    weight = jnp.sum(framed * framed, axis=0)
    neighbours = (
        framed[:, 2:, 1:-1, 1:-1]
        + framed[:, :-2, 1:-1, 1:-1]
        + framed[:, 1:-1, 2:, 1:-1]
        + framed[:, 1:-1, :-2, 1:-1]
        + framed[:, 1:-1, 1:-1, 2:]
        + framed[:, 1:-1, 1:-1, :-2]
    )
    present = (
        weight[2:, 1:-1, 1:-1]
        + weight[:-2, 1:-1, 1:-1]
        + weight[1:-1, 2:, 1:-1]
        + weight[1:-1, :-2, 1:-1]
        + weight[1:-1, 1:-1, 2:]
        + weight[1:-1, 1:-1, :-2]
    )
    laplace = neighbours - present[None] * direction
    zeros = jnp.zeros_like(sat_cell)
    uniaxial = jnp.stack([zeros, zeros, 2.0 * anis_cell / sat_cell * direction[2]])
    field = (
        exchange_coef * laplace / sat_cell[None] + demag + applied[:, None, None, None] + uniaxial
    )
    torque = cross(direction, field)
    rate = (
        -(torque + damp_cell[None] * cross(direction, torque)) / (1.0 + damp_cell * damp_cell)[None]
    )
    return (rate, demag)


def split_table(table):
    high = jnp.asarray(np.asarray(table, np.float32)).astype(jnp.bfloat16)
    high64 = np.asarray(np.asarray(table, np.float32).astype(high.dtype), np.float64)
    low = (table - high64).astype(np.float32).astype(high.dtype)
    return np.asarray(high64.astype(high.dtype)), low


class Plan:
    def __init__(self, wide, narrow, layers, width_x, width_y, planes, rows_x, length_y):
        self.wide, self.narrow = wide, narrow
        self.layers, self.width_x, self.width_y = layers, width_x, width_y
        self.planes, self.rows_x = planes, rows_x
        self.length_z, self.length_x, self.length_y = planes * wide, rows_x * narrow, length_y
        self.cells_x, self.cells_y = width_x * wide, width_y * narrow
        self.devices = wide * narrow
        self.special, self.holder = 1, self.narrow * (wide // 2)

    def fits(self):
        return (
            self.narrow == 2
            and self.planes == 4
            and self.wide % 16 == 0
            and self.devices * 2 == self.length_z
            and self.length_z == 2 * self.layers
            and self.length_x == 2 * self.cells_x
            and self.length_y == 2 * self.cells_y
            and self.width_x == 2
            and self.width_y % 128 == 0
            and self.rows_x % 16 == 0
            and 6 * self.cells_x <= self.cells_y
            and (self.layers * self.width_x) % 8 == 0
            and 6 * self.rows_x == 3 * self.layers * self.width_x
        )

    def wave(self):
        w, n = np.divmod(np.arange(self.devices), self.narrow)
        return self.planes * w + np.where(w < self.wide // 2, 1 - n, 1 + n)

    def thickness_tables(self):
        wave = self.wave()
        z = np.arange(self.layers)
        angle = 2.0 * np.pi * ((wave[:, None] * z[None]) % self.length_z) / self.length_z
        ahead = np.stack([np.cos(angle), -np.sin(angle)], 1)
        back = np.stack([2.0 * np.cos(angle), -2.0 * np.sin(angle)], 1)
        middle = 1.0 - 2.0 * (z % 2)
        ahead[self.special, 1] = middle
        back[self.special, 0] = 1.0
        back[self.special, 1] = middle
        back *= -1.0 / (self.length_z * self.length_x * self.length_y)
        n = np.arange(self.devices) % self.narrow
        x = np.arange(self.width_x)
        sign = 1.0 - 2.0 * ((n[:, None] * x[None]) % 2)
        unit_x = np.eye(self.width_x)
        ahead = np.einsum("drz,dx,xv->rxdzv", ahead, sign, unit_x)
        back = np.einsum("drz,dx,xv->zvrxd", back, sign, unit_x)
        count = self.devices * 6 * self.width_x
        cells = 3 * self.layers * self.width_x
        return ahead.reshape(count // 3, cells // 3), back.reshape(cells // 3, count // 3)

    def lateral_tables(self):
        half = self.cells_y
        y, k = np.arange(half), np.arange(half)
        angle = 2.0 * np.pi * ((y[:, None] * k[None]) % self.length_y) / self.length_y
        cosine, sine = np.cos(angle), np.sin(angle)
        sine[:, 0] = 1.0 - 2.0 * (y % 2)
        ahead_y = np.concatenate([cosine, sine], 1)
        x = (np.arange(self.wide)[None] * self.width_x + np.arange(self.width_x)[:, None]).reshape(-1)
        kx = np.arange(self.length_x)
        angle = 2.0 * np.pi * ((kx[:, None] * x[None]) % self.length_x) / self.length_x
        cosine, sine = np.cos(angle), np.sin(angle)
        ahead_x = np.block([[cosine, sine], [-sine, cosine]])
        back_x = np.block([[cosine.T, -sine.T], [sine.T, cosine.T]])
        return ahead_y, ahead_x, back_x


def halves(value):
    high = value.astype(jnp.bfloat16)
    return high, (value - high.astype(jnp.float32)).astype(jnp.bfloat16)


def mul(left, right):
    return jnp.dot(left, right, preferred_element_type=jnp.float32)


def mul_back(left, right):
    return lax.dot_general(left, right, (((1,), (1,)), ((), ())), preferred_element_type=jnp.float32)


def pick(material, entries, species):
    value = jnp.zeros(material.shape, jnp.float32)
    for s in range(species):
        value = jnp.where(material == s, entries[s], value)
    return value


def rows_of(plan):
    w, n = lax.axis_index("wide"), lax.axis_index("narrow")
    low = w >= plan.wide // 2
    own = jnp.where(low, 1 + n, 1 - n)
    other = jnp.where(low, 2 - n, n)
    return w, n, own, other


def first_kernel(plan, species, spin_at, region_at, material_at, saturation_at, table_at, tensor,
                 out_at, near_at, next_at, swap_at, lower_at, upper_at, turned_at, side_at,
                 spin, region, material, saturation, table, held, held0,
                 out, near, next_, swap, lower, upper, turned, side, sems, done):
    w, n, _, other = rows_of(plan)
    count = plan.rows_x
    moves = [
        pltpu.make_async_copy(source, target, sems.at[k])
        for k, (source, target) in enumerate((
            (saturation_at, saturation), (material_at, material), (region_at, region), (spin_at, spin),
            (table_at, table), (tensor.at[:, other], held),
        ))
    ]
    for move in moves:
        move.start()
    fetch0 = pltpu.make_async_copy(tensor.at[:, 0], held0, sems.at[7])

    @pl.when(w == plan.wide // 2)
    def _():
        fetch0.start()

    sent = []

    def send(source, target):
        move = pltpu.make_async_copy(source, target, done.at[len(sent)])
        move.start()
        sent.append(move)

    for move in moves[:4]:
        move.wait()
    cells = plan.layers * plan.width_x
    magnet = region[...].astype(jnp.float32)
    sat = pick(material[...], saturation, species)
    high, low = [], []
    for c in range(3):
        direction = spin[c * cells : (c + 1) * cells, :] * magnet
        turned[c * cells : (c + 1) * cells, :] = direction
        a, b = halves(direction * sat)
        high.append(a)
        low.append(b)
    high, low = jnp.concatenate(high, 1), jnp.concatenate(low, 1)
    send(turned, turned_at)
    moves[5].wait()
    for t in range(6):
        rows = slice(t * count, (t + 1) * count)
        swap[rows, : plan.length_y] = held[t].astype(jnp.float32)
    send(swap, swap_at)
    moves[4].wait()
    result = mul(table[...], jnp.concatenate([high, low, high], 0))
    group, lanes = plan.devices, plan.width_y
    for c in range(3):
        for j in range(2 * plan.width_x):
            out[pl.ds(c * 2 * plan.width_x + j, group, stride=6 * plan.width_x), :] = result[
                j * group : (j + 1) * group, c * lanes : (c + 1) * lanes]
    send(out, out_at)
    layers3 = 3 * plan.layers
    up, down = turned[pl.ds(1, layers3, stride=2), :], turned[pl.ds(0, layers3, stride=2), :]
    near[...] = jnp.where(w % 2 == 0, up, down)
    next_[...] = jnp.where(w % 2 == 0, down, up)
    send(near, near_at)
    send(next_, next_at)
    column = lax.broadcasted_iota(jnp.int32, (8, plan.width_y), 1)
    chosen = jnp.where(column == jnp.where(n == 0, plan.width_y - 1, 0), 1.0, 0.0).astype(jnp.bfloat16)
    high = turned[...].astype(jnp.bfloat16)
    rest = turned[...] - high.astype(jnp.float32)
    middle, low = halves(rest)
    side[...] = mul_back(chosen, high) + mul_back(chosen, middle) + mul_back(chosen, low)
    send(side, side_at)

    @pl.when(w == plan.wide // 2)
    def _():
        fetch0.wait()
        cut, half = SPLIT * count, plan.cells_y
        flip = flip_of(half)
        minus = mul(jnp.concatenate([held0[t, :, half:] for t in range(6)], 0), flip)
        lower[(6 - SPLIT) * count :, :] = jnp.zeros((8, plan.length_y), jnp.float32)
        upper[cut:, :] = jnp.zeros((8, plan.length_y), jnp.float32)
        for t in range(6):
            plus, rest = held0[t, :, :half].astype(jnp.float32), minus[t * count : (t + 1) * count, :]
            if t < SPLIT:
                here, there, at, edge = upper, lower, t * count, (6 - SPLIT) * count + t
            else:
                here, there, at, edge = lower, upper, (t - SPLIT) * count, cut + t
            here[at : at + count, :half] = plus
            here[at : at + count, half:] = rest
            there[edge : edge + 1, :half] = plus[0:1, :]
            there[edge : edge + 1, half:] = rest[0:1, :]
        sends = [pltpu.make_async_copy(lower, lower_at, sems.at[8]), pltpu.make_async_copy(upper, upper_at, sems.at[9])]
        for move in sends:
            move.start()
        for move in sends:
            move.wait()

    for move in sent:
        move.wait()


def flip_of(half):
    sum_of = lax.broadcasted_iota(jnp.int32, (half, half), 0) + lax.broadcasted_iota(jnp.int32, (half, half), 1)
    return jnp.where((sum_of == half) | (sum_of == 0), 1.0, 0.0).astype(jnp.bfloat16)


SPLIT = 4


def unfold_zero(plan, lower, upper, second):
    half, count = plan.cells_y, plan.rows_x
    row = lax.broadcasted_iota(jnp.int32, (count, count), 0)
    col = lax.broadcasted_iota(jnp.int32, (count, count), 1)
    turn = jnp.where(row + col == count, 1.0, 0.0).astype(jnp.bfloat16)
    first = lax.broadcasted_iota(jnp.int32, (count, 2 * half), 0) == 0
    lane0 = lax.broadcasted_iota(jnp.int32, (count, half), 1) == 0
    for t in range(6):
        here, at, there, edge = (
            (upper, t, lower, (6 - SPLIT) * count + t) if t < SPLIT else (lower, t - SPLIT, upper, SPLIT * count + t)
        )
        rows = slice(at * count, (at + 1) * count)
        plus, minus = here[rows, :half], here[rows, half:]
        crossed = jnp.concatenate([jnp.where(lane0, plus, minus), jnp.where(lane0, minus, plus)], 1)
        crossed = mul(turn, crossed.astype(jnp.bfloat16))
        second[t] = jnp.where(first, there[edge : edge + 1, :], crossed)


COUPLINGS = ((0, 3, 4), (3, 1, 5), (4, 5, 2))


def ready_kernel(plan, tensor, table_at, own_part, table):
    _, _, own, _ = rows_of(plan)
    half, count = plan.cells_y, plan.rows_x
    table[...] = table_at[...]
    turned = mul(jnp.concatenate([tensor[t, own, :, half:] for t in range(6)], 0), flip_of(half))
    for t in range(6):
        own_part[t, :, :half] = tensor[t, own, :, :half].astype(jnp.float32)
        own_part[t, :, half:] = turned[t * count : (t + 1) * count, :]


def ahead_kernel(plan, got, table, swapped, mixed, far_part):
    w, n, _, _ = rows_of(plan)
    half, wide = plan.cells_y, plan.wide
    cells_x, length_x, narrow = plan.cells_x, plan.length_x, plan.narrow
    block = 6 * plan.width_x
    lines = []
    for c in range(3):
        for j in range(2 * plan.width_x):
            row = c * 2 * plan.width_x + j
            lines.append(jnp.concatenate(
                [got[pl.ds(m * block + row, wide, stride=narrow * block), :] for m in range(narrow)], 1))
    lines = jnp.concatenate(lines, 0)
    high, low = halves(lines)
    y_high, y_low = table[:half, :], table[half : 2 * half, :]
    x_ahead = table[2 * half : 2 * half + 2 * length_x, : 6 * cells_x]
    waves = mul(high, y_high) + (mul(low, y_high) + mul(high, y_low))
    flip = flip_of(half)
    count = plan.rows_x
    turned_far = mul(swapped[:, half : 2 * half].astype(jnp.bfloat16), flip)
    for t in range(6):
        rows = slice(t * count, (t + 1) * count)
        far_part[t, :, :half] = swapped[rows, :half]
        far_part[t, :, half:] = turned_far[rows, :]
    edge = lax.broadcasted_iota(jnp.int32, (cells_x, half), 1) == 0
    parts = [(waves[g * cells_x : (g + 1) * cells_x, :half], waves[g * cells_x : (g + 1) * cells_x, half:])
             for g in range(6)]

    def stage(g, real, imag):
        (pr, qr), (pi, qi) = real, imag
        plus = jnp.where(edge, pr, pr + qi), jnp.where(edge, pi, pi - qr)
        minus = jnp.where(edge, qr, pr - qi), jnp.where(edge, qi, pi + qr)
        stack = jnp.concatenate([jnp.concatenate([p, m], 1) for p, m in zip(plus, minus)], 0)
        a, b = halves(stack)
        mixed[g] = mul(x_ahead, jnp.concatenate([a, b, a], 0))

    special = jnp.logical_and(w == 0, n == 1)

    @pl.when(special)
    def _():
        none = jnp.zeros((cells_x, half), jnp.float32)
        for g in range(6):
            stage(g, parts[g], (none, none))

    @pl.when(jnp.logical_not(special))
    def _():
        for c in range(3):
            stage(c, parts[2 * c], parts[2 * c + 1])


def back_kernel(plan, mixed, own_part, far_part, table, lower, upper, out, packed, second):
    w, n, _, _ = rows_of(plan)
    lanes, half, wide = plan.width_y, plan.cells_y, plan.wide
    length_x, narrow = plan.length_x, plan.narrow
    block, per_c = 6 * plan.width_x, 2 * plan.cells_x
    y_high, y_low = table[:half, :], table[half : 2 * half, :]
    base = 2 * half
    xb_pair = table[base : base + per_c, half : half + 4 * length_x]
    xb_low = table[base + per_c : base + 2 * per_c, half : half + 2 * length_x]
    step = 16

    def couple(paired):
        for lane in range(0, half, 128):
            for row in range(0, length_x, step):
                left = slice(lane, lane + 128)
                right = slice(half + lane, half + lane + 128)
                cr, sr = slice(row, row + step), slice(length_x + row, length_x + row + step)
                part = own_part if row < plan.rows_x else far_part
                at = slice(row % plan.rows_x, row % plan.rows_x + step)
                if lane == 0:
                    edge = lax.broadcasted_iota(jnp.int32, (step, 128), 1) == 0
                fields = [
                    (mixed[g, cr, left], mixed[g, sr, left], mixed[g, cr, right], mixed[g, sr, right])
                    for g in range(6 if paired else 3)
                ]
                for i in range(3):
                    sums = []
                    for s, lanes_at in ((0, left), (2, right)):
                        real = imag = None
                        for j in range(3):
                            t = COUPLINGS[i][j]
                            ka = part[t, at, lanes_at]
                            if paired:
                                straight = (row < plan.rows_x) == (t < SPLIT)
                                base_at = (t if t < SPLIT else t - SPLIT) * plan.rows_x + row % plan.rows_x
                                source = upper if t < SPLIT else lower
                                kb = source[base_at : base_at + step, lanes_at] if straight else second[t, at, lanes_at]
                                a, b = fields[2 * j], fields[2 * j + 1]
                                re = ka * a[s] - kb * b[s + 1]
                                im = ka * a[s + 1] + kb * b[s]
                            else:
                                re, im = ka * fields[j][s], ka * fields[j][s + 1]
                            real = re if real is None else real + re
                            imag = im if imag is None else imag + im
                        sums.append((real, imag))
                    (pr, pi), (mr, mi) = sums
                    even_re, even_im, odd_re, odd_im = pr + mr, pi + mi, mi - pi, pr - mr
                    if lane == 0:
                        even_re, even_im = jnp.where(edge, pr, even_re), jnp.where(edge, pi, even_im)
                        odd_re, odd_im = jnp.where(edge, mr, odd_re), jnp.where(edge, mi, odd_im)
                    for value, base_at, lanes_at in (
                        (even_re, 0, left), (even_im, length_x, left),
                        (odd_re, 0, right), (odd_im, length_x, right),
                    ):
                        a, b = halves(value)
                        high_at, low_at = base_at + row, 2 * length_x + base_at + row
                        packed[i, high_at : high_at + step, lanes_at] = a
                        packed[i, low_at : low_at + step, lanes_at] = b

    special = jnp.logical_and(w == 0, n == 1)

    @pl.when(special)
    def _():
        unfold_zero(plan, lower, upper, second)
        couple(True)

    pl.when(jnp.logical_not(special))(lambda: couple(False))
    back = []
    for i in range(3):
        back.append(mul(xb_pair, packed[i]) + mul(xb_low, packed[i, : 2 * length_x, :]))
    high, low = halves(jnp.concatenate(back, 0))
    result = mul_back(high, y_high) + (mul_back(low, y_high) + mul_back(high, y_low))
    for c in range(3):
        for j in range(2 * plan.width_x):
            row = c * 2 * plan.width_x + j
            for m in range(narrow):
                out[pl.ds(m * block + row, wide, stride=narrow * block), :] = result[
                    row * wide : (row + 1) * wide, m * lanes : (m + 1) * lanes]


def local_kernel(plan, species, turned, side, near, next_, material, saturation, anisotropy,
                 damping, applied, table, out, damp, woven):
    w, n = lax.axis_index("wide"), lax.axis_index("narrow")
    cells, layers = plan.layers * plan.width_x, plan.layers
    row = lax.broadcasted_iota(jnp.int32, (cells, plan.width_y), 0)
    col = lax.broadcasted_iota(jnp.int32, (cells, plan.width_y), 1)
    first, last = col == 0, col == plan.width_y - 1
    even = row % 2 == 0
    ahead = jnp.where(n == 0, 1.0, 0.0)
    sat = pick(material[...], saturation, species)
    anis = pick(material[...], anisotropy, species)
    damp[...] = pick(material[...], damping, species)
    square = lax.broadcasted_iota(jnp.int32, (cells, cells), 0) == lax.broadcasted_iota(
        jnp.int32, (cells, cells), 1)
    sums, present, own = [], jnp.zeros((cells, plan.width_y), jnp.float32), []
    for c in range(3):
        d = turned[c * cells : (c + 1) * cells, :]
        line = jnp.broadcast_to(side[0:1, c * cells : (c + 1) * cells], (cells, cells))
        s = jnp.sum(jnp.where(square, line, 0.0), axis=1, keepdims=True)
        a, b = near[c * layers : (c + 1) * layers, :], next_[c * layers : (c + 1) * layers, :]
        woven[pl.ds(0, layers, stride=2), :] = jnp.where(w % 2 == 0, b, a)
        woven[pl.ds(1, layers, stride=2), :] = jnp.where(w % 2 == 0, a, b)
        beside = (
            jnp.where(row >= 2, pltpu.roll(d, 2, 0), 0.0),
            jnp.where(row < cells - 2, pltpu.roll(d, cells - 2, 0), 0.0),
            woven[...],
            jnp.where(even, pltpu.roll(d, cells - 1, 0), pltpu.roll(d, 1, 0)),
            pltpu.roll(jnp.where(first, s * ahead, d), plan.width_y - 1, 1),
            pltpu.roll(jnp.where(last, s * (1.0 - ahead), d), 1, 1),
        )
        total = beside[0]
        present = present + beside[0] * beside[0]
        for v in beside[1:]:
            total = total + v
            present = present + v * v
        sums.append(total)
        own.append(d)
    for c in range(3):
        field = exchange_coef * (sums[c] - present * own[c]) / sat + applied[c]
        if c == 2:
            field = field + 2.0 * anis / sat * own[2]
        out[c * cells : (c + 1) * cells, :] = field


def last_kernel(plan, got, table, base, turned, damping, rate_at, demag_at, rate, demag, sems):
    cells = plan.layers * plan.width_x
    group, lanes, block = plan.devices, plan.width_y, 2 * plan.width_x
    lines = jnp.concatenate([
        jnp.concatenate([got[pl.ds(c * block + j, group, stride=3 * block), :] for c in range(3)], 1)
        for j in range(block)
    ], 0)
    high, low = halves(lines)
    result = mul(table[...], jnp.concatenate([high, low, high], 0))
    for c in range(3):
        demag[c * cells : (c + 1) * cells, :] = result[:, c * lanes : (c + 1) * lanes]
    moves = [pltpu.make_async_copy(demag, demag_at, sems.at[3])]
    moves[0].start()
    damp = damping[...]
    d = [turned[c * cells : (c + 1) * cells, :] for c in range(3)]
    f = [demag[c * cells : (c + 1) * cells, :] + base[c * cells : (c + 1) * cells, :] for c in range(3)]

    def turn(u, v):
        return [u[1] * v[2] - u[2] * v[1], u[2] * v[0] - u[0] * v[2], u[0] * v[1] - u[1] * v[0]]

    torque = turn(d, f)
    again = turn(d, torque)
    scale = -1.0 / (1.0 + damp * damp)
    for c in range(3):
        rows = pl.ds(c * cells, cells)
        rate[rows, :] = (torque[c] + damp * again[c]) * scale
        moves.append(pltpu.make_async_copy(rate.at[rows], rate_at.at[rows], sems.at[c]))
        moves[-1].start()
    for move in moves:
        move.wait()


LIMITS = (67043328, 8 << 20, 8 << 20, 4 << 20, 8 << 20)
VMEM = pl.BlockSpec(memory_space=pltpu.VMEM)
SMEM = pl.BlockSpec(memory_space=pltpu.SMEM)
HBM = pl.BlockSpec(memory_space=pltpu.HBM)


def plane_shards(plan, spin, region, material, saturation, anisotropy, damping, applied, demag_spectrum):
    f32, bf16 = jnp.float32, jnp.bfloat16
    cells, lanes = plan.layers * plan.width_x, plan.width_y
    count, length_y, length_x = plan.devices * 6 * plan.width_x, plan.length_y, plan.length_x
    species = saturation.shape[0]
    shape = jax.ShapeDtypeStruct
    spin2 = spin.reshape(3 * cells, lanes)
    region2, material2 = region.reshape(cells, lanes), material.reshape(cells, lanes)
    ahead_z, back_z = plan.thickness_tables()
    ahead_y, ahead_x, back_x = plan.lateral_tables()
    az, bz, ay = (split_table(t) for t in (ahead_z, back_z, ahead_y))
    ax, bx = split_table(ahead_x), split_table(back_x)
    x_ahead = np.concatenate([ax[0], ax[0], ax[1]], 1)
    xb_pair = np.concatenate([bx[0], bx[0]], 1)

    def call(body, out_shape, in_specs, out_specs, scratch, flops, limit=24 << 20):
        return pl.pallas_call(
            body, out_shape=out_shape, in_specs=in_specs, out_specs=out_specs, scratch_shapes=scratch,
            compiler_params=pltpu.CompilerParams(vmem_limit_bytes=limit),
            cost_estimate=pl.CostEstimate(flops=flops, bytes_accessed=1 << 20, transcendentals=0),
        )

    rows6 = 6 * plan.rows_x
    table_in = jnp.asarray(np.concatenate([az[0], az[0], az[1]], 1))
    table_out = jnp.asarray(np.concatenate([bz[0], bz[0], bz[1]], 1))
    outs = ((count, lanes), (3 * plan.layers, lanes), (3 * plan.layers, lanes), (rows6, length_y),
            ((6 - SPLIT) * plan.rows_x + 8, length_y), (SPLIT * plan.rows_x + 8, length_y), (3 * cells, lanes),
            (8, 3 * cells))
    outs = tuple(shape(o, f32) for o in outs)
    half = plan.cells_y
    small = np.zeros((2 * length_x, 2 * half), ax[0].dtype)
    small[:, : 6 * plan.cells_x] = x_ahead
    small[: 2 * plan.cells_x, half : half + 4 * length_x] = xb_pair
    small[2 * plan.cells_x : 4 * plan.cells_x, half : half + 2 * length_x] = bx[1]
    table = jnp.asarray(np.concatenate([ay[0], ay[1], small], 0))

    out, near, next_, swap, lower, upper, turned, side = call(
        partial(first_kernel, plan, species),
        outs, [HBM] * 6, (HBM,) * len(outs),
        [pltpu.VMEM((3 * cells, lanes), f32), pltpu.VMEM((cells, lanes), jnp.int32),
         pltpu.VMEM((cells, lanes), jnp.int32), pltpu.SMEM((species,), f32),
         pltpu.VMEM(table_in.shape, bf16),
         pltpu.VMEM((6, plan.rows_x, length_y), bf16), pltpu.VMEM((6, plan.rows_x, length_y), bf16)]
        + [pltpu.VMEM(o.shape, o.dtype) for o in outs]
        + [pltpu.SemaphoreType.DMA((10,)), pltpu.SemaphoreType.DMA((6,))],
        1 << 28, LIMITS[0],
    )(spin2, region2, material2, saturation, table_in, demag_spectrum)

    both = ("wide", "narrow")
    swapped = lax.ppermute(swap, "narrow", [(0, 1), (1, 0)])
    blocks = (plan.devices, 3, 2 * plan.width_x, lanes)
    got = lax.all_to_all(out.reshape(blocks), both, 0, 0, tiled=True).reshape(count, lanes)
    lower = lax.ppermute(lower, both, [(plan.holder, plan.special)])
    upper = lax.ppermute(upper, both, [(plan.holder + 1, plan.special)])
    side = lax.ppermute(side, "narrow", [(0, 1), (1, 0)])
    pairs = [(i ^ 1, i) for i in range(plan.wide)]
    near = lax.ppermute(near, "wide", pairs)
    pairs = [(i, j) for i in range(1, plan.wide - 1, 2) for i, j in ((i, i + 1), (i + 1, i))]
    next_ = lax.ppermute(next_, "wide", pairs)

    half_shape = shape((6, plan.rows_x, length_y), f32)
    own_part, table = call(
        partial(ready_kernel, plan), (half_shape, shape(table.shape, bf16)), [VMEM] * 2, (VMEM, VMEM), [],
        1 << 26, LIMITS[1],
    )(demag_spectrum, table)
    mixed, far_part = call(
        partial(ahead_kernel, plan), (shape((6, 2 * length_x, length_y), f32), half_shape),
        [VMEM] * 3, (VMEM, VMEM), [], 1 << 29, LIMITS[2],
    )(got, table, swapped)
    sent = call(
        partial(back_kernel, plan),
        shape((count, lanes), f32),
        [VMEM] * 6, VMEM,
        [pltpu.VMEM((3, 4 * length_x, length_y), bf16), pltpu.VMEM((6, plan.rows_x, length_y), f32)],
        1 << 29, LIMITS[2],
    )(mixed, own_part, far_part, table, lower, upper)

    back = lax.all_to_all(sent.reshape(blocks), both, 0, 0, tiled=True).reshape(count, lanes)
    base, damp = call(
        partial(local_kernel, plan, species), (shape((3 * cells, lanes), f32), shape((cells, lanes), f32)),
        [VMEM] * 5 + [SMEM] * 4 + [VMEM], (VMEM, VMEM), [pltpu.VMEM((cells, lanes), f32)], 1 << 22, LIMITS[3],
    )(turned, side, near, next_, material2, saturation, anisotropy, damping, applied, table_out)

    rate, demag = call(
        partial(last_kernel, plan),
        (shape((3 * cells, lanes), f32), shape((3 * cells, lanes), f32)),
        [VMEM] * 5, (HBM, HBM),
        [pltpu.VMEM((3 * cells, lanes), f32), pltpu.VMEM((3 * cells, lanes), f32), pltpu.SemaphoreType.DMA((4,))],
        1 << 28, LIMITS[4],
    )(back, table_out, base, turned, damp)
    return rate.reshape(spin.shape), demag.reshape(spin.shape)


def shards(*args):
    spin, demag_spectrum = args[0], args[-1]
    _, layers, width_x, width_y = spin.shape
    _, planes, rows_x, length_y = demag_spectrum.shape
    plan = Plan(lax.axis_size("wide"), lax.axis_size("narrow"), layers, width_x, width_y,
                planes, rows_x, length_y)
    if plan.fits():
        return plane_shards(plan, *args)
    return general_shards(*args)


def solution(mesh):
    placed = (
        P(None, None, "wide", "narrow"),
        P(None, "wide", "narrow"),
        P(None, "wide", "narrow"),
        P(),
        P(),
        P(),
        P(),
        P(None, "wide", "narrow", None),
    )
    return jax.shard_map(
        shards,
        mesh=mesh,
        in_specs=placed,
        out_specs=(P(None, None, "wide", "narrow"), P(None, None, "wide", "narrow")),
        check_vma=False,
    )
```

```python
from functools import partial
import math

import jax
import jax.numpy as jnp
import numpy as np
from jax import lax
from jax.experimental import pallas as pl
from jax.experimental.pallas import tpu as pltpu
from jax.sharding import PartitionSpec as P


exchange_coef = 0.3
highest = lax.Precision.HIGHEST


def extended(x, sides, width):
    for axis, dim in sides:
        peers, length = (lax.axis_size(axis), x.shape[dim])
        up = [(i, (i + 1) % peers) for i in range(peers - 1)]
        down = [(j, i) for i, j in up]
        last = lax.slice_in_dim(x, length - width, length, axis=dim)
        leading = lax.slice_in_dim(x, 0, width, axis=dim)
        before = lax.ppermute(last, axis, up)
        after = lax.ppermute(leading, axis, down)
        x = jnp.concatenate([before, x, after], axis=dim)
    return x


def phase_table(rows_count, cols_count, length, sign):
    left_index = lax.broadcasted_iota(jnp.int32, (rows_count, cols_count), 0)
    right_index = lax.broadcasted_iota(jnp.int32, (rows_count, cols_count), 1)
    angle = (left_index * right_index % length).astype(jnp.float32) * (2.0 * math.pi / length)
    return (jnp.cos(angle), sign * jnp.sin(angle))


def contract(pattern, phases, values):
    phase_re, phase_im = phases
    value_re, value_im = values
    product = partial(jnp.einsum, pattern, precision=highest)
    if value_im is None:
        return (product(phase_re, value_re), product(phase_im, value_re))
    return (
        product(phase_re, value_re) - product(phase_im, value_im),
        product(phase_re, value_im) + product(phase_im, value_re),
    )


def factors(half_size, at_end):
    if at_end:
        inner_size = math.gcd(half_size, 128)
    else:
        inner_size = max(
            (
                divisor
                for divisor in range(1, half_size + 1)
                if half_size % divisor == 0 and divisor * divisor <= 2 * half_size
            )
        )
    return (inner_size, 2 * half_size // inner_size)


def forward(values, at_end, natural):
    value_re, value_im = values
    extent = value_re.shape
    half_size = extent[1]
    length = 2 * half_size
    inner_size, outer_size = factors(half_size, at_end)
    tail_index = "" if at_end else "b"
    blocked = (extent[0], outer_size // 2, inner_size) + extent[2:]
    value_re = value_re.reshape(blocked)
    value_im = None if value_im is None else value_im.reshape(blocked)
    phases = phase_table(outer_size, outer_size // 2, outer_size, -1.0)
    work_re, work_im = contract(
        "kn,anp" + tail_index + "->akp" + tail_index, phases, (value_re, value_im)
    )
    twist_re, twist_im = phase_table(outer_size, inner_size, length, -1.0)
    if not at_end:
        twist_re, twist_im = (twist_re[:, :, None], twist_im[:, :, None])
    work_re, work_im = (
        work_re * twist_re - work_im * twist_im,
        work_re * twist_im + work_im * twist_re,
    )
    target = "ajk" if natural else "akj"
    phases = phase_table(inner_size, inner_size, inner_size, -1.0)
    out_re, out_im = contract(
        "jp,akp" + tail_index + "->" + target + tail_index, phases, (work_re, work_im)
    )
    merged = (extent[0], length) + extent[2:]
    return (out_re.reshape(merged), out_im.reshape(merged))


def inverse(values, at_end, natural, real_only):
    value_re, value_im = values
    extent = value_re.shape
    length = extent[1]
    half_size = length // 2
    inner_size, outer_size = factors(half_size, at_end)
    tail_index = "" if at_end else "b"
    if natural:
        blocked = (extent[0], inner_size, outer_size) + extent[2:]
        source = "ajk"
    else:
        blocked = (extent[0], outer_size, inner_size) + extent[2:]
        source = "akj"
    phases = phase_table(inner_size, inner_size, inner_size, 1.0)
    work_re, work_im = contract(
        "pj," + source + tail_index + "->akp" + tail_index,
        phases,
        (value_re.reshape(blocked), value_im.reshape(blocked)),
    )
    twist_re, twist_im = phase_table(outer_size, inner_size, length, 1.0)
    if not at_end:
        twist_re, twist_im = (twist_re[:, :, None], twist_im[:, :, None])
    work_re, work_im = (
        work_re * twist_re - work_im * twist_im,
        work_re * twist_im + work_im * twist_re,
    )
    phases = phase_table(outer_size // 2, outer_size, outer_size, 1.0)
    pattern = "nk,akp" + tail_index + "->anp" + tail_index
    scale = 1.0 / length
    merged = (extent[0], half_size) + extent[2:]
    if real_only:
        product = partial(jnp.einsum, pattern, precision=highest)
        result = product(phases[0], work_re) - product(phases[1], work_im)
        return result.reshape(merged) * scale
    out_re, out_im = contract(pattern, phases, (work_re, work_im))
    return (out_re.reshape(merged) * scale, out_im.reshape(merged) * scale)


def along_x(pieces):
    piece_re, piece_im = pieces
    members, planes, cells_x, cells_y = piece_re.shape
    extent = (members * planes, cells_x, cells_y)
    out_re, out_im = forward((piece_re.reshape(extent), piece_im.reshape(extent)), False, True)
    merged = (members, planes, 2 * cells_x, cells_y)
    return (out_re.reshape(merged), out_im.reshape(merged))


def along_y(pieces):
    piece_re, piece_im = pieces
    members, planes, rows_x, cells_y = piece_re.shape
    extent = (members * planes * rows_x, cells_y)
    out_re, out_im = forward((piece_re.reshape(extent), piece_im.reshape(extent)), True, False)
    merged = (members, planes, rows_x, 2 * cells_y)
    return (out_re.reshape(merged), out_im.reshape(merged))


def back_to_bricks(field_re, field_im):
    members, planes, rows_x, length_y = field_re.shape
    flattened = (members * planes * rows_x, length_y)
    grid_re, grid_im = inverse(
        (field_re.reshape(flattened), field_im.reshape(flattened)), True, False, False
    )
    merged = (members, planes, rows_x, length_y // 2)
    piece_re = lax.all_to_all(
        grid_re.reshape(merged), "narrow", split_axis=3, concat_axis=2, tiled=True
    )
    piece_im = lax.all_to_all(
        grid_im.reshape(merged), "narrow", split_axis=3, concat_axis=2, tiled=True
    )
    members, planes, length_x, cells_y = piece_re.shape
    extent = (members * planes, length_x, cells_y)
    out_re, out_im = inverse(
        (piece_re.reshape(extent), piece_im.reshape(extent)), False, True, False
    )
    invert_merged = (members, planes, length_x // 2, cells_y)
    columns = (out_re.reshape(invert_merged), out_im.reshape(invert_merged))
    piece_re, piece_im = lax.all_to_all(columns, "wide", split_axis=2, concat_axis=1, tiled=True)
    members, planes, cells_x, cells_y = piece_re.shape
    extent = (members, planes, cells_x * cells_y)
    result = inverse((piece_re.reshape(extent), piece_im.reshape(extent)), False, True, True)
    merged = (members, planes // 2, cells_x, cells_y)
    return result.reshape(merged)


def couple(kernel, values, picks):
    return -(
        kernel[picks[0]] * values[0] + kernel[picks[1]] * values[1] + kernel[picks[2]] * values[2]
    )


def cross(left, right):
    return jnp.stack(
        [
            left[1] * right[2] - left[2] * right[1],
            left[2] * right[0] - left[0] * right[2],
            left[0] * right[1] - left[1] * right[0],
        ]
    )


def general_shards(spin, region, material, saturation, anisotropy, damping, applied, demag_spectrum):
    magnet = region.astype(jnp.float32)
    direction = spin * magnet[None]
    species = saturation.shape[0]
    chosen = (
        material[None] == lax.broadcasted_iota(jnp.int32, (species,) + material.shape, 0)
    ).astype(jnp.float32)

    def lookup(entries):
        return jnp.sum(chosen * entries[:, None, None, None], axis=0)

    sat_cell = lookup(saturation)
    anis_cell = lookup(anisotropy)
    damp_cell = lookup(damping)
    moment = direction * sat_cell[None]
    components, layers, width_x, width_y = spin.shape
    flattened = moment.reshape(components, layers, width_x * width_y)
    spec_re, spec_im = forward((flattened, None), False, True)
    stacked = (components, 2 * layers, width_x, width_y)
    spectra = along_x(
        (
            lax.all_to_all(
                spec_re.reshape(stacked), "wide", split_axis=1, concat_axis=2, tiled=True
            ),
            lax.all_to_all(
                spec_im.reshape(stacked), "wide", split_axis=1, concat_axis=2, tiled=True
            ),
        )
    )
    spec_re, spec_im = along_y(
        lax.all_to_all(spectra, "narrow", split_axis=2, concat_axis=3, tiled=True)
    )
    parts, planes, rows_x, length_y = demag_spectrum.shape
    inner_size, outer_size = factors(length_y // 2, True)
    kernel = demag_spectrum.reshape(parts, planes, rows_x, inner_size, outer_size)
    kernel = (
        kernel.transpose(0, 1, 2, 4, 3).reshape(parts, planes, rows_x, length_y).astype(jnp.float32)
    )
    couplings = ((0, 3, 4), (3, 1, 5), (4, 5, 2))
    field_re = [couple(kernel, spec_re, picks) for picks in couplings]
    field_im = [couple(kernel, spec_im, picks) for picks in couplings]
    demag = back_to_bricks(jnp.stack(field_re), jnp.stack(field_im))
    framed = extended(direction, (("wide", 2), ("narrow", 3)), 1)
    framed = jnp.pad(framed, ((0, 0), (1, 1), (0, 0), (0, 0)))
    weight = jnp.sum(framed * framed, axis=0)
    neighbours = (
        framed[:, 2:, 1:-1, 1:-1]
        + framed[:, :-2, 1:-1, 1:-1]
        + framed[:, 1:-1, 2:, 1:-1]
        + framed[:, 1:-1, :-2, 1:-1]
        + framed[:, 1:-1, 1:-1, 2:]
        + framed[:, 1:-1, 1:-1, :-2]
    )
    present = (
        weight[2:, 1:-1, 1:-1]
        + weight[:-2, 1:-1, 1:-1]
        + weight[1:-1, 2:, 1:-1]
        + weight[1:-1, :-2, 1:-1]
        + weight[1:-1, 1:-1, 2:]
        + weight[1:-1, 1:-1, :-2]
    )
    laplace = neighbours - present[None] * direction
    zeros = jnp.zeros_like(sat_cell)
    uniaxial = jnp.stack([zeros, zeros, 2.0 * anis_cell / sat_cell * direction[2]])
    field = (
        exchange_coef * laplace / sat_cell[None] + demag + applied[:, None, None, None] + uniaxial
    )
    torque = cross(direction, field)
    rate = (
        -(torque + damp_cell[None] * cross(direction, torque)) / (1.0 + damp_cell * damp_cell)[None]
    )
    return (rate, demag)


def split_table(table):
    high = jnp.asarray(np.asarray(table, np.float32)).astype(jnp.bfloat16)
    high64 = np.asarray(np.asarray(table, np.float32).astype(high.dtype), np.float64)
    low = (table - high64).astype(np.float32).astype(high.dtype)
    return np.asarray(high64.astype(high.dtype)), low


class Plan:
    def __init__(self, wide, narrow, layers, width_x, width_y, planes, rows_x, length_y):
        self.wide, self.narrow = wide, narrow
        self.layers, self.width_x, self.width_y = layers, width_x, width_y
        self.planes, self.rows_x = planes, rows_x
        self.length_z, self.length_x, self.length_y = planes * wide, rows_x * narrow, length_y
        self.cells_x, self.cells_y = width_x * wide, width_y * narrow
        self.devices = wide * narrow
        self.special, self.holder = 1, self.narrow * (wide // 2)

    def fits(self):
        return (
            self.narrow == 2
            and self.planes == 4
            and self.wide % 16 == 0
            and self.devices * 2 == self.length_z
            and self.length_z == 2 * self.layers
            and self.length_x == 2 * self.cells_x
            and self.length_y == 2 * self.cells_y
            and self.width_x == 2
            and self.width_y % 128 == 0
            and self.rows_x % 16 == 0
            and 6 * self.cells_x <= self.cells_y
            and (self.layers * self.width_x) % 8 == 0
            and 6 * self.rows_x == 3 * self.layers * self.width_x
        )

    def wave(self):
        w, n = np.divmod(np.arange(self.devices), self.narrow)
        return self.planes * w + np.where(w < self.wide // 2, 1 - n, 1 + n)

    def thickness_tables(self):
        wave = self.wave()
        z = np.arange(self.layers)
        angle = 2.0 * np.pi * ((wave[:, None] * z[None]) % self.length_z) / self.length_z
        ahead = np.stack([np.cos(angle), -np.sin(angle)], 1)
        back = np.stack([2.0 * np.cos(angle), -2.0 * np.sin(angle)], 1)
        middle = 1.0 - 2.0 * (z % 2)
        ahead[self.special, 1] = middle
        back[self.special, 0] = 1.0
        back[self.special, 1] = middle
        back *= -1.0 / (self.length_z * self.length_x * self.length_y)
        n = np.arange(self.devices) % self.narrow
        x = np.arange(self.width_x)
        sign = 1.0 - 2.0 * ((n[:, None] * x[None]) % 2)
        unit_x = np.eye(self.width_x)
        ahead = np.einsum("drz,dx,xv->rxdzv", ahead, sign, unit_x)
        back = np.einsum("drz,dx,xv->zvrxd", back, sign, unit_x)
        count = self.devices * 6 * self.width_x
        cells = 3 * self.layers * self.width_x
        return ahead.reshape(count // 3, cells // 3), back.reshape(cells // 3, count // 3)

    def lateral_tables(self):
        half = self.cells_y
        y, k = np.arange(half), np.arange(half)
        angle = 2.0 * np.pi * ((y[:, None] * k[None]) % self.length_y) / self.length_y
        cosine, sine = np.cos(angle), np.sin(angle)
        sine[:, 0] = 1.0 - 2.0 * (y % 2)
        ahead_y = np.concatenate([cosine, sine], 1)
        x = (np.arange(self.wide)[None] * self.width_x + np.arange(self.width_x)[:, None]).reshape(-1)
        kx = np.arange(self.length_x)
        angle = 2.0 * np.pi * ((kx[:, None] * x[None]) % self.length_x) / self.length_x
        cosine, sine = np.cos(angle), np.sin(angle)
        ahead_x = np.block([[cosine, sine], [-sine, cosine]])
        back_x = np.block([[cosine.T, -sine.T], [sine.T, cosine.T]])
        return ahead_y, ahead_x, back_x


def halves(value):
    high = value.astype(jnp.bfloat16)
    return high, (value - high.astype(jnp.float32)).astype(jnp.bfloat16)


def mul(left, right):
    return jnp.dot(left, right, preferred_element_type=jnp.float32)


def mul_back(left, right):
    return lax.dot_general(left, right, (((1,), (1,)), ((), ())), preferred_element_type=jnp.float32)


def pick(material, entries, species):
    value = jnp.zeros(material.shape, jnp.float32)
    for s in range(species):
        value = jnp.where(material == s, entries[s], value)
    return value


def rows_of(plan):
    w, n = lax.axis_index("wide"), lax.axis_index("narrow")
    low = w >= plan.wide // 2
    own = jnp.where(low, 1 + n, 1 - n)
    other = jnp.where(low, 2 - n, n)
    return w, n, own, other


def first_kernel(plan, species, spin_at, region_at, material_at, saturation_at, table_at, tensor,
                 out_at, swap_at, lower_at, upper_at,
                 spin, region, material, saturation, table, held, held0,
                 out, swap, lower, upper, sems, done):
    w, _, _, other = rows_of(plan)
    count = plan.rows_x
    moves = [
        pltpu.make_async_copy(source, target, sems.at[k])
        for k, (source, target) in enumerate((
            (saturation_at, saturation), (material_at, material), (region_at, region), (spin_at, spin),
            (table_at, table), (tensor.at[:, other], held),
        ))
    ]
    for move in moves:
        move.start()
    fetch0 = pltpu.make_async_copy(tensor.at[:, 0], held0, sems.at[7])

    @pl.when(w == plan.wide // 2)
    def _():
        fetch0.start()

    sent = []

    def send(source, target):
        move = pltpu.make_async_copy(source, target, done.at[len(sent)])
        move.start()
        sent.append(move)

    for move in moves[:4]:
        move.wait()
    cells = plan.layers * plan.width_x
    magnet = region[...].astype(jnp.float32)
    sat = pick(material[...], saturation, species)
    high, low = [], []
    for c in range(3):
        direction = spin[c * cells : (c + 1) * cells, :] * magnet
        a, b = halves(direction * sat)
        high.append(a)
        low.append(b)
    high, low = jnp.concatenate(high, 1), jnp.concatenate(low, 1)
    moves[5].wait()
    for t in range(6):
        rows = slice(t * count, (t + 1) * count)
        swap[rows, : plan.length_y] = held[t].astype(jnp.float32)
    send(swap, swap_at)
    moves[4].wait()
    result = mul(table[...], jnp.concatenate([high, low, high], 0))
    group, lanes = plan.devices, plan.width_y
    for c in range(3):
        for j in range(2 * plan.width_x):
            out[pl.ds(c * 2 * plan.width_x + j, group, stride=6 * plan.width_x), :] = result[
                j * group : (j + 1) * group, c * lanes : (c + 1) * lanes]
    send(out, out_at)

    @pl.when(w == plan.wide // 2)
    def _():
        fetch0.wait()
        cut, half = SPLIT * count, plan.cells_y
        flip = flip_of(half)
        minus = mul(jnp.concatenate([held0[t, :, half:] for t in range(6)], 0), flip)
        lower[(6 - SPLIT) * count :, :] = jnp.zeros((8, plan.length_y), jnp.float32)
        upper[cut:, :] = jnp.zeros((8, plan.length_y), jnp.float32)
        for t in range(6):
            plus, rest = held0[t, :, :half].astype(jnp.float32), minus[t * count : (t + 1) * count, :]
            if t < SPLIT:
                here, there, at, edge = upper, lower, t * count, (6 - SPLIT) * count + t
            else:
                here, there, at, edge = lower, upper, (t - SPLIT) * count, cut + t
            here[at : at + count, :half] = plus
            here[at : at + count, half:] = rest
            there[edge : edge + 1, :half] = plus[0:1, :]
            there[edge : edge + 1, half:] = rest[0:1, :]
        sends = [pltpu.make_async_copy(lower, lower_at, sems.at[8]), pltpu.make_async_copy(upper, upper_at, sems.at[9])]
        for move in sends:
            move.start()
        for move in sends:
            move.wait()

    for move in sent:
        move.wait()


def halo_kernel(plan, spin, region, turned, near, next_, side):
    w, n = lax.axis_index("wide"), lax.axis_index("narrow")
    cells = plan.layers * plan.width_x
    magnet = region[...].astype(jnp.float32)
    for c in range(3):
        turned[c * cells : (c + 1) * cells, :] = spin[c * cells : (c + 1) * cells, :] * magnet
    layers3 = 3 * plan.layers
    up, down = turned[pl.ds(1, layers3, stride=2), :], turned[pl.ds(0, layers3, stride=2), :]
    near[...] = jnp.where(w % 2 == 0, up, down)
    next_[...] = jnp.where(w % 2 == 0, down, up)
    column = lax.broadcasted_iota(jnp.int32, (8, plan.width_y), 1)
    chosen = jnp.where(column == jnp.where(n == 0, plan.width_y - 1, 0), 1.0, 0.0).astype(jnp.bfloat16)
    high = turned[...].astype(jnp.bfloat16)
    rest = turned[...] - high.astype(jnp.float32)
    middle, low = halves(rest)
    side[...] = mul_back(chosen, high) + mul_back(chosen, middle) + mul_back(chosen, low)


def flip_of(half):
    sum_of = lax.broadcasted_iota(jnp.int32, (half, half), 0) + lax.broadcasted_iota(jnp.int32, (half, half), 1)
    return jnp.where((sum_of == half) | (sum_of == 0), 1.0, 0.0).astype(jnp.bfloat16)


SPLIT = 4


def unfold_zero(plan, lower, upper, second):
    half, count = plan.cells_y, plan.rows_x
    row = lax.broadcasted_iota(jnp.int32, (count, count), 0)
    col = lax.broadcasted_iota(jnp.int32, (count, count), 1)
    turn = jnp.where(row + col == count, 1.0, 0.0).astype(jnp.bfloat16)
    first = lax.broadcasted_iota(jnp.int32, (count, 2 * half), 0) == 0
    lane0 = lax.broadcasted_iota(jnp.int32, (count, half), 1) == 0
    for t in range(6):
        here, at, there, edge = (
            (upper, t, lower, (6 - SPLIT) * count + t) if t < SPLIT else (lower, t - SPLIT, upper, SPLIT * count + t)
        )
        rows = slice(at * count, (at + 1) * count)
        plus, minus = here[rows, :half], here[rows, half:]
        crossed = jnp.concatenate([jnp.where(lane0, plus, minus), jnp.where(lane0, minus, plus)], 1)
        crossed = mul(turn, crossed.astype(jnp.bfloat16))
        second[t] = jnp.where(first, there[edge : edge + 1, :], crossed)


COUPLINGS = ((0, 3, 4), (3, 1, 5), (4, 5, 2))


def ready_kernel(plan, tensor, table_at, own_part, table):
    _, _, own, _ = rows_of(plan)
    half, count = plan.cells_y, plan.rows_x
    table[...] = table_at[...]
    turned = mul(jnp.concatenate([tensor[t, own, :, half:] for t in range(6)], 0), flip_of(half))
    for t in range(6):
        own_part[t, :, :half] = tensor[t, own, :, :half].astype(jnp.float32)
        own_part[t, :, half:] = turned[t * count : (t + 1) * count, :]


def ahead_kernel(plan, got, table, swapped, mixed, far_part):
    w, n, _, _ = rows_of(plan)
    half, wide = plan.cells_y, plan.wide
    cells_x, length_x, narrow = plan.cells_x, plan.length_x, plan.narrow
    block = 6 * plan.width_x
    lines = []
    for c in range(3):
        for j in range(2 * plan.width_x):
            row = c * 2 * plan.width_x + j
            lines.append(jnp.concatenate(
                [got[pl.ds(m * block + row, wide, stride=narrow * block), :] for m in range(narrow)], 1))
    lines = jnp.concatenate(lines, 0)
    high, low = halves(lines)
    y_high, y_low = table[:half, :], table[half : 2 * half, :]
    x_ahead = table[2 * half : 2 * half + 2 * length_x, : 6 * cells_x]
    waves = mul(high, y_high) + (mul(low, y_high) + mul(high, y_low))
    flip = flip_of(half)
    count = plan.rows_x
    turned_far = mul(swapped[:, half : 2 * half].astype(jnp.bfloat16), flip)
    for t in range(6):
        rows = slice(t * count, (t + 1) * count)
        far_part[t, :, :half] = swapped[rows, :half]
        far_part[t, :, half:] = turned_far[rows, :]
    edge = lax.broadcasted_iota(jnp.int32, (cells_x, half), 1) == 0
    parts = [(waves[g * cells_x : (g + 1) * cells_x, :half], waves[g * cells_x : (g + 1) * cells_x, half:])
             for g in range(6)]

    def stage(g, real, imag):
        (pr, qr), (pi, qi) = real, imag
        plus = jnp.where(edge, pr, pr + qi), jnp.where(edge, pi, pi - qr)
        minus = jnp.where(edge, qr, pr - qi), jnp.where(edge, qi, pi + qr)
        stack = jnp.concatenate([jnp.concatenate([p, m], 1) for p, m in zip(plus, minus)], 0)
        a, b = halves(stack)
        mixed[g] = mul(x_ahead, jnp.concatenate([a, b, a], 0))

    special = jnp.logical_and(w == 0, n == 1)

    @pl.when(special)
    def _():
        none = jnp.zeros((cells_x, half), jnp.float32)
        for g in range(6):
            stage(g, parts[g], (none, none))

    @pl.when(jnp.logical_not(special))
    def _():
        for c in range(3):
            stage(c, parts[2 * c], parts[2 * c + 1])


def back_kernel(plan, mixed, own_part, far_part, table, lower, upper, out, packed, second):
    w, n, _, _ = rows_of(plan)
    lanes, half, wide = plan.width_y, plan.cells_y, plan.wide
    length_x, narrow = plan.length_x, plan.narrow
    block, per_c = 6 * plan.width_x, 2 * plan.cells_x
    y_high, y_low = table[:half, :], table[half : 2 * half, :]
    base = 2 * half
    xb_pair = table[base : base + per_c, half : half + 4 * length_x]
    xb_low = table[base + per_c : base + 2 * per_c, half : half + 2 * length_x]
    step = 16

    def couple(paired):
        for lane in range(0, half, 128):
            for row in range(0, length_x, step):
                left = slice(lane, lane + 128)
                right = slice(half + lane, half + lane + 128)
                cr, sr = slice(row, row + step), slice(length_x + row, length_x + row + step)
                part = own_part if row < plan.rows_x else far_part
                at = slice(row % plan.rows_x, row % plan.rows_x + step)
                if lane == 0:
                    edge = lax.broadcasted_iota(jnp.int32, (step, 128), 1) == 0
                fields = [
                    (mixed[g, cr, left], mixed[g, sr, left], mixed[g, cr, right], mixed[g, sr, right])
                    for g in range(6 if paired else 3)
                ]
                for i in range(3):
                    sums = []
                    for s, lanes_at in ((0, left), (2, right)):
                        real = imag = None
                        for j in range(3):
                            t = COUPLINGS[i][j]
                            ka = part[t, at, lanes_at]
                            if paired:
                                straight = (row < plan.rows_x) == (t < SPLIT)
                                base_at = (t if t < SPLIT else t - SPLIT) * plan.rows_x + row % plan.rows_x
                                source = upper if t < SPLIT else lower
                                kb = source[base_at : base_at + step, lanes_at] if straight else second[t, at, lanes_at]
                                a, b = fields[2 * j], fields[2 * j + 1]
                                re = ka * a[s] - kb * b[s + 1]
                                im = ka * a[s + 1] + kb * b[s]
                            else:
                                re, im = ka * fields[j][s], ka * fields[j][s + 1]
                            real = re if real is None else real + re
                            imag = im if imag is None else imag + im
                        sums.append((real, imag))
                    (pr, pi), (mr, mi) = sums
                    even_re, even_im, odd_re, odd_im = pr + mr, pi + mi, mi - pi, pr - mr
                    if lane == 0:
                        even_re, even_im = jnp.where(edge, pr, even_re), jnp.where(edge, pi, even_im)
                        odd_re, odd_im = jnp.where(edge, mr, odd_re), jnp.where(edge, mi, odd_im)
                    for value, base_at, lanes_at in (
                        (even_re, 0, left), (even_im, length_x, left),
                        (odd_re, 0, right), (odd_im, length_x, right),
                    ):
                        a, b = halves(value)
                        high_at, low_at = base_at + row, 2 * length_x + base_at + row
                        packed[i, high_at : high_at + step, lanes_at] = a
                        packed[i, low_at : low_at + step, lanes_at] = b

    special = jnp.logical_and(w == 0, n == 1)

    @pl.when(special)
    def _():
        unfold_zero(plan, lower, upper, second)
        couple(True)

    pl.when(jnp.logical_not(special))(lambda: couple(False))
    back = []
    for i in range(3):
        back.append(mul(xb_pair, packed[i]) + mul(xb_low, packed[i, : 2 * length_x, :]))
    high, low = halves(jnp.concatenate(back, 0))
    result = mul_back(high, y_high) + (mul_back(low, y_high) + mul_back(high, y_low))
    for c in range(3):
        for j in range(2 * plan.width_x):
            row = c * 2 * plan.width_x + j
            for m in range(narrow):
                out[pl.ds(m * block + row, wide, stride=narrow * block), :] = result[
                    row * wide : (row + 1) * wide, m * lanes : (m + 1) * lanes]


def local_kernel(plan, species, turned, side, near, next_, material, saturation, anisotropy,
                 damping, applied, table, out, damp, woven):
    w, n = lax.axis_index("wide"), lax.axis_index("narrow")
    cells, layers = plan.layers * plan.width_x, plan.layers
    row = lax.broadcasted_iota(jnp.int32, (cells, plan.width_y), 0)
    col = lax.broadcasted_iota(jnp.int32, (cells, plan.width_y), 1)
    first, last = col == 0, col == plan.width_y - 1
    even = row % 2 == 0
    ahead = jnp.where(n == 0, 1.0, 0.0)
    sat = pick(material[...], saturation, species)
    anis = pick(material[...], anisotropy, species)
    damp[...] = pick(material[...], damping, species)
    square = lax.broadcasted_iota(jnp.int32, (cells, cells), 0) == lax.broadcasted_iota(
        jnp.int32, (cells, cells), 1)
    sums, present, own = [], jnp.zeros((cells, plan.width_y), jnp.float32), []
    for c in range(3):
        d = turned[c * cells : (c + 1) * cells, :]
        line = jnp.broadcast_to(side[0:1, c * cells : (c + 1) * cells], (cells, cells))
        s = jnp.sum(jnp.where(square, line, 0.0), axis=1, keepdims=True)
        a, b = near[c * layers : (c + 1) * layers, :], next_[c * layers : (c + 1) * layers, :]
        woven[pl.ds(0, layers, stride=2), :] = jnp.where(w % 2 == 0, b, a)
        woven[pl.ds(1, layers, stride=2), :] = jnp.where(w % 2 == 0, a, b)
        beside = (
            jnp.where(row >= 2, pltpu.roll(d, 2, 0), 0.0),
            jnp.where(row < cells - 2, pltpu.roll(d, cells - 2, 0), 0.0),
            woven[...],
            jnp.where(even, pltpu.roll(d, cells - 1, 0), pltpu.roll(d, 1, 0)),
            pltpu.roll(jnp.where(first, s * ahead, d), plan.width_y - 1, 1),
            pltpu.roll(jnp.where(last, s * (1.0 - ahead), d), 1, 1),
        )
        total = beside[0]
        present = present + beside[0] * beside[0]
        for v in beside[1:]:
            total = total + v
            present = present + v * v
        sums.append(total)
        own.append(d)
    for c in range(3):
        field = exchange_coef * (sums[c] - present * own[c]) / sat + applied[c]
        if c == 2:
            field = field + 2.0 * anis / sat * own[2]
        out[c * cells : (c + 1) * cells, :] = field


def last_kernel(plan, got, table, base, turned, damping, rate_at, demag_at, rate, demag, sems):
    cells = plan.layers * plan.width_x
    group, lanes, block = plan.devices, plan.width_y, 2 * plan.width_x
    lines = jnp.concatenate([
        jnp.concatenate([got[pl.ds(c * block + j, group, stride=3 * block), :] for c in range(3)], 1)
        for j in range(block)
    ], 0)
    high, low = halves(lines)
    result = mul(table[...], jnp.concatenate([high, low, high], 0))
    for c in range(3):
        demag[c * cells : (c + 1) * cells, :] = result[:, c * lanes : (c + 1) * lanes]
    moves = [pltpu.make_async_copy(demag, demag_at, sems.at[3])]
    moves[0].start()
    damp = damping[...]
    d = [turned[c * cells : (c + 1) * cells, :] for c in range(3)]
    f = [demag[c * cells : (c + 1) * cells, :] + base[c * cells : (c + 1) * cells, :] for c in range(3)]

    def turn(u, v):
        return [u[1] * v[2] - u[2] * v[1], u[2] * v[0] - u[0] * v[2], u[0] * v[1] - u[1] * v[0]]

    torque = turn(d, f)
    again = turn(d, torque)
    scale = -1.0 / (1.0 + damp * damp)
    for c in range(3):
        rows = pl.ds(c * cells, cells)
        rate[rows, :] = (torque[c] + damp * again[c]) * scale
        moves.append(pltpu.make_async_copy(rate.at[rows], rate_at.at[rows], sems.at[c]))
        moves[-1].start()
    for move in moves:
        move.wait()


LIMITS = (67043328, 8 << 20, 8 << 20, 4 << 20, 8 << 20)
VMEM = pl.BlockSpec(memory_space=pltpu.VMEM)
SMEM = pl.BlockSpec(memory_space=pltpu.SMEM)
HBM = pl.BlockSpec(memory_space=pltpu.HBM)


def plane_shards(plan, spin, region, material, saturation, anisotropy, damping, applied, demag_spectrum):
    f32, bf16 = jnp.float32, jnp.bfloat16
    cells, lanes = plan.layers * plan.width_x, plan.width_y
    count, length_y, length_x = plan.devices * 6 * plan.width_x, plan.length_y, plan.length_x
    species = saturation.shape[0]
    shape = jax.ShapeDtypeStruct
    spin2 = spin.reshape(3 * cells, lanes)
    region2, material2 = region.reshape(cells, lanes), material.reshape(cells, lanes)
    ahead_z, back_z = plan.thickness_tables()
    ahead_y, ahead_x, back_x = plan.lateral_tables()
    az, bz, ay = (split_table(t) for t in (ahead_z, back_z, ahead_y))
    ax, bx = split_table(ahead_x), split_table(back_x)
    x_ahead = np.concatenate([ax[0], ax[0], ax[1]], 1)
    xb_pair = np.concatenate([bx[0], bx[0]], 1)

    def call(body, out_shape, in_specs, out_specs, scratch, flops, limit=24 << 20):
        return pl.pallas_call(
            body, out_shape=out_shape, in_specs=in_specs, out_specs=out_specs, scratch_shapes=scratch,
            compiler_params=pltpu.CompilerParams(vmem_limit_bytes=limit),
            cost_estimate=pl.CostEstimate(flops=flops, bytes_accessed=1 << 20, transcendentals=0),
        )

    rows6 = 6 * plan.rows_x
    table_in = jnp.asarray(np.concatenate([az[0], az[0], az[1]], 1))
    table_out = jnp.asarray(np.concatenate([bz[0], bz[0], bz[1]], 1))
    outs = ((count, lanes), (rows6, length_y), ((6 - SPLIT) * plan.rows_x + 8, length_y),
            (SPLIT * plan.rows_x + 8, length_y))
    outs = tuple(shape(o, f32) for o in outs)
    half = plan.cells_y
    small = np.zeros((2 * length_x, 2 * half), ax[0].dtype)
    small[:, : 6 * plan.cells_x] = x_ahead
    small[: 2 * plan.cells_x, half : half + 4 * length_x] = xb_pair
    small[2 * plan.cells_x : 4 * plan.cells_x, half : half + 2 * length_x] = bx[1]
    table = jnp.asarray(np.concatenate([ay[0], ay[1], small], 0))

    out, swap, lower, upper = call(
        partial(first_kernel, plan, species),
        outs, [HBM] * 6, (HBM,) * len(outs),
        [pltpu.VMEM((3 * cells, lanes), f32), pltpu.VMEM((cells, lanes), jnp.int32),
         pltpu.VMEM((cells, lanes), jnp.int32), pltpu.SMEM((species,), f32),
         pltpu.VMEM(table_in.shape, bf16),
         pltpu.VMEM((6, plan.rows_x, length_y), bf16), pltpu.VMEM((6, plan.rows_x, length_y), bf16)]
        + [pltpu.VMEM(o.shape, o.dtype) for o in outs]
        + [pltpu.SemaphoreType.DMA((10,)), pltpu.SemaphoreType.DMA((2,))],
        1 << 28, LIMITS[0],
    )(spin2, region2, material2, saturation, table_in, demag_spectrum)

    both = ("wide", "narrow")
    swapped = lax.ppermute(swap, "narrow", [(0, 1), (1, 0)])
    blocks = (plan.devices, 3, 2 * plan.width_x, lanes)
    got = lax.all_to_all(out.reshape(blocks), both, 0, 0, tiled=True).reshape(count, lanes)
    lower = lax.ppermute(lower, both, [(plan.holder, plan.special)])
    upper = lax.ppermute(upper, both, [(plan.holder + 1, plan.special)])
    edge_shape = shape((3 * plan.layers, lanes), f32)
    turned, near, next_, side = call(
        partial(halo_kernel, plan),
        (shape((3 * cells, lanes), f32), edge_shape, edge_shape, shape((8, 3 * cells), f32)),
        [VMEM] * 2, (VMEM,) * 4, [], 1 << 22, LIMITS[1],
    )(spin2, region2)
    side = lax.ppermute(side, "narrow", [(0, 1), (1, 0)])
    pairs = [(i ^ 1, i) for i in range(plan.wide)]
    near = lax.ppermute(near, "wide", pairs)
    pairs = [(i, j) for i in range(1, plan.wide - 1, 2) for i, j in ((i, i + 1), (i + 1, i))]
    next_ = lax.ppermute(next_, "wide", pairs)

    half_shape = shape((6, plan.rows_x, length_y), f32)
    own_part, table = call(
        partial(ready_kernel, plan), (half_shape, shape(table.shape, bf16)), [VMEM] * 2, (VMEM, VMEM), [],
        1 << 26, LIMITS[1],
    )(demag_spectrum, table)
    mixed, far_part = call(
        partial(ahead_kernel, plan), (shape((6, 2 * length_x, length_y), f32), half_shape),
        [VMEM] * 3, (VMEM, VMEM), [], 1 << 29, LIMITS[2],
    )(got, table, swapped)
    sent = call(
        partial(back_kernel, plan),
        shape((count, lanes), f32),
        [VMEM] * 6, VMEM,
        [pltpu.VMEM((3, 4 * length_x, length_y), bf16), pltpu.VMEM((6, plan.rows_x, length_y), f32)],
        1 << 29, LIMITS[2],
    )(mixed, own_part, far_part, table, lower, upper)

    back = lax.all_to_all(sent.reshape(blocks), both, 0, 0, tiled=True).reshape(count, lanes)
    base, damp = call(
        partial(local_kernel, plan, species), (shape((3 * cells, lanes), f32), shape((cells, lanes), f32)),
        [VMEM] * 5 + [SMEM] * 4 + [VMEM], (VMEM, VMEM), [pltpu.VMEM((cells, lanes), f32)], 1 << 22, LIMITS[3],
    )(turned, side, near, next_, material2, saturation, anisotropy, damping, applied, table_out)

    rate, demag = call(
        partial(last_kernel, plan),
        (shape((3 * cells, lanes), f32), shape((3 * cells, lanes), f32)),
        [VMEM] * 5, (HBM, HBM),
        [pltpu.VMEM((3 * cells, lanes), f32), pltpu.VMEM((3 * cells, lanes), f32), pltpu.SemaphoreType.DMA((4,))],
        1 << 28, LIMITS[4],
    )(back, table_out, base, turned, damp)
    return rate.reshape(spin.shape), demag.reshape(spin.shape)


def shards(*args):
    spin, demag_spectrum = args[0], args[-1]
    _, layers, width_x, width_y = spin.shape
    _, planes, rows_x, length_y = demag_spectrum.shape
    plan = Plan(lax.axis_size("wide"), lax.axis_size("narrow"), layers, width_x, width_y,
                planes, rows_x, length_y)
    if plan.fits():
        return plane_shards(plan, *args)
    return general_shards(*args)


def solution(mesh):
    placed = (
        P(None, None, "wide", "narrow"),
        P(None, "wide", "narrow"),
        P(None, "wide", "narrow"),
        P(),
        P(),
        P(),
        P(),
        P(None, "wide", "narrow", None),
    )
    return jax.shard_map(
        shards,
        mesh=mesh,
        in_specs=placed,
        out_specs=(P(None, None, "wide", "narrow"), P(None, None, "wide", "narrow")),
        check_vma=False,
    )
```

```python
from functools import partial
import math

import jax
import jax.numpy as jnp
import numpy as np
from jax import lax
from jax.experimental import pallas as pl
from jax.experimental.pallas import tpu as pltpu
from jax.sharding import PartitionSpec as P


exchange_coef = 0.3
highest = lax.Precision.HIGHEST


def extended(x, sides, width):
    for axis, dim in sides:
        peers, length = (lax.axis_size(axis), x.shape[dim])
        up = [(i, (i + 1) % peers) for i in range(peers - 1)]
        down = [(j, i) for i, j in up]
        last = lax.slice_in_dim(x, length - width, length, axis=dim)
        leading = lax.slice_in_dim(x, 0, width, axis=dim)
        before = lax.ppermute(last, axis, up)
        after = lax.ppermute(leading, axis, down)
        x = jnp.concatenate([before, x, after], axis=dim)
    return x


def phase_table(rows_count, cols_count, length, sign):
    left_index = lax.broadcasted_iota(jnp.int32, (rows_count, cols_count), 0)
    right_index = lax.broadcasted_iota(jnp.int32, (rows_count, cols_count), 1)
    angle = (left_index * right_index % length).astype(jnp.float32) * (2.0 * math.pi / length)
    return (jnp.cos(angle), sign * jnp.sin(angle))


def contract(pattern, phases, values):
    phase_re, phase_im = phases
    value_re, value_im = values
    product = partial(jnp.einsum, pattern, precision=highest)
    if value_im is None:
        return (product(phase_re, value_re), product(phase_im, value_re))
    return (
        product(phase_re, value_re) - product(phase_im, value_im),
        product(phase_re, value_im) + product(phase_im, value_re),
    )


def factors(half_size, at_end):
    if at_end:
        inner_size = math.gcd(half_size, 128)
    else:
        inner_size = max(
            (
                divisor
                for divisor in range(1, half_size + 1)
                if half_size % divisor == 0 and divisor * divisor <= 2 * half_size
            )
        )
    return (inner_size, 2 * half_size // inner_size)


def forward(values, at_end, natural):
    value_re, value_im = values
    extent = value_re.shape
    half_size = extent[1]
    length = 2 * half_size
    inner_size, outer_size = factors(half_size, at_end)
    tail_index = "" if at_end else "b"
    blocked = (extent[0], outer_size // 2, inner_size) + extent[2:]
    value_re = value_re.reshape(blocked)
    value_im = None if value_im is None else value_im.reshape(blocked)
    phases = phase_table(outer_size, outer_size // 2, outer_size, -1.0)
    work_re, work_im = contract(
        "kn,anp" + tail_index + "->akp" + tail_index, phases, (value_re, value_im)
    )
    twist_re, twist_im = phase_table(outer_size, inner_size, length, -1.0)
    if not at_end:
        twist_re, twist_im = (twist_re[:, :, None], twist_im[:, :, None])
    work_re, work_im = (
        work_re * twist_re - work_im * twist_im,
        work_re * twist_im + work_im * twist_re,
    )
    target = "ajk" if natural else "akj"
    phases = phase_table(inner_size, inner_size, inner_size, -1.0)
    out_re, out_im = contract(
        "jp,akp" + tail_index + "->" + target + tail_index, phases, (work_re, work_im)
    )
    merged = (extent[0], length) + extent[2:]
    return (out_re.reshape(merged), out_im.reshape(merged))


def inverse(values, at_end, natural, real_only):
    value_re, value_im = values
    extent = value_re.shape
    length = extent[1]
    half_size = length // 2
    inner_size, outer_size = factors(half_size, at_end)
    tail_index = "" if at_end else "b"
    if natural:
        blocked = (extent[0], inner_size, outer_size) + extent[2:]
        source = "ajk"
    else:
        blocked = (extent[0], outer_size, inner_size) + extent[2:]
        source = "akj"
    phases = phase_table(inner_size, inner_size, inner_size, 1.0)
    work_re, work_im = contract(
        "pj," + source + tail_index + "->akp" + tail_index,
        phases,
        (value_re.reshape(blocked), value_im.reshape(blocked)),
    )
    twist_re, twist_im = phase_table(outer_size, inner_size, length, 1.0)
    if not at_end:
        twist_re, twist_im = (twist_re[:, :, None], twist_im[:, :, None])
    work_re, work_im = (
        work_re * twist_re - work_im * twist_im,
        work_re * twist_im + work_im * twist_re,
    )
    phases = phase_table(outer_size // 2, outer_size, outer_size, 1.0)
    pattern = "nk,akp" + tail_index + "->anp" + tail_index
    scale = 1.0 / length
    merged = (extent[0], half_size) + extent[2:]
    if real_only:
        product = partial(jnp.einsum, pattern, precision=highest)
        result = product(phases[0], work_re) - product(phases[1], work_im)
        return result.reshape(merged) * scale
    out_re, out_im = contract(pattern, phases, (work_re, work_im))
    return (out_re.reshape(merged) * scale, out_im.reshape(merged) * scale)


def along_x(pieces):
    piece_re, piece_im = pieces
    members, planes, cells_x, cells_y = piece_re.shape
    extent = (members * planes, cells_x, cells_y)
    out_re, out_im = forward((piece_re.reshape(extent), piece_im.reshape(extent)), False, True)
    merged = (members, planes, 2 * cells_x, cells_y)
    return (out_re.reshape(merged), out_im.reshape(merged))


def along_y(pieces):
    piece_re, piece_im = pieces
    members, planes, rows_x, cells_y = piece_re.shape
    extent = (members * planes * rows_x, cells_y)
    out_re, out_im = forward((piece_re.reshape(extent), piece_im.reshape(extent)), True, False)
    merged = (members, planes, rows_x, 2 * cells_y)
    return (out_re.reshape(merged), out_im.reshape(merged))


def back_to_bricks(field_re, field_im):
    members, planes, rows_x, length_y = field_re.shape
    flattened = (members * planes * rows_x, length_y)
    grid_re, grid_im = inverse(
        (field_re.reshape(flattened), field_im.reshape(flattened)), True, False, False
    )
    merged = (members, planes, rows_x, length_y // 2)
    piece_re = lax.all_to_all(
        grid_re.reshape(merged), "narrow", split_axis=3, concat_axis=2, tiled=True
    )
    piece_im = lax.all_to_all(
        grid_im.reshape(merged), "narrow", split_axis=3, concat_axis=2, tiled=True
    )
    members, planes, length_x, cells_y = piece_re.shape
    extent = (members * planes, length_x, cells_y)
    out_re, out_im = inverse(
        (piece_re.reshape(extent), piece_im.reshape(extent)), False, True, False
    )
    invert_merged = (members, planes, length_x // 2, cells_y)
    columns = (out_re.reshape(invert_merged), out_im.reshape(invert_merged))
    piece_re, piece_im = lax.all_to_all(columns, "wide", split_axis=2, concat_axis=1, tiled=True)
    members, planes, cells_x, cells_y = piece_re.shape
    extent = (members, planes, cells_x * cells_y)
    result = inverse((piece_re.reshape(extent), piece_im.reshape(extent)), False, True, True)
    merged = (members, planes // 2, cells_x, cells_y)
    return result.reshape(merged)


def couple(kernel, values, picks):
    return -(
        kernel[picks[0]] * values[0] + kernel[picks[1]] * values[1] + kernel[picks[2]] * values[2]
    )


def cross(left, right):
    return jnp.stack(
        [
            left[1] * right[2] - left[2] * right[1],
            left[2] * right[0] - left[0] * right[2],
            left[0] * right[1] - left[1] * right[0],
        ]
    )


def general_shards(spin, region, material, saturation, anisotropy, damping, applied, demag_spectrum):
    magnet = region.astype(jnp.float32)
    direction = spin * magnet[None]
    species = saturation.shape[0]
    chosen = (
        material[None] == lax.broadcasted_iota(jnp.int32, (species,) + material.shape, 0)
    ).astype(jnp.float32)

    def lookup(entries):
        return jnp.sum(chosen * entries[:, None, None, None], axis=0)

    sat_cell = lookup(saturation)
    anis_cell = lookup(anisotropy)
    damp_cell = lookup(damping)
    moment = direction * sat_cell[None]
    components, layers, width_x, width_y = spin.shape
    flattened = moment.reshape(components, layers, width_x * width_y)
    spec_re, spec_im = forward((flattened, None), False, True)
    stacked = (components, 2 * layers, width_x, width_y)
    spectra = along_x(
        (
            lax.all_to_all(
                spec_re.reshape(stacked), "wide", split_axis=1, concat_axis=2, tiled=True
            ),
            lax.all_to_all(
                spec_im.reshape(stacked), "wide", split_axis=1, concat_axis=2, tiled=True
            ),
        )
    )
    spec_re, spec_im = along_y(
        lax.all_to_all(spectra, "narrow", split_axis=2, concat_axis=3, tiled=True)
    )
    parts, planes, rows_x, length_y = demag_spectrum.shape
    inner_size, outer_size = factors(length_y // 2, True)
    kernel = demag_spectrum.reshape(parts, planes, rows_x, inner_size, outer_size)
    kernel = (
        kernel.transpose(0, 1, 2, 4, 3).reshape(parts, planes, rows_x, length_y).astype(jnp.float32)
    )
    couplings = ((0, 3, 4), (3, 1, 5), (4, 5, 2))
    field_re = [couple(kernel, spec_re, picks) for picks in couplings]
    field_im = [couple(kernel, spec_im, picks) for picks in couplings]
    demag = back_to_bricks(jnp.stack(field_re), jnp.stack(field_im))
    framed = extended(direction, (("wide", 2), ("narrow", 3)), 1)
    framed = jnp.pad(framed, ((0, 0), (1, 1), (0, 0), (0, 0)))
    weight = jnp.sum(framed * framed, axis=0)
    neighbours = (
        framed[:, 2:, 1:-1, 1:-1]
        + framed[:, :-2, 1:-1, 1:-1]
        + framed[:, 1:-1, 2:, 1:-1]
        + framed[:, 1:-1, :-2, 1:-1]
        + framed[:, 1:-1, 1:-1, 2:]
        + framed[:, 1:-1, 1:-1, :-2]
    )
    present = (
        weight[2:, 1:-1, 1:-1]
        + weight[:-2, 1:-1, 1:-1]
        + weight[1:-1, 2:, 1:-1]
        + weight[1:-1, :-2, 1:-1]
        + weight[1:-1, 1:-1, 2:]
        + weight[1:-1, 1:-1, :-2]
    )
    laplace = neighbours - present[None] * direction
    zeros = jnp.zeros_like(sat_cell)
    uniaxial = jnp.stack([zeros, zeros, 2.0 * anis_cell / sat_cell * direction[2]])
    field = (
        exchange_coef * laplace / sat_cell[None] + demag + applied[:, None, None, None] + uniaxial
    )
    torque = cross(direction, field)
    rate = (
        -(torque + damp_cell[None] * cross(direction, torque)) / (1.0 + damp_cell * damp_cell)[None]
    )
    return (rate, demag)


def split_table(table):
    high = jnp.asarray(np.asarray(table, np.float32)).astype(jnp.bfloat16)
    high64 = np.asarray(np.asarray(table, np.float32).astype(high.dtype), np.float64)
    low = (table - high64).astype(np.float32).astype(high.dtype)
    return np.asarray(high64.astype(high.dtype)), low


class Plan:
    def __init__(self, wide, narrow, layers, width_x, width_y, planes, rows_x, length_y):
        self.wide, self.narrow = wide, narrow
        self.layers, self.width_x, self.width_y = layers, width_x, width_y
        self.planes, self.rows_x = planes, rows_x
        self.length_z, self.length_x, self.length_y = planes * wide, rows_x * narrow, length_y
        self.cells_x, self.cells_y = width_x * wide, width_y * narrow
        self.devices = wide * narrow
        self.special, self.holder = 1, self.narrow * (wide // 2)

    def fits(self):
        return (
            self.narrow == 2
            and self.planes == 4
            and self.wide % 16 == 0
            and self.devices * 2 == self.length_z
            and self.length_z == 2 * self.layers
            and self.length_x == 2 * self.cells_x
            and self.length_y == 2 * self.cells_y
            and self.width_x == 2
            and self.width_y % 128 == 0
            and self.rows_x % 16 == 0
            and 6 * self.cells_x <= self.cells_y
            and (self.layers * self.width_x) % 8 == 0
            and 6 * self.rows_x == 3 * self.layers * self.width_x
        )

    def wave(self):
        w, n = np.divmod(np.arange(self.devices), self.narrow)
        return self.planes * w + np.where(w < self.wide // 2, 1 - n, 1 + n)

    def thickness_tables(self):
        wave = self.wave()
        z = np.arange(self.layers)
        angle = 2.0 * np.pi * ((wave[:, None] * z[None]) % self.length_z) / self.length_z
        ahead = np.stack([np.cos(angle), -np.sin(angle)], 1)
        back = np.stack([2.0 * np.cos(angle), -2.0 * np.sin(angle)], 1)
        middle = 1.0 - 2.0 * (z % 2)
        ahead[self.special, 1] = middle
        back[self.special, 0] = 1.0
        back[self.special, 1] = middle
        back *= -1.0 / (self.length_z * self.length_x * self.length_y)
        n = np.arange(self.devices) % self.narrow
        x = np.arange(self.width_x)
        sign = 1.0 - 2.0 * ((n[:, None] * x[None]) % 2)
        unit_x = np.eye(self.width_x)
        ahead = np.einsum("drz,dx,xv->rxdzv", ahead, sign, unit_x)
        back = np.einsum("drz,dx,xv->zvrxd", back, sign, unit_x)
        count = self.devices * 6 * self.width_x
        cells = 3 * self.layers * self.width_x
        return ahead.reshape(count // 3, cells // 3), back.reshape(cells // 3, count // 3)

    def lateral_tables(self):
        half = self.cells_y
        y, k = np.arange(half), np.arange(half)
        angle = 2.0 * np.pi * ((y[:, None] * k[None]) % self.length_y) / self.length_y
        cosine, sine = np.cos(angle), np.sin(angle)
        sine[:, 0] = 1.0 - 2.0 * (y % 2)
        ahead_y = np.concatenate([cosine, sine], 1)
        x = (np.arange(self.wide)[None] * self.width_x + np.arange(self.width_x)[:, None]).reshape(-1)
        kx = np.arange(self.length_x)
        angle = 2.0 * np.pi * ((kx[:, None] * x[None]) % self.length_x) / self.length_x
        cosine, sine = np.cos(angle), np.sin(angle)
        ahead_x = np.block([[cosine, sine], [-sine, cosine]])
        back_x = np.block([[cosine.T, -sine.T], [sine.T, cosine.T]])
        return ahead_y, ahead_x, back_x


def halves(value):
    high = value.astype(jnp.bfloat16)
    return high, (value - high.astype(jnp.float32)).astype(jnp.bfloat16)


def mul(left, right):
    return jnp.dot(left, right, preferred_element_type=jnp.float32)


def mul_back(left, right):
    return lax.dot_general(left, right, (((1,), (1,)), ((), ())), preferred_element_type=jnp.float32)


def pick(material, entries, species):
    value = jnp.zeros(material.shape, jnp.float32)
    for s in range(species):
        value = jnp.where(material == s, entries[s], value)
    return value


def rows_of(plan):
    w, n = lax.axis_index("wide"), lax.axis_index("narrow")
    low = w >= plan.wide // 2
    own = jnp.where(low, 1 + n, 1 - n)
    other = jnp.where(low, 2 - n, n)
    return w, n, own, other


def first_kernel(plan, species, spin_at, region_at, material_at, saturation_at, table_at, tensor,
                 out_at, swap_at, lower_at, upper_at,
                 spin, region, material, saturation, table, held, held0,
                 out, swap, lower, upper, sems, done):
    w, _, _, other = rows_of(plan)
    count = plan.rows_x
    moves = [
        pltpu.make_async_copy(source, target, sems.at[k])
        for k, (source, target) in enumerate((
            (saturation_at, saturation), (material_at, material), (region_at, region), (spin_at, spin),
            (table_at, table), (tensor.at[:, other], held),
        ))
    ]
    fetch0 = pltpu.make_async_copy(tensor.at[:, 0], held0, sems.at[7])

    @pl.when(w == plan.wide // 2)
    def _():
        fetch0.start()

    for move in moves[::-1]:
        move.start()
    sent = []

    def send(source, target):
        move = pltpu.make_async_copy(source, target, done.at[len(sent)])
        move.start()
        sent.append(move)

    for move in moves[:4]:
        move.wait()
    cells = plan.layers * plan.width_x
    magnet = region[...].astype(jnp.float32)
    sat = pick(material[...], saturation, species)
    high, low = [], []
    for c in range(3):
        direction = spin[c * cells : (c + 1) * cells, :] * magnet
        a, b = halves(direction * sat)
        high.append(a)
        low.append(b)
    high, low = jnp.concatenate(high, 1), jnp.concatenate(low, 1)
    moves[5].wait()
    for t in range(6):
        rows = slice(t * count, (t + 1) * count)
        swap[rows, : plan.length_y] = held[t].astype(jnp.float32)
    send(swap, swap_at)
    far = [pltpu.make_async_copy(lower, lower_at, sems.at[8]), pltpu.make_async_copy(upper, upper_at, sems.at[9])]

    @pl.when(w == plan.wide // 2)
    def _():
        fetch0.wait()
        cut, half = SPLIT * count, plan.cells_y
        flip = flip_of(half)
        minus = mul(jnp.concatenate([held0[t, :, half:] for t in range(6)], 0), flip)
        lower[(6 - SPLIT) * count :, :] = jnp.zeros((8, plan.length_y), jnp.float32)
        upper[cut:, :] = jnp.zeros((8, plan.length_y), jnp.float32)
        for t in range(6):
            plus, rest = held0[t, :, :half].astype(jnp.float32), minus[t * count : (t + 1) * count, :]
            if t < SPLIT:
                here, there, at, edge = upper, lower, t * count, (6 - SPLIT) * count + t
            else:
                here, there, at, edge = lower, upper, (t - SPLIT) * count, cut + t
            here[at : at + count, :half] = plus
            here[at : at + count, half:] = rest
            there[edge : edge + 1, :half] = plus[0:1, :]
            there[edge : edge + 1, half:] = rest[0:1, :]
        for move in far:
            move.start()

    moves[4].wait()
    result = mul(table[...], jnp.concatenate([high, low, high], 0))
    group, lanes = plan.devices, plan.width_y
    for c in range(3):
        for j in range(2 * plan.width_x):
            out[pl.ds(c * 2 * plan.width_x + j, group, stride=6 * plan.width_x), :] = result[
                j * group : (j + 1) * group, c * lanes : (c + 1) * lanes]
    send(out, out_at)

    @pl.when(w == plan.wide // 2)
    def _():
        for move in far:
            move.wait()

    for move in sent:
        move.wait()


def halo_kernel(plan, spin, region, turned, near, next_, side):
    w, n = lax.axis_index("wide"), lax.axis_index("narrow")
    cells = plan.layers * plan.width_x
    magnet = region[...].astype(jnp.float32)
    for c in range(3):
        turned[c * cells : (c + 1) * cells, :] = spin[c * cells : (c + 1) * cells, :] * magnet
    layers3 = 3 * plan.layers
    up, down = turned[pl.ds(1, layers3, stride=2), :], turned[pl.ds(0, layers3, stride=2), :]
    near[...] = jnp.where(w % 2 == 0, up, down)
    next_[...] = jnp.where(w % 2 == 0, down, up)
    column = lax.broadcasted_iota(jnp.int32, (8, plan.width_y), 1)
    chosen = jnp.where(column == jnp.where(n == 0, plan.width_y - 1, 0), 1.0, 0.0).astype(jnp.bfloat16)
    high = turned[...].astype(jnp.bfloat16)
    rest = turned[...] - high.astype(jnp.float32)
    middle, low = halves(rest)
    side[...] = mul_back(chosen, high) + mul_back(chosen, middle) + mul_back(chosen, low)


def flip_of(half):
    sum_of = lax.broadcasted_iota(jnp.int32, (half, half), 0) + lax.broadcasted_iota(jnp.int32, (half, half), 1)
    return jnp.where((sum_of == half) | (sum_of == 0), 1.0, 0.0).astype(jnp.bfloat16)


SPLIT = 4


def unfold_zero(plan, lower, upper, second):
    half, count = plan.cells_y, plan.rows_x
    row = lax.broadcasted_iota(jnp.int32, (count, count), 0)
    col = lax.broadcasted_iota(jnp.int32, (count, count), 1)
    turn = jnp.where(row + col == count, 1.0, 0.0).astype(jnp.bfloat16)
    first = lax.broadcasted_iota(jnp.int32, (count, 2 * half), 0) == 0
    lane0 = lax.broadcasted_iota(jnp.int32, (count, half), 1) == 0
    for t in range(6):
        here, at, there, edge = (
            (upper, t, lower, (6 - SPLIT) * count + t) if t < SPLIT else (lower, t - SPLIT, upper, SPLIT * count + t)
        )
        rows = slice(at * count, (at + 1) * count)
        plus, minus = here[rows, :half], here[rows, half:]
        crossed = jnp.concatenate([jnp.where(lane0, plus, minus), jnp.where(lane0, minus, plus)], 1)
        crossed = mul(turn, crossed.astype(jnp.bfloat16))
        second[t] = jnp.where(first, there[edge : edge + 1, :], crossed)


COUPLINGS = ((0, 3, 4), (3, 1, 5), (4, 5, 2))


def ready_kernel(plan, tensor, table_at, own_part, table):
    _, _, own, _ = rows_of(plan)
    half, count = plan.cells_y, plan.rows_x
    table[...] = table_at[...]
    turned = mul(jnp.concatenate([tensor[t, own, :, half:] for t in range(6)], 0), flip_of(half))
    for t in range(6):
        own_part[t, :, :half] = tensor[t, own, :, :half].astype(jnp.float32)
        own_part[t, :, half:] = turned[t * count : (t + 1) * count, :]


def ahead_kernel(plan, got, table, swapped, mixed, far_part):
    w, n, _, _ = rows_of(plan)
    half, wide = plan.cells_y, plan.wide
    cells_x, length_x, narrow = plan.cells_x, plan.length_x, plan.narrow
    block = 6 * plan.width_x
    lines = []
    for c in range(3):
        for j in range(2 * plan.width_x):
            row = c * 2 * plan.width_x + j
            lines.append(jnp.concatenate(
                [got[pl.ds(m * block + row, wide, stride=narrow * block), :] for m in range(narrow)], 1))
    lines = jnp.concatenate(lines, 0)
    high, low = halves(lines)
    y_high, y_low = table[:half, :], table[half : 2 * half, :]
    x_ahead = table[2 * half : 2 * half + 2 * length_x, : 6 * cells_x]
    waves = mul(high, y_high) + (mul(low, y_high) + mul(high, y_low))
    flip = flip_of(half)
    count = plan.rows_x
    turned_far = mul(swapped[:, half : 2 * half].astype(jnp.bfloat16), flip)
    for t in range(6):
        rows = slice(t * count, (t + 1) * count)
        far_part[t, :, :half] = swapped[rows, :half]
        far_part[t, :, half:] = turned_far[rows, :]
    edge = lax.broadcasted_iota(jnp.int32, (cells_x, half), 1) == 0
    parts = [(waves[g * cells_x : (g + 1) * cells_x, :half], waves[g * cells_x : (g + 1) * cells_x, half:])
             for g in range(6)]

    def stage(g, real, imag):
        (pr, qr), (pi, qi) = real, imag
        plus = jnp.where(edge, pr, pr + qi), jnp.where(edge, pi, pi - qr)
        minus = jnp.where(edge, qr, pr - qi), jnp.where(edge, qi, pi + qr)
        stack = jnp.concatenate([jnp.concatenate([p, m], 1) for p, m in zip(plus, minus)], 0)
        a, b = halves(stack)
        mixed[g] = mul(x_ahead, jnp.concatenate([a, b, a], 0))

    special = jnp.logical_and(w == 0, n == 1)

    @pl.when(special)
    def _():
        none = jnp.zeros((cells_x, half), jnp.float32)
        for g in range(6):
            stage(g, parts[g], (none, none))

    @pl.when(jnp.logical_not(special))
    def _():
        for c in range(3):
            stage(c, parts[2 * c], parts[2 * c + 1])


def back_kernel(plan, mixed, own_part, far_part, table, lower, upper, out, packed, second):
    w, n, _, _ = rows_of(plan)
    lanes, half, wide = plan.width_y, plan.cells_y, plan.wide
    length_x, narrow = plan.length_x, plan.narrow
    block, per_c = 6 * plan.width_x, 2 * plan.cells_x
    y_high, y_low = table[:half, :], table[half : 2 * half, :]
    base = 2 * half
    xb_pair = table[base : base + per_c, half : half + 4 * length_x]
    xb_low = table[base + per_c : base + 2 * per_c, half : half + 2 * length_x]
    step = 16

    def couple(paired):
        for lane in range(0, half, 128):
            for row in range(0, length_x, step):
                left = slice(lane, lane + 128)
                right = slice(half + lane, half + lane + 128)
                cr, sr = slice(row, row + step), slice(length_x + row, length_x + row + step)
                part = own_part if row < plan.rows_x else far_part
                at = slice(row % plan.rows_x, row % plan.rows_x + step)
                if lane == 0:
                    edge = lax.broadcasted_iota(jnp.int32, (step, 128), 1) == 0
                fields = [
                    (mixed[g, cr, left], mixed[g, sr, left], mixed[g, cr, right], mixed[g, sr, right])
                    for g in range(6 if paired else 3)
                ]
                for i in range(3):
                    sums = []
                    for s, lanes_at in ((0, left), (2, right)):
                        real = imag = None
                        for j in range(3):
                            t = COUPLINGS[i][j]
                            ka = part[t, at, lanes_at]
                            if paired:
                                straight = (row < plan.rows_x) == (t < SPLIT)
                                base_at = (t if t < SPLIT else t - SPLIT) * plan.rows_x + row % plan.rows_x
                                source = upper if t < SPLIT else lower
                                kb = source[base_at : base_at + step, lanes_at] if straight else second[t, at, lanes_at]
                                a, b = fields[2 * j], fields[2 * j + 1]
                                re = ka * a[s] - kb * b[s + 1]
                                im = ka * a[s + 1] + kb * b[s]
                            else:
                                re, im = ka * fields[j][s], ka * fields[j][s + 1]
                            real = re if real is None else real + re
                            imag = im if imag is None else imag + im
                        sums.append((real, imag))
                    (pr, pi), (mr, mi) = sums
                    even_re, even_im, odd_re, odd_im = pr + mr, pi + mi, mi - pi, pr - mr
                    if lane == 0:
                        even_re, even_im = jnp.where(edge, pr, even_re), jnp.where(edge, pi, even_im)
                        odd_re, odd_im = jnp.where(edge, mr, odd_re), jnp.where(edge, mi, odd_im)
                    for value, base_at, lanes_at in (
                        (even_re, 0, left), (even_im, length_x, left),
                        (odd_re, 0, right), (odd_im, length_x, right),
                    ):
                        a, b = halves(value)
                        high_at, low_at = base_at + row, 2 * length_x + base_at + row
                        packed[i, high_at : high_at + step, lanes_at] = a
                        packed[i, low_at : low_at + step, lanes_at] = b

    special = jnp.logical_and(w == 0, n == 1)

    @pl.when(special)
    def _():
        unfold_zero(plan, lower, upper, second)
        couple(True)

    pl.when(jnp.logical_not(special))(lambda: couple(False))
    back = []
    for i in range(3):
        back.append(mul(xb_pair, packed[i]) + mul(xb_low, packed[i, : 2 * length_x, :]))
    high, low = halves(jnp.concatenate(back, 0))
    result = mul_back(high, y_high) + (mul_back(low, y_high) + mul_back(high, y_low))
    for c in range(3):
        for j in range(2 * plan.width_x):
            row = c * 2 * plan.width_x + j
            for m in range(narrow):
                out[pl.ds(m * block + row, wide, stride=narrow * block), :] = result[
                    row * wide : (row + 1) * wide, m * lanes : (m + 1) * lanes]


def local_kernel(plan, species, turned, side, near, next_, material, saturation, anisotropy,
                 damping, applied, table, out, damp, woven):
    w, n = lax.axis_index("wide"), lax.axis_index("narrow")
    cells, layers = plan.layers * plan.width_x, plan.layers
    row = lax.broadcasted_iota(jnp.int32, (cells, plan.width_y), 0)
    col = lax.broadcasted_iota(jnp.int32, (cells, plan.width_y), 1)
    first, last = col == 0, col == plan.width_y - 1
    even = row % 2 == 0
    ahead = jnp.where(n == 0, 1.0, 0.0)
    sat = pick(material[...], saturation, species)
    anis = pick(material[...], anisotropy, species)
    damp[...] = pick(material[...], damping, species)
    square = lax.broadcasted_iota(jnp.int32, (cells, cells), 0) == lax.broadcasted_iota(
        jnp.int32, (cells, cells), 1)
    sums, present, own = [], jnp.zeros((cells, plan.width_y), jnp.float32), []
    for c in range(3):
        d = turned[c * cells : (c + 1) * cells, :]
        line = jnp.broadcast_to(side[0:1, c * cells : (c + 1) * cells], (cells, cells))
        s = jnp.sum(jnp.where(square, line, 0.0), axis=1, keepdims=True)
        a, b = near[c * layers : (c + 1) * layers, :], next_[c * layers : (c + 1) * layers, :]
        woven[pl.ds(0, layers, stride=2), :] = jnp.where(w % 2 == 0, b, a)
        woven[pl.ds(1, layers, stride=2), :] = jnp.where(w % 2 == 0, a, b)
        beside = (
            jnp.where(row >= 2, pltpu.roll(d, 2, 0), 0.0),
            jnp.where(row < cells - 2, pltpu.roll(d, cells - 2, 0), 0.0),
            woven[...],
            jnp.where(even, pltpu.roll(d, cells - 1, 0), pltpu.roll(d, 1, 0)),
            pltpu.roll(jnp.where(first, s * ahead, d), plan.width_y - 1, 1),
            pltpu.roll(jnp.where(last, s * (1.0 - ahead), d), 1, 1),
        )
        total = beside[0]
        present = present + beside[0] * beside[0]
        for v in beside[1:]:
            total = total + v
            present = present + v * v
        sums.append(total)
        own.append(d)
    for c in range(3):
        field = exchange_coef * (sums[c] - present * own[c]) / sat + applied[c]
        if c == 2:
            field = field + 2.0 * anis / sat * own[2]
        out[c * cells : (c + 1) * cells, :] = field


def last_kernel(plan, got, table, base, turned, damping, rate_at, demag_at, rate, demag, sems):
    cells = plan.layers * plan.width_x
    group, lanes, block = plan.devices, plan.width_y, 2 * plan.width_x
    lines = jnp.concatenate([
        jnp.concatenate([got[pl.ds(c * block + j, group, stride=3 * block), :] for c in range(3)], 1)
        for j in range(block)
    ], 0)
    high, low = halves(lines)
    result = mul(table[...], jnp.concatenate([high, low, high], 0))
    for c in range(3):
        demag[c * cells : (c + 1) * cells, :] = result[:, c * lanes : (c + 1) * lanes]
    moves = [pltpu.make_async_copy(demag, demag_at, sems.at[3])]
    moves[0].start()
    damp = damping[...]
    d = [turned[c * cells : (c + 1) * cells, :] for c in range(3)]
    f = [demag[c * cells : (c + 1) * cells, :] + base[c * cells : (c + 1) * cells, :] for c in range(3)]

    def turn(u, v):
        return [u[1] * v[2] - u[2] * v[1], u[2] * v[0] - u[0] * v[2], u[0] * v[1] - u[1] * v[0]]

    torque = turn(d, f)
    again = turn(d, torque)
    scale = -1.0 / (1.0 + damp * damp)
    for c in range(3):
        rows = pl.ds(c * cells, cells)
        rate[rows, :] = (torque[c] + damp * again[c]) * scale
        moves.append(pltpu.make_async_copy(rate.at[rows], rate_at.at[rows], sems.at[c]))
        moves[-1].start()
    for move in moves:
        move.wait()


LIMITS = (67043328, 8 << 20, 8 << 20, 4 << 20, 8 << 20)
VMEM = pl.BlockSpec(memory_space=pltpu.VMEM)
SMEM = pl.BlockSpec(memory_space=pltpu.SMEM)
HBM = pl.BlockSpec(memory_space=pltpu.HBM)


def plane_shards(plan, spin, region, material, saturation, anisotropy, damping, applied, demag_spectrum):
    f32, bf16 = jnp.float32, jnp.bfloat16
    cells, lanes = plan.layers * plan.width_x, plan.width_y
    count, length_y, length_x = plan.devices * 6 * plan.width_x, plan.length_y, plan.length_x
    species = saturation.shape[0]
    shape = jax.ShapeDtypeStruct
    spin2 = spin.reshape(3 * cells, lanes)
    region2, material2 = region.reshape(cells, lanes), material.reshape(cells, lanes)
    ahead_z, back_z = plan.thickness_tables()
    ahead_y, ahead_x, back_x = plan.lateral_tables()
    az, bz, ay = (split_table(t) for t in (ahead_z, back_z, ahead_y))
    ax, bx = split_table(ahead_x), split_table(back_x)
    x_ahead = np.concatenate([ax[0], ax[0], ax[1]], 1)
    xb_pair = np.concatenate([bx[0], bx[0]], 1)

    def call(body, out_shape, in_specs, out_specs, scratch, flops, limit=24 << 20):
        return pl.pallas_call(
            body, out_shape=out_shape, in_specs=in_specs, out_specs=out_specs, scratch_shapes=scratch,
            compiler_params=pltpu.CompilerParams(vmem_limit_bytes=limit),
            cost_estimate=pl.CostEstimate(flops=flops, bytes_accessed=1 << 20, transcendentals=0),
        )

    rows6 = 6 * plan.rows_x
    table_in = jnp.asarray(np.concatenate([az[0], az[0], az[1]], 1))
    table_out = jnp.asarray(np.concatenate([bz[0], bz[0], bz[1]], 1))
    outs = ((count, lanes), (rows6, length_y), ((6 - SPLIT) * plan.rows_x + 8, length_y),
            (SPLIT * plan.rows_x + 8, length_y))
    outs = tuple(shape(o, f32) for o in outs)
    half = plan.cells_y
    small = np.zeros((2 * length_x, 2 * half), ax[0].dtype)
    small[:, : 6 * plan.cells_x] = x_ahead
    small[: 2 * plan.cells_x, half : half + 4 * length_x] = xb_pair
    small[2 * plan.cells_x : 4 * plan.cells_x, half : half + 2 * length_x] = bx[1]
    table = jnp.asarray(np.concatenate([ay[0], ay[1], small], 0))

    out, swap, lower, upper = call(
        partial(first_kernel, plan, species),
        outs, [HBM] * 6, (HBM,) * len(outs),
        [pltpu.VMEM((3 * cells, lanes), f32), pltpu.VMEM((cells, lanes), jnp.int32),
         pltpu.VMEM((cells, lanes), jnp.int32), pltpu.SMEM((species,), f32),
         pltpu.VMEM(table_in.shape, bf16),
         pltpu.VMEM((6, plan.rows_x, length_y), bf16), pltpu.VMEM((6, plan.rows_x, length_y), bf16)]
        + [pltpu.VMEM(o.shape, o.dtype) for o in outs]
        + [pltpu.SemaphoreType.DMA((10,)), pltpu.SemaphoreType.DMA((2,))],
        1 << 28, LIMITS[0],
    )(spin2, region2, material2, saturation, table_in, demag_spectrum)

    both = ("wide", "narrow")
    swapped = lax.ppermute(swap, "narrow", [(0, 1), (1, 0)])
    blocks = (plan.devices, 3, 2 * plan.width_x, lanes)
    got = lax.all_to_all(out.reshape(blocks), both, 0, 0, tiled=True).reshape(count, lanes)
    lower = lax.ppermute(lower, both, [(plan.holder, plan.special)])
    upper = lax.ppermute(upper, both, [(plan.holder + 1, plan.special)])
    edge_shape = shape((3 * plan.layers, lanes), f32)
    turned, near, next_, side = call(
        partial(halo_kernel, plan),
        (shape((3 * cells, lanes), f32), edge_shape, edge_shape, shape((8, 3 * cells), f32)),
        [VMEM] * 2, (VMEM,) * 4, [], 1 << 22, LIMITS[1],
    )(spin2, region2)
    side = lax.ppermute(side, "narrow", [(0, 1), (1, 0)])
    pairs = [(i ^ 1, i) for i in range(plan.wide)]
    near = lax.ppermute(near, "wide", pairs)
    pairs = [(i, j) for i in range(1, plan.wide - 1, 2) for i, j in ((i, i + 1), (i + 1, i))]
    next_ = lax.ppermute(next_, "wide", pairs)

    half_shape = shape((6, plan.rows_x, length_y), f32)
    own_part, table = call(
        partial(ready_kernel, plan), (half_shape, shape(table.shape, bf16)), [VMEM] * 2, (VMEM, VMEM), [],
        1 << 26, LIMITS[1],
    )(demag_spectrum, table)
    mixed, far_part = call(
        partial(ahead_kernel, plan), (shape((6, 2 * length_x, length_y), f32), half_shape),
        [VMEM] * 3, (VMEM, VMEM), [], 1 << 29, LIMITS[2],
    )(got, table, swapped)
    sent = call(
        partial(back_kernel, plan),
        shape((count, lanes), f32),
        [VMEM] * 6, VMEM,
        [pltpu.VMEM((3, 4 * length_x, length_y), bf16), pltpu.VMEM((6, plan.rows_x, length_y), f32)],
        1 << 29, LIMITS[2],
    )(mixed, own_part, far_part, table, lower, upper)

    back = lax.all_to_all(sent.reshape(blocks), both, 0, 0, tiled=True).reshape(count, lanes)
    base, damp = call(
        partial(local_kernel, plan, species), (shape((3 * cells, lanes), f32), shape((cells, lanes), f32)),
        [VMEM] * 5 + [SMEM] * 4 + [VMEM], (VMEM, VMEM), [pltpu.VMEM((cells, lanes), f32)], 1 << 22, LIMITS[3],
    )(turned, side, near, next_, material2, saturation, anisotropy, damping, applied, table_out)

    rate, demag = call(
        partial(last_kernel, plan),
        (shape((3 * cells, lanes), f32), shape((3 * cells, lanes), f32)),
        [VMEM] * 5, (HBM, HBM),
        [pltpu.VMEM((3 * cells, lanes), f32), pltpu.VMEM((3 * cells, lanes), f32), pltpu.SemaphoreType.DMA((4,))],
        1 << 28, LIMITS[4],
    )(back, table_out, base, turned, damp)
    return rate.reshape(spin.shape), demag.reshape(spin.shape)


def shards(*args):
    spin, demag_spectrum = args[0], args[-1]
    _, layers, width_x, width_y = spin.shape
    _, planes, rows_x, length_y = demag_spectrum.shape
    plan = Plan(lax.axis_size("wide"), lax.axis_size("narrow"), layers, width_x, width_y,
                planes, rows_x, length_y)
    if plan.fits():
        return plane_shards(plan, *args)
    return general_shards(*args)


def solution(mesh):
    placed = (
        P(None, None, "wide", "narrow"),
        P(None, "wide", "narrow"),
        P(None, "wide", "narrow"),
        P(),
        P(),
        P(),
        P(),
        P(None, "wide", "narrow", None),
    )
    return jax.shard_map(
        shards,
        mesh=mesh,
        in_specs=placed,
        out_specs=(P(None, None, "wide", "narrow"), P(None, None, "wide", "narrow")),
        check_vma=False,
    )
```
